128 devices in a mesh: dev: 128 (over z, y, x, core).
Axes of the slice: x: 4, y: 4, z: 4, core: 2. Of those that a mesh axis runs over, the one named last changes fastest.
Arguments:
- tile_lists: int32 [3072, 512], P('dev'), may hold values from -1 to 8191, as said below
- send_rows: int32 [128, 8192], P('dev'), may hold values from -1 to 2047, as said below
- centres: float32 [2, 262144], P(None, 'dev'), may hold values from -12 to 12
- conic: float32 [2, 262144], P(None, 'dev'), may hold values from 0.015625 to 0.25
- rho: float32 [1, 262144], P(None, 'dev'), may hold values from -0.6 to 0.6
- opacity: float32 [1, 262144], P(None, 'dev'), may hold values from 0.002 to 0.03
- colors: float32 [3, 262144], P(None, 'dev'), may hold values from 0 to 1
- target: float32 [3, 2048, 384], P(None, 'dev'), may hold values from 0 to 1
Outputs:
- rendered: float32 [3, 2048, 384], P(None, 'dev')
- grads: float32 [9, 262144], P(None, 'dev')
The draws below stay inside these ranges and needn't reach their ends.
Inputs may be any that keep to these rules, and one draw needn't show every extreme that they name: `tile_lists`: row t belongs to strip t // 24. An entry is -1 only after all live entries of its row; a live entry s * 64 + m names a slot m that owner s fills for that strip. Some row has no -1. `send_rows`: entry [s, r * 64 + m] is the local index on owner s of the Gaussian in slot m for strip r, or -1 for an unused slot. The used slots of an owner and strip come first, are distinct, and number at least 32; some owner fills all 64 slots for some strip.
All inputs are finite; a program needn't handle non-finite values.
Results may differ from the reference program's by a relative error of at most 0.0003.
Values sent between devices are 32-bit elements; how exact they have to be, the bound alone decides.
A program may use at most 256 MiB of HBM per device.

```python
import math
import jax
import jax.numpy as jnp
from jax import lax

TILE = 16
LIST = 512
TILES_DEV = 24
G_DEV = 2048
CAP = 64
TILES = 3072
HEIGHT = 2048
WIDTH = 384
GAUSSIANS = 262144
N_DEV = 128


def shared_tables(key):
    keys = jax.random.split(jax.random.fold_in(key, 7), 8)
    used = jax.random.randint(keys[0], (N_DEV, N_DEV), CAP // 2, CAP + 1)
    chosen = jax.random.randint(keys[1], (2,), 0, N_DEV)
    used = used.at[chosen[0], chosen[1]].set(CAP)
    offset = jax.random.randint(keys[2], (N_DEV, N_DEV), 0, G_DEV)
    position = jnp.arange(CAP)
    rows = jnp.where(position[None, None, :] < used[:, :, None], (offset[:, :, None] + position[None, None, :]) % G_DEV, -1)
    send_table = rows.reshape(N_DEV, N_DEV * CAP).astype(jnp.int32)
    levels = jnp.array([1, 2, 4, 8], jnp.int32)
    weight = levels[jax.random.randint(keys[3], (N_DEV,), 0, 4)]
    strip_of = jnp.arange(TILES) // TILES_DEV
    tile_weight = weight[strip_of]
    lowest = LIST * tile_weight // 16
    highest = LIST * tile_weight // 8 + 1
    length = jax.random.randint(keys[4], (TILES,), lowest, highest)
    longest = jax.random.randint(keys[5], (), 0, TILES)
    length = length.at[longest].set(LIST)
    source = jax.random.randint(keys[6], (TILES, LIST), 0, N_DEV)
    room = used[source, strip_of[:, None]]
    within = jax.random.randint(keys[7], (TILES, LIST), 0, room)
    place = jnp.arange(LIST)
    lists = jnp.where(place[None, :] < length[:, None], source * CAP + within, -1).astype(jnp.int32)
    return (lists, send_table)


def draw_tile_lists(key, part):
    return shared_tables(key)[0]


def draw_send_rows(key, part):
    return shared_tables(key)[1]


def shard_levels(own_key, shape, shards, low, high):
    def one(dim, parts):
        heights = jax.random.uniform(jax.random.fold_in(jax.random.fold_in(own_key, 6), dim), (parts,), jnp.float32, low / len(shards), high / len(shards))
        return jnp.repeat(jnp.exp(heights), shape[dim] // parts).reshape((-1,) + (1,) * (len(shape) - dim - 1))

    loudness = one(*shards[0])
    for cut in shards[1:]:
        loudness = loudness * one(*cut)
    return loudness


def setup_inputs(seed: int = 0) -> dict:
    arg_keys = jax.random.split(jax.random.key(seed), 9)
    tile_lists = draw_tile_lists(jax.random.fold_in(arg_keys[8], 71), 0)
    send_rows = draw_send_rows(jax.random.fold_in(arg_keys[8], 71), 0)
    centres = jnp.clip(jax.random.uniform(arg_keys[2], (2, GAUSSIANS), jnp.float32, -12.0, 12.0) * shard_levels(arg_keys[2], (2, GAUSSIANS), ((1, 128),), -0.4, 0.0), -12.0, 12.0)
    conic = jnp.clip(jnp.exp(math.log(0.25) - 2.7725887 * jax.random.uniform(arg_keys[3], (2, GAUSSIANS), jnp.float32) ** shard_levels(arg_keys[3], (2, GAUSSIANS), ((1, 128),), -0.2, 0.2)), 0.015625, 0.25)
    rho = jnp.clip(jax.random.uniform(arg_keys[4], (1, GAUSSIANS), jnp.float32, -0.6, 0.6) * shard_levels(arg_keys[4], (1, GAUSSIANS), ((1, 128),), -0.4, 0.0), -0.6, 0.6)
    opacity = jnp.clip(jnp.exp(math.log(0.03) - 2.70805 * jax.random.uniform(arg_keys[5], (1, GAUSSIANS), jnp.float32) ** shard_levels(arg_keys[5], (1, GAUSSIANS), ((1, 128),), -0.2, 0.2)), 0.002, 0.03)
    colors = jnp.clip(1.0 * jax.random.uniform(arg_keys[6], (3, GAUSSIANS), jnp.float32) ** shard_levels(arg_keys[6], (3, GAUSSIANS), ((1, 128),), -0.2, 0.2), 0.0, 1.0)
    target = jnp.clip(1.0 * jax.random.uniform(arg_keys[7], (3, HEIGHT, WIDTH), jnp.float32) ** shard_levels(arg_keys[7], (3, HEIGHT, WIDTH), ((1, 128),), -0.2, 0.2), 0.0, 1.0)
    return {"tile_lists": tile_lists, "send_rows": send_rows, "centres": centres, "conic": conic, "rho": rho, "opacity": opacity, "colors": colors, "target": target}


def filter_taps():
    offsets = jnp.arange(11).astype(jnp.float32) - 5.0
    taps = jnp.exp(-offsets * offsets / 4.5)
    return taps / jnp.sum(taps)

def blur_strip(values):
    taps = filter_taps()
    count = values.shape[1] - 10
    width = values.shape[2]
    rows_done = taps[0] * values[:, 0:count]
    for shift in range(1, 11):
        rows_done = rows_done + taps[shift] * values[:, shift:shift + count]
    padded = jnp.pad(rows_done, ((0, 0), (0, 0), (5, 5)))
    result = taps[0] * padded[:, :, 0:width]
    for shift in range(1, 11):
        result = result + taps[shift] * padded[:, :, shift:shift + width]
    return result

def local_loss(render_pad, target_pad):
    mean_r = blur_strip(render_pad)
    mean_t = blur_strip(target_pad)
    var_r = blur_strip(render_pad * render_pad) - mean_r * mean_r
    var_t = blur_strip(target_pad * target_pad) - mean_t * mean_t
    covar = blur_strip(render_pad * target_pad) - mean_r * mean_t
    ssim = (2.0 * mean_r * mean_t + 0.0001) * (2.0 * covar + 0.0009) / ((mean_r * mean_r + mean_t * mean_t + 0.0001) * (var_r + var_t + 0.0009))
    centre_r = render_pad[:, 5:-5]
    centre_t = target_pad[:, 5:-5]
    diff = centre_r - centre_t
    return jnp.sum(0.8 * diff * diff + 0.2 * (1.0 - ssim))

def composite(params, live, tile):
    count = tile * tile
    pixel = jnp.arange(count)
    vert = (pixel // tile).astype(jnp.float32) - (tile - 1) / 2.0
    horiz = (pixel % tile).astype(jnp.float32) - (tile - 1) / 2.0
    delta_x = horiz[None, :] - params[0][:, None]
    delta_y = vert[None, :] - params[1][:, None]
    cross = params[4] * jnp.sqrt(params[2] * params[3])
    quad = params[2][:, None] * delta_x * delta_x + 2.0 * cross[:, None] * delta_x * delta_y + params[3][:, None] * delta_y * delta_y
    alpha = jnp.where(live[:, None], params[5][:, None] * jnp.exp(-0.5 * quad), 0.0)
    logs = jnp.log1p(-alpha)
    before = jnp.cumsum(logs, axis=0) - logs
    weight = alpha * jnp.exp(before)
    return jnp.dot(params[6:9], weight, precision=lax.Precision.HIGHEST, preferred_element_type=jnp.float32)

def reference(tile_lists, send_rows, centres, conic, rho, opacity, colors, target):
    params = jnp.concatenate([centres, conic, rho, opacity, colors], axis=0)
    strip_of = (jnp.arange(TILES) // TILES_DEV).astype(jnp.int32)
    live = tile_lists >= 0
    entry = jnp.maximum(tile_lists, 0)
    source = (entry // CAP).astype(jnp.int32)
    column = (strip_of[:, None] * CAP + entry % CAP).astype(jnp.int32)
    global_id = source * G_DEV + send_rows[source, column]
    global_id = jnp.where(live, global_id, 0).astype(jnp.int32)

    def render_tile(args):
        ids, mask = args
        return composite(params[:, ids], mask, TILE)
    tiles = lax.map(render_tile, (global_id, live))
    rendered = tiles.reshape(N_DEV, TILES_DEV, 3, TILE, TILE).transpose(2, 0, 3, 1, 4).reshape(3, HEIGHT, WIDTH)
    target_pad = jnp.pad(target, ((0, 0), (5, 5), (0, 0)))

    def total(image):
        return local_loss(jnp.pad(image, ((0, 0), (5, 5), (0, 0))), target_pad)
    loss_value, pull = jax.vjp(total, rendered)
    cotangent = pull(jnp.ones_like(loss_value))[0]
    cot_tiles = cotangent.reshape(3, N_DEV, TILE, TILES_DEV, TILE).transpose(1, 3, 0, 2, 4).reshape(TILES, 3, TILE * TILE)

    def accumulate(carry, args):
        ids, mask, cot = args
        _, back = jax.vjp(lambda chosen: composite(chosen, mask, TILE), params[:, ids])
        entry_grad = back(cot)[0]
        carry = carry.at[:, ids].add(jnp.where(mask[None, :], entry_grad, 0.0))
        return (carry, None)
    grads, _ = lax.scan(accumulate, jnp.zeros_like(params), (global_id, live, cot_tiles))
    return (rendered, grads)
```

```python
import functools
import math

import jax
import jax.numpy as jnp
import numpy as np
from jax import lax
from jax.experimental import pallas as pl
from jax.experimental.pallas import tpu as pltpu
from jax.sharding import PartitionSpec as P

F32 = jnp.float32
BF16 = jnp.bfloat16
LOG2E = math.log2(math.e)
SUB, LANE = 8, 128
DEAD = -10000.0


def lane_pick(table, lanes):
    return jnp.take_along_axis(table, lanes, axis=1, mode="promise_in_bounds")


def iota(shape, dim):
    return lax.broadcasted_iota(jnp.int32, shape, dim)


def sub_sum(x):
    for d in (4, 2, 1):
        x = x + pltpu.roll(x, d, 0)
    return x


def split2(x):
    one = x.astype(BF16).astype(F32)
    return one, x - one


def coefficient_rows(cx, cy, a, c, rho, op):
    b = rho * jnp.sqrt(a * c)
    bx, by = a * cx + b * cy, c * cy + b * cx
    one = jnp.log(op) - 0.5 * (cx * bx + cy * by)
    return [LOG2E * k for k in (-0.5 * a, -b, -0.5 * c, bx, by, one)]


def owner_kernel(send, centres, conic, rho, opacity, colors, out, table, ninth):
    rows = coefficient_rows(
        centres[0:1, :], centres[1:2, :], conic[0:1, :], conic[1:2, :], rho[...], opacity[...]
    )
    for p, row in enumerate(rows + [colors[0:1, :], colors[1:2, :]]):
        table[p : p + 1, :] = row
    blocks = table.shape[1] // LANE
    for h in range(blocks):
        ninth[h : h + 1, :] = colors[2:3, h * LANE : (h + 1) * LANE]
    lane = iota((SUB, LANE), 1)
    row = iota((SUB, LANE), 0)

    def pair(i, carry):
        start = pl.multiple_of(i * LANE, LANE)
        idx = jnp.broadcast_to(jnp.maximum(send[0:1, pl.ds(start, LANE)], 0), (SUB, LANE))
        hi, lo = lax.shift_right_logical(idx, 7), lax.bitwise_and(idx, 127)
        acc = jnp.zeros((SUB, LANE), F32)
        for h in range(blocks):
            acc = jnp.where(hi == h, lane_pick(table[:, h * LANE : (h + 1) * LANE], lo), acc)
        last = jnp.zeros((SUB, LANE), F32)
        for v in range(blocks // SUB):
            got = lane_pick(ninth[v * SUB : (v + 1) * SUB, :], lo)
            last = jnp.where(hi == row + v * SUB, got, last)
        last = sub_sum(last)
        left = lane < 64
        top = jnp.where(row == 0, 1.0, 0.0)
        out[2 * i] = jnp.where(left, acc, pltpu.roll(last, 64, 1) * top)
        out[2 * i + 1] = jnp.where(left, pltpu.roll(acc, 64, 1), last * top)
        return carry

    lax.fori_loop(0, send.shape[1] // LANE, pair, 0)


def basis_rows(lanes):
    pixel = iota((1, lanes), 1)
    v = lax.shift_right_logical(pixel, 4).astype(F32) - 7.5
    u = lax.bitwise_and(pixel, 15).astype(F32) - 7.5
    return [u * u, u * v, v * v, u, v, jnp.ones_like(u)]


def stack_rows(rows, count):
    shape = (count, next(r for r in rows if r is not None).shape[1])
    at = iota(shape, 0)
    result = jnp.zeros(shape, F32)
    for p, row in enumerate(rows):
        if row is not None:
            result = jnp.where(at == p, jnp.broadcast_to(row, shape), result)
    return result


def scan_sub(x):
    at = iota(x.shape, 0)
    x = jnp.where(at == 0, 1.0, pltpu.roll(x, 1, 0))
    for d in (1, 2, 4):
        x = x * jnp.where(at >= d, pltpu.roll(x, d, 0), 1.0)
    return x


def forward_kernel(lists, recv, rend, chunk_rend, chunk_start, left_out, table, ninth, cols, alphas):
    lane = iota((SUB, LANE), 1)
    row = iota((SUB, LANE), 0)

    @pl.when(pl.program_id(0) == 0)
    def _():
        def pair(h, carry):
            even, odd = recv[2 * h], recv[2 * h + 1]
            left = lane < 64
            table[h] = jnp.where(left, even, pltpu.roll(odd, 64, 1))
            both = jnp.where(left, pltpu.roll(even, 64, 1), odd)
            ninth[pl.ds(h, 1), :] = both[0:1, :]
            return carry

        lax.fori_loop(0, recv.shape[0] // 2, pair, 0)

    blocks = table.shape[0]
    count = lists.shape[2]

    for q in range(count // LANE):
        span = slice(q * LANE, (q + 1) * LANE)
        raw = jnp.broadcast_to(lists[0, 0:1, span], (SUB, LANE))
        idx = jnp.maximum(raw, 0)
        hi, lo = lax.shift_right_logical(idx, 7), lax.bitwise_and(idx, 127)
        acc = jnp.zeros((SUB, LANE), F32)
        for h in range(blocks):
            acc = jnp.where(hi == h, lane_pick(table[h], lo), acc)
        last = jnp.zeros((SUB, LANE), F32)
        for v in range(blocks // SUB):
            got = lane_pick(ninth[v * SUB : (v + 1) * SUB, :], lo)
            last = jnp.where(hi == row + v * SUB, got, last)
        last = sub_sum(last)
        acc = jnp.where((row == 5) & (raw < 0), DEAD, acc)
        one, rest = split2(acc)
        two, three = split2(rest)
        b_one, b_two = split2(last)
        more = jnp.where(row == 1, b_two, jnp.where(row == 7, last, b_one))
        more = jnp.where((row == 3) | (row == 4), pltpu.roll(one, 5, 0), more)
        more = jnp.where((row == 5) | (row == 6), pltpu.roll(acc, 7, 0), more)
        stack = jnp.concatenate([one, two, three, more], axis=0)
        cols[span, :] = jnp.concatenate([stack, jnp.zeros((LANE - 32, LANE), F32)], axis=0).T

    left = cols[:, 0:32].astype(BF16)
    left_out[0] = left
    basis = stack_rows((basis_rows(256) + [None, None]) * 3, 32).astype(BF16)
    alphas[...] = jnp.dot(left, basis, preferred_element_type=F32)

    groups = count // SUB
    step = 8

    def first(j, product):
        for k in range(step):
            at = pl.ds(pl.multiple_of((j * step + k) * SUB, SUB), SUB)
            alpha = jnp.exp2(alphas[at, :])
            alphas[at, :] = alpha
            product = product * (1.0 - alpha)
        return product

    product = lax.fori_loop(0, groups // step, first, jnp.ones((SUB, 256), F32))
    trans = scan_sub(product)
    chunk_start[0] = trans

    def second(j, carry):
        trans, red, green, blue = carry
        for k in range(step):
            at = pl.ds(pl.multiple_of((j * step + k) * SUB, SUB), SUB)
            weight = trans * alphas[at, :]
            trans = trans - weight
            color = cols[at, :]
            red = red + weight * color[:, 29:30]
            green = green + weight * color[:, 30:31]
            blue = blue + weight * color[:, 31:32]
        return trans, red, green, blue

    zero = jnp.zeros((SUB, 256), F32)
    _, *channels = lax.fori_loop(0, groups // step, second, (trans, zero, zero, zero))
    for ch, part in enumerate(channels):
        chunk_rend[0, ch] = part
        rend[0, ch : ch + 1, :] = sub_sum(part)[0:1, :]


def taps_of():
    offsets = np.arange(11, dtype=np.float32) - np.float32(5)
    taps = np.exp(-offsets * offsets / np.float32(4.5)).astype(np.float32)
    return [float(t) for t in taps / taps.sum(dtype=np.float32)]


TAPS = taps_of()


def blur_rows(read, start, count):
    total = TAPS[5] * read(start, count)
    for m in range(1, 6):
        total = total + TAPS[5 + m] * (read(start - m, count) + read(start + m, count))
    return total


def blur_lanes(x):
    rows, width = x.shape
    pad = jnp.zeros((rows, LANE), F32)
    wide = jnp.concatenate([x, pad], axis=1)
    total = TAPS[5] * x
    for m in range(1, 6):
        both = pltpu.roll(wide, m, 1) + pltpu.roll(wide, width + LANE - m, 1)
        total = total + TAPS[5 + m] * both[:, :width]
    return total


def loss_kernel(me, before, centre, after, t_before, t_centre, t_after, grad, pads, maps):
    height = centre.shape[1]
    mine = me[0]
    total_rows = me[1]
    width = centre.shape[2]
    at = iota((2 * height, width), 0) - height // 2 + mine * height
    inside = (at >= 0) & (at < total_rows)
    for ch in range(3):
        for i, (r, t) in enumerate(((before, t_before), (centre, t_centre), (after, t_after))):
            span = slice(i * height, (i + 1) * height)
            rr, tt = r[ch], t[ch]
            pads[0, span, :] = rr
            pads[1, span, :] = tt
            pads[2, span, :] = rr * rr
            pads[3, span, :] = tt * tt
            pads[4, span, :] = rr * tt

        def wide_blur(k):
            vertical = blur_rows(lambda s, n: pads[k, s : s + n, :], height // 2, 2 * height)
            return blur_lanes(vertical)

        mr, mt, rr, tt, rt = (wide_blur(k) for k in range(5))
        cv = rt - mr * mt
        top1 = 2.0 * mr * mt + 0.0001
        top2 = 2.0 * cv + 0.0009
        low1 = mr * mr + mt * mt + 0.0001
        low2 = (rr - mr * mr) + (tt - mt * mt) + 0.0009
        inv1, inv2 = 1.0 / low1, 1.0 / low2
        both = inv1 * inv2
        ssim = top1 * top2 * both
        d_rr = -ssim * inv2
        d_rt = 2.0 * top1 * both
        d_mr = 2.0 * (mt * (top2 - top1) * both + mr * ssim * (inv2 - inv1))
        for k, value in enumerate((d_mr, d_rr, d_rt)):
            maps[k] = jnp.where(inside, value, 0.0)

        def back_blur(k):
            vertical = blur_rows(lambda s, n: maps[k, s : s + n, :], height // 2, height)
            return blur_lanes(vertical)

        g_mr, g_rr, g_rt = (back_blur(k) for k in range(3))
        r, t = centre[ch], t_centre[ch]
        grad[ch] = 1.6 * (r - t) - 0.2 * (g_mr + 2.0 * r * g_rr + t * g_rt)


NT = (((1,), (1,)), ((), ()))


def onehot(lo, rows):
    return jnp.where(iota((rows, lo.shape[1]), 0) == lo, 1.0, 0.0).astype(BF16)


def spread(values, hi, blocks):
    masked = [jnp.where(hi == h, values, 0.0) for h in range(blocks)]
    return jnp.concatenate(masked, axis=0)


def scatter_block(eight, ninth, idx, blocks):
    span = idx.shape[1]
    hi, lo = lax.shift_right_arithmetic(idx, 8), lax.bitwise_and(idx, 255)
    hot = onehot(lo, 256)
    hi8 = jnp.broadcast_to(hi, (SUB, span))
    own = iota((blocks, span), 0) == hi
    total = None
    for values, extra in zip(split2(eight), split2(ninth)):
        left = jnp.concatenate(
            [spread(values, hi8, blocks), jnp.where(own, jnp.broadcast_to(extra, own.shape), 0.0)],
            axis=0,
        ).astype(BF16)
        part = lax.dot_general(left, hot, NT, preferred_element_type=F32)
        total = part if total is None else total + part
    return total


def backward_kernel(lists, left_in, cot, chunk_rend, chunk_start, out, fields, weights, halves, grads, slots):
    tile = pl.program_id(0)
    count = lists.shape[2]
    groups = count // SUB
    step = 8
    rows = [cot[0, ch : ch + 1, :] for ch in range(3)]
    ones, twos = zip(*(split2(r) for r in rows))
    basis = stack_rows((basis_rows(256) + [None, None]) * 3, 32)
    back = stack_rows(
        [None] * 6 + [ones[0], ones[1]] + [None] * 6 + [ones[0], ones[1]] + [None] * 6
        + [ones[0], ones[1], ones[2], ones[2], twos[2], twos[0], twos[1]], 32
    )
    right = jnp.concatenate([basis, back], axis=1).astype(BF16)
    fields[...] = jnp.dot(left_in[0], right, preferred_element_type=F32)
    start = chunk_start[0]

    def first(j, trans):
        for k in range(step):
            at = pl.ds(pl.multiple_of((j * step + k) * SUB, SUB), SUB)
            alpha = jnp.exp2(fields[at, 0:256])
            fields[at, 0:256] = alpha
            weight = trans * alpha
            weights[at, :] = weight
            trans = trans - weight
        return trans

    final = lax.fori_loop(0, groups // step, first, start)
    behind = sum(chunk_rend[0, ch] * rows[ch] for ch in range(3))
    at8 = iota((SUB, 256), 0)
    behind = jnp.where(at8 == SUB - 1, 0.0, pltpu.roll(behind, SUB - 1, 0))
    for d in (1, 2, 4):
        behind = behind + jnp.where(at8 < SUB - d, pltpu.roll(behind, SUB - d, 0), 0.0)
    shade = behind / final

    def second(jj, shade):
        j = groups // step - 1 - jj
        parts = []
        for k in reversed(range(step)):
            at = pl.ds(pl.multiple_of((j * step + k) * SUB, SUB), SUB)
            alpha, weight = fields[at, 0:256], weights[at, :]
            diff = fields[at, 256:512] - shade
            shade = shade + alpha * diff
            parts.append((weight * diff, weight))
        parts = parts[::-1]
        for k in range(0, step, 2):
            at = pl.ds(pl.multiple_of((j * step + k) * SUB, 2 * SUB), 2 * SUB)
            for i in range(2):
                value = jnp.concatenate([parts[k][i], parts[k + 1][i]], axis=0)
                one = value.astype(BF16)
                halves[at, 512 * i : 512 * i + 256] = one
                halves[at, 512 * i + 256 : 512 * i + 512] = (value - one.astype(F32)).astype(BF16)
        return shade

    lax.fori_loop(0, groups // step, second, shade)
    base = stack_rows(basis_rows(256), 16)
    firsts = stack_rows([None] * 6 + list(ones) + list(twos), 16)
    seconds = stack_rows([None] * 6 + list(ones), 16)
    kernel = jnp.concatenate([base, base, firsts, seconds], axis=1).astype(BF16)
    found = lax.dot_general(kernel, halves[...], NT, preferred_element_type=F32)
    low = found[8:16, :]
    at16 = iota(low.shape, 0)
    top = found[0:8, :] + jnp.where(at16 >= 6, pltpu.roll(low, 5, 0), 0.0)
    last = low[0:1, :] + low[3:4, :]
    idx = jnp.maximum(lists[0], 0)
    blocks = slots.shape[0] // (SUB + 1)
    part = scatter_block(top, last, idx, blocks)

    @pl.when(tile == 0)
    def _():
        slots[...] = part

    @pl.when(tile > 0)
    def _():
        slots[...] = slots[...] + part

    @pl.when(tile == pl.num_programs(0) - 1)
    def _():
        lane = iota((SUB, LANE), 1)
        left = lane < 64
        top8 = jnp.where(iota((SUB, LANE), 0) == 0, 1.0, 0.0)

        for h in range(blocks):
            for half in range(2):
                span = slice(half * LANE, (half + 1) * LANE)
                acc = slots[h * SUB : (h + 1) * SUB, span]
                extra = jnp.broadcast_to(slots[blocks * SUB + h : blocks * SUB + h + 1, span], (SUB, LANE))
                owner = 4 * h + 2 * half
                out[owner] = jnp.where(left, acc, pltpu.roll(extra, 64, 1) * top8)
                out[owner + 1] = jnp.where(left, pltpu.roll(acc, 64, 1), extra * top8)


def home_kernel(back, send, centres, conic, rho, opacity, out, total, rows):
    lane = iota((SUB, LANE), 1)
    left = lane < 64
    pairs = back.shape[0] // 2
    per = 8
    blocks = centres.shape[1] // 256
    total[...] = jnp.zeros_like(total)

    def chunk(c, carry):
        eight, ninth = [], []
        for k in range(per):
            i = c * per + k
            even, odd = back[2 * i], back[2 * i + 1]
            eight.append(jnp.where(left, even, pltpu.roll(odd, 64, 1)))
            ninth.append(jnp.where(left, pltpu.roll(even, 64, 1), odd)[0:1, :])
        start = pl.multiple_of(c * per * LANE, per * LANE)
        idx = send[0:1, pl.ds(start, per * LANE)]
        total[...] = total[...] + scatter_block(
            jnp.concatenate(eight, axis=1), jnp.concatenate(ninth, axis=1), idx, blocks
        )
        return carry

    lax.fori_loop(0, pairs // per, chunk, 0)
    for h in range(blocks):
        span = slice(h * 256, (h + 1) * 256)
        rows[0:8, span] = total[h * SUB : (h + 1) * SUB, :]
        rows[8:9, span] = total[blocks * SUB + h : blocks * SUB + h + 1, :]
    m_uu, m_uv, m_vv, m_u, m_v, m_1 = (rows[p : p + 1, :] for p in range(6))
    cx, cy = centres[0:1, :], centres[1:2, :]
    a, c = conic[0:1, :], conic[1:2, :]
    r = rho[...]
    root = jnp.sqrt(a * c)
    b = r * root
    x1, y1 = m_u - cx * m_1, m_v - cy * m_1
    xx = m_uu - cx * (m_u + x1)
    yy = m_vv - cy * (m_v + y1)
    xy = m_uv - cx * m_v - cy * x1
    out[0:1, :] = a * x1 + b * y1
    out[1:2, :] = c * y1 + b * x1
    out[2:3, :] = -0.5 * xx - xy * (0.5 * r * (root / a))
    out[3:4, :] = -0.5 * yy - xy * (0.5 * r * (root / c))
    out[4:5, :] = -xy * root
    out[5:6, :] = m_1 / opacity[...]
    out[6:9, :] = rows[6:9, :]


def struct(*shape, dtype=F32):
    return jax.ShapeDtypeStruct(shape, dtype)


def shards(tile_lists, send_rows, centres, conic, rho, opacity, colors, target):
    devices = lax.axis_size("dev")
    owned = centres.shape[1]
    tiles, count = tile_lists.shape
    height, width = target.shape[1], target.shape[2]
    pixels = height * height
    params = pltpu.CompilerParams(vmem_limit_bytes=48 << 20)
    outgoing = pl.pallas_call(
        owner_kernel,
        out_shape=struct(devices, SUB, LANE),
        scratch_shapes=[pltpu.VMEM((SUB, owned), F32), pltpu.VMEM((owned // LANE, LANE), F32)],
        name="owner_gather",
    )(send_rows, centres, conic, rho, opacity, colors)
    incoming = lax.all_to_all(outgoing, "dev", split_axis=0, concat_axis=0, tiled=True)

    lists = tile_lists.reshape(tiles, SUB, count // SUB).transpose(0, 2, 1).reshape(tiles, 1, count)
    whole = lambda *shape: pl.BlockSpec(shape, lambda t: (0,) * len(shape))
    per_tile = lambda *shape: pl.BlockSpec((1,) + shape, lambda t: (t,) + (0,) * len(shape))
    rend, chunk_rend, chunk_start, left = pl.pallas_call(
        forward_kernel,
        grid=(tiles,),
        in_specs=[per_tile(1, count), whole(devices, SUB, LANE)],
        out_specs=[per_tile(3, pixels), per_tile(3, SUB, pixels), per_tile(SUB, pixels), per_tile(count, 32)],
        out_shape=[
            struct(tiles, 3, pixels),
            struct(tiles, 3, SUB, pixels),
            struct(tiles, SUB, pixels),
            struct(tiles, count, 32, dtype=BF16),
        ],
        scratch_shapes=[
            pltpu.VMEM((devices // 2, SUB, LANE), F32),
            pltpu.VMEM((devices // 2, LANE), F32),
            pltpu.VMEM((count, LANE), F32),
            pltpu.VMEM((count, pixels), F32),
        ],
        compiler_params=params,
        name="tile_forward",
    )(lists, incoming)
    image = rend.reshape(tiles, 3, height, height).transpose(1, 2, 0, 3).reshape(3, height, width)

    up = [(i, i + 1) for i in range(devices - 1)]
    down = [(j, i) for i, j in up]
    me = lax.axis_index("dev")
    where = jnp.stack([me, devices * height]).astype(jnp.int32)
    pixel_grad = pl.pallas_call(
        loss_kernel,
        in_specs=[pl.BlockSpec(memory_space=pltpu.SMEM)] + [pl.BlockSpec(memory_space=pltpu.VMEM)] * 6,
        out_shape=struct(3, height, width),
        scratch_shapes=[pltpu.VMEM((5, 3 * height, width), F32), pltpu.VMEM((3, 2 * height, width), F32)],
        name="loss_gradient",
    )(
        where,
        lax.ppermute(image, "dev", up), image, lax.ppermute(image, "dev", down),
        lax.ppermute(target, "dev", up), target, lax.ppermute(target, "dev", down),
    )
    cot = pixel_grad.reshape(3, height, tiles, height).transpose(2, 0, 1, 3).reshape(tiles, 3, pixels)

    hi_blocks = devices * 64 // 256
    slot_grads = pl.pallas_call(
        backward_kernel,
        grid=(tiles,),
        in_specs=[
            per_tile(1, count), per_tile(count, 32), per_tile(3, pixels),
            per_tile(3, SUB, pixels), per_tile(SUB, pixels),
        ],
        out_specs=whole(devices, SUB, LANE),
        out_shape=struct(devices, SUB, LANE),
        scratch_shapes=[
            pltpu.VMEM((count, 2 * pixels), F32),
            pltpu.VMEM((count, pixels), F32),
            pltpu.VMEM((count, 4 * pixels), BF16),
            pltpu.VMEM((16, count), F32),
            pltpu.VMEM((hi_blocks * (SUB + 1), 256), F32),
        ],
        compiler_params=params,
        name="tile_backward",
    )(lists, left, cot, chunk_rend, chunk_start)
    returned = lax.all_to_all(slot_grads, "dev", split_axis=0, concat_axis=0, tiled=True)
    grads = pl.pallas_call(
        home_kernel,
        out_shape=struct(9, owned),
        scratch_shapes=[
            pltpu.VMEM((owned // 256 * (SUB + 1), 256), F32),
            pltpu.VMEM((16, owned), F32),
        ],
        name="owner_scatter",
    )(returned, send_rows, centres, conic, rho, opacity)
    return image, grads


def solution(mesh):
    return jax.shard_map(
        shards,
        mesh=mesh,
        in_specs=(
            P("dev", None),
            P("dev", None),
            P(None, "dev"),
            P(None, "dev"),
            P(None, "dev"),
            P(None, "dev"),
            P(None, "dev"),
            P(None, "dev", None),
        ),
        out_specs=(P(None, "dev", None), P(None, "dev")),
        check_vma=False,
    )
```

```python
import functools
import math

import jax
import jax.numpy as jnp
import numpy as np
from jax import lax
from jax.experimental import pallas as pl
from jax.experimental.pallas import tpu as pltpu
from jax.sharding import PartitionSpec as P

F32 = jnp.float32
BF16 = jnp.bfloat16
LOG2E = math.log2(math.e)
SUB, LANE = 8, 128
DEAD = -10000.0


def lane_pick(table, lanes):
    return jnp.take_along_axis(table, lanes, axis=1, mode="promise_in_bounds")


def iota(shape, dim):
    return lax.broadcasted_iota(jnp.int32, shape, dim)


def sub_sum(x):
    for d in (4, 2, 1):
        x = x + pltpu.roll(x, d, 0)
    return x


def split2(x):
    one = x.astype(BF16).astype(F32)
    return one, x - one


def coefficient_rows(cx, cy, a, c, rho, op):
    b = rho * jnp.sqrt(a * c)
    bx, by = a * cx + b * cy, c * cy + b * cx
    one = jnp.log(op) - 0.5 * (cx * bx + cy * by)
    return [LOG2E * k for k in (-0.5 * a, -b, -0.5 * c, bx, by, one)]


def pick_tree(parts, bits):
    if len(parts) == 1:
        return parts[0]()
    half = len(parts) // 2
    return jnp.where(bits[half], pick_tree(parts[half:], bits), pick_tree(parts[:half], bits))


def pick_nine(table, ninth, idx, row, blocks):
    hi, lo = lax.shift_right_logical(idx, 7), lax.bitwise_and(idx, 127)
    bits = {1 << k: lax.bitwise_and(hi, 1 << k) != 0 for k in range(blocks.bit_length() - 1)}
    eight = pick_tree([lambda h=h: lane_pick(table(h), lo) for h in range(blocks)], bits)
    coarse = {k // SUB: v for k, v in bits.items() if k >= SUB}
    last = pick_tree(
        [lambda v=v: lane_pick(ninth[v * SUB : (v + 1) * SUB, :], lo) for v in range(blocks // SUB)], coarse
    )
    return eight, sub_sum(jnp.where(lax.bitwise_and(hi, 7) == row, last, 0.0))


def owner_kernel(send, centres, conic, rho, opacity, colors, out, table, ninth):
    rows = coefficient_rows(
        centres[0:1, :], centres[1:2, :], conic[0:1, :], conic[1:2, :], rho[...], opacity[...]
    )
    for p, row in enumerate(rows + [colors[0:1, :], colors[1:2, :]]):
        table[p : p + 1, :] = row
    blocks = table.shape[1] // LANE
    for h in range(blocks):
        ninth[h : h + 1, :] = colors[2:3, h * LANE : (h + 1) * LANE]
    left = iota((SUB, LANE), 1) < 64
    row = iota((SUB, LANE), 0)
    top = jnp.where(row == 0, 1.0, 0.0)
    step = 4

    def pairs(ii, carry):
        for k in range(step):
            i = ii * step + k
            start = pl.multiple_of(i * LANE, LANE)
            idx = jnp.broadcast_to(jnp.maximum(send[0:1, pl.ds(start, LANE)], 0), (SUB, LANE))
            eight, last = pick_nine(lambda h: table[:, h * LANE : (h + 1) * LANE], ninth, idx, row, blocks)
            out[2 * i] = jnp.where(left, eight, pltpu.roll(last, 64, 1) * top)
            out[2 * i + 1] = jnp.where(left, pltpu.roll(eight, 64, 1), last * top)
        return carry

    lax.fori_loop(0, send.shape[1] // LANE // step, pairs, 0)


MESH = pl.DeviceIdType.MESH


def exchange_kernel(x, out, local_sem, send_sem, recv_sem):
    me = lax.axis_index("dev")
    n = lax.axis_size("dev")
    barrier = pltpu.get_barrier_semaphore()

    def greet(k, carry):
        peer = lax.rem(me + k, n)
        pl.semaphore_signal(barrier, inc=1, device_id=(peer,), device_id_type=MESH)
        return carry

    lax.fori_loop(1, n, greet, 0)
    own = pltpu.make_async_copy(x.at[me], out.at[me], local_sem)
    own.start()
    pl.semaphore_wait(barrier, n - 1)

    def start(k, carry):
        peer = lax.rem(me + k, n)
        pltpu.make_async_remote_copy(
            src_ref=x.at[peer], dst_ref=out.at[me], send_sem=send_sem, recv_sem=recv_sem,
            device_id=(peer,), device_id_type=MESH,
        ).start()
        return carry

    lax.fori_loop(1, n, start, 0)
    own.wait()
    rest = pl.ds(0, n - 1)
    pltpu.make_async_copy(x.at[rest], x.at[rest], send_sem).wait()
    pltpu.make_async_copy(out.at[rest], out.at[rest], recv_sem).wait()


def exchange(x, number):
    return pl.pallas_call(
        exchange_kernel,
        out_shape=jax.ShapeDtypeStruct(x.shape, x.dtype),
        in_specs=[pl.BlockSpec(memory_space=pltpu.VMEM)],
        out_specs=pl.BlockSpec(memory_space=pltpu.VMEM),
        scratch_shapes=[pltpu.SemaphoreType.DMA] * 3,
        compiler_params=pltpu.CompilerParams(collective_id=number, has_side_effects=True),
        name="exchange",
    )(x)


def block_transpose(x):
    row = iota(x.shape, 0)
    block = lax.shift_right_logical(iota(x.shape, 1), 4)
    for d in (1, 2, 4):
        low_row = lax.bitwise_and(row, d) == 0
        low_block = lax.bitwise_and(block, d) == 0
        down = pltpu.roll(pltpu.roll(x, SUB - d, 0), 16 * d, 1)
        back = pltpu.roll(pltpu.roll(x, d, 0), LANE - 16 * d, 1)
        x = jnp.where(low_row == low_block, x, jnp.where(low_row, down, back))
    return x


def basis_rows(lanes):
    pixel = iota((1, lanes), 1)
    v = lax.shift_right_logical(pixel, 4).astype(F32) - 7.5
    u = lax.bitwise_and(pixel, 15).astype(F32) - 7.5
    return [u * u, u * v, v * v, u, v, jnp.ones_like(u)]


def stack_rows(rows, count):
    shape = (count, next(r for r in rows if r is not None).shape[1])
    at = iota(shape, 0)
    result = jnp.zeros(shape, F32)
    for p, row in enumerate(rows):
        if row is not None:
            result = jnp.where(at == p, jnp.broadcast_to(row, shape), result)
    return result


def scan_sub(x):
    at = iota(x.shape, 0)
    x = jnp.where(at == 0, 1.0, pltpu.roll(x, 1, 0))
    for d in (1, 2, 4):
        x = x * jnp.where(at >= d, pltpu.roll(x, d, 0), 1.0)
    return x


def segments(count):
    groups = count // SUB // 2
    return [(seg, j, (seg * groups + j) * SUB) for j in range(groups) for seg in range(2)]


def forward_kernel(lists, recv, image, chunk_rend, chunk_start, left_out, table, ninth, cols, alphas, rends):
    tile = pl.program_id(0)
    row = iota((SUB, LANE), 0)

    @pl.when(tile == 0)
    def _():
        def pair(h, carry):
            even, odd = recv[2 * h], recv[2 * h + 1]
            left = iota((SUB, LANE), 1) < 64
            table[h] = jnp.where(left, even, pltpu.roll(odd, 64, 1))
            both = jnp.where(left, pltpu.roll(even, 64, 1), odd)
            ninth[pl.ds(h, 1), :] = both[0:1, :]
            return carry

        lax.fori_loop(0, recv.shape[0] // 2, pair, 0)

    blocks = table.shape[0]
    count = lists.shape[2]
    for q in range(count // LANE):
        span = slice(q * LANE, (q + 1) * LANE)
        raw = jnp.broadcast_to(lists[0, 0:1, span], (SUB, LANE))
        acc, last = pick_nine(lambda h: table[h], ninth, jnp.maximum(raw, 0), row, blocks)
        acc = jnp.where((row == 5) & (raw < 0), DEAD, acc)
        one, rest = split2(acc)
        two, three = split2(rest)
        b_one, b_two = split2(last)
        more = jnp.where(row == 1, b_two, jnp.where(row == 7, last, b_one))
        more = jnp.where((row == 3) | (row == 4), pltpu.roll(one, 5, 0), more)
        more = jnp.where((row == 5) | (row == 6), pltpu.roll(acc, 7, 0), more)
        stack = jnp.concatenate([one, two, three, more], axis=0)
        cols[span, :] = jnp.concatenate([stack, jnp.zeros((LANE - 32, LANE), F32)], axis=0).T

    basis = stack_rows((basis_rows(256) + [None, None]) * 3, 32).astype(BF16)
    ones = jnp.ones((SUB, 256), F32)
    product = [ones, ones]
    piece = 64
    for c in range(count // piece):
        span = slice(c * piece, (c + 1) * piece)
        left = cols[span, 0:32].astype(BF16)
        left_out[0, span, :] = left
        alpha = jnp.exp2(jnp.dot(left, basis, preferred_element_type=F32))
        alphas[span, :] = alpha
        rest = 1.0 - alpha
        parts = [rest[k * SUB : (k + 1) * SUB, :] for k in range(piece // SUB)]
        while len(parts) > 1:
            parts = [parts[k] * parts[k + 1] for k in range(0, len(parts), 2)]
        seg = 2 * c * piece // count
        product[seg] = product[seg] * parts[0]

    begin = scan_sub(product[0] * product[1])
    trans = [begin, begin * product[0]]
    zero = jnp.zeros((SUB, 256), F32)
    sums = [[zero] * 3, [zero] * 3]
    for seg in range(2):
        chunk_start[0, seg] = trans[seg]
    for seg, j, at in segments(count):
        weight = trans[seg] * alphas[at : at + SUB, :]
        trans[seg] = trans[seg] - weight
        color = cols[at : at + SUB, :]
        sums[seg] = [t + weight * color[:, 29 + ch : 30 + ch] for ch, t in enumerate(sums[seg])]
    for ch in range(3):
        for seg in range(2):
            chunk_rend[0, ch, seg] = sums[seg][ch]
        rends[ch, pl.ds(tile, 1), :] = sub_sum(sums[0][ch] + sums[1][ch])[0:1, :]

    @pl.when(tile == pl.num_programs(0) - 1)
    def _():
        for ch in range(3):
            for g in range(rends.shape[1] // SUB):
                for h in range(2):
                    image[ch, h * SUB : (h + 1) * SUB, g * LANE : (g + 1) * LANE] = block_transpose(
                        rends[ch, g * SUB : (g + 1) * SUB, h * LANE : (h + 1) * LANE]
                    )


def taps_of():
    offsets = np.arange(11, dtype=np.float32) - np.float32(5)
    taps = np.exp(-offsets * offsets / np.float32(4.5)).astype(np.float32)
    return [float(t) for t in taps / taps.sum(dtype=np.float32)]


TAPS = taps_of()


def blur_rows(read, start, count):
    total = TAPS[5] * read(start, count)
    for m in range(1, 6):
        total = total + TAPS[5 + m] * (read(start - m, count) + read(start + m, count))
    return total


def blur_lanes(x):
    rows, width = x.shape
    pad = jnp.zeros((rows, LANE), F32)
    wide = jnp.concatenate([x, pad], axis=1)
    total = TAPS[5] * x
    for m in range(1, 6):
        both = pltpu.roll(wide, m, 1) + pltpu.roll(wide, width + LANE - m, 1)
        total = total + TAPS[5 + m] * both[:, :width]
    return total


def loss_kernel(me, before, centre, after, t_before, t_centre, t_after, grad, pads, maps):
    height = centre.shape[1]
    mine = me[0]
    total_rows = me[1]
    width = centre.shape[2]
    at = iota((2 * height, width), 0) - height // 2 + mine * height
    inside = (at >= 0) & (at < total_rows)
    for ch in range(3):
        for i, (r, t) in enumerate(((before, t_before), (centre, t_centre), (after, t_after))):
            span = slice(i * height, (i + 1) * height)
            rr, tt = r[ch], t[ch]
            pads[0, span, :] = rr
            pads[1, span, :] = tt
            pads[2, span, :] = rr * rr
            pads[3, span, :] = tt * tt
            pads[4, span, :] = rr * tt

        def wide_blur(k):
            vertical = blur_rows(lambda s, n: pads[k, s : s + n, :], height // 2, 2 * height)
            return blur_lanes(vertical)

        mr, mt, rr, tt, rt = (wide_blur(k) for k in range(5))
        cv = rt - mr * mt
        top1 = 2.0 * mr * mt + 0.0001
        top2 = 2.0 * cv + 0.0009
        low1 = mr * mr + mt * mt + 0.0001
        low2 = (rr - mr * mr) + (tt - mt * mt) + 0.0009
        inv1, inv2 = 1.0 / low1, 1.0 / low2
        both = inv1 * inv2
        ssim = top1 * top2 * both
        d_rr = -ssim * inv2
        d_rt = 2.0 * top1 * both
        d_mr = 2.0 * (mt * (top2 - top1) * both + mr * ssim * (inv2 - inv1))
        for k, value in enumerate((d_mr, d_rr, d_rt)):
            maps[k] = jnp.where(inside, value, 0.0)

        def back_blur(k):
            vertical = blur_rows(lambda s, n: maps[k, s : s + n, :], height // 2, height)
            return blur_lanes(vertical)

        g_mr, g_rr, g_rt = (back_blur(k) for k in range(3))
        r, t = centre[ch], t_centre[ch]
        grad[ch] = 1.6 * (r - t) - 0.2 * (g_mr + 2.0 * r * g_rr + t * g_rt)


NT = (((1,), (1,)), ((), ()))


def onehot(lo, rows):
    return jnp.where(iota((rows, lo.shape[1]), 0) == lo, 1.0, 0.0).astype(BF16)


def spread(values, hi, blocks):
    masked = [jnp.where(hi == h, values, 0.0) for h in range(blocks)]
    return jnp.concatenate(masked, axis=0)


def scatter_block(eight, ninth, idx, blocks):
    span = idx.shape[1]
    hi, lo = lax.shift_right_arithmetic(idx, 8), lax.bitwise_and(idx, 255)
    hot = onehot(lo, 256)
    hi8 = jnp.broadcast_to(hi, (SUB, span))
    own = iota((blocks, span), 0) == hi
    left = []
    for values, extra in zip(split2(eight), split2(ninth)):
        left.append(spread(values, hi8, blocks))
        left.append(jnp.where(own, jnp.broadcast_to(extra, own.shape), 0.0))
    left = jnp.concatenate(left, axis=0).astype(BF16)
    both = lax.dot_general(left, hot, NT, preferred_element_type=F32)
    return both[: blocks * (SUB + 1), :] + both[blocks * (SUB + 1) :, :]


def backward_kernel(lists, left_in, grad, chunk_rend, chunk_start, out, cots, halves, grads, slots):
    tile = pl.program_id(0)
    tiles = pl.num_programs(0)
    count = left_in.shape[1]

    @pl.when(tile == 0)
    def _():
        for ch in range(3):
            for g in range(cots.shape[0] // SUB):
                for h in range(2):
                    span = slice(h * LANE, (h + 1) * LANE)
                    block = block_transpose(grad[ch, h * SUB : (h + 1) * SUB, g * LANE : (g + 1) * LANE])
                    for t in range(SUB):
                        cots[g * SUB + t, ch : ch + 1, span] = block[t : t + 1, :]

    rows = [cots[tile, ch : ch + 1, :] for ch in range(3)]
    ones, twos = zip(*(split2(r) for r in rows))
    basis = stack_rows((basis_rows(256) + [None, None]) * 3, 32)
    back = stack_rows(
        [None] * 6 + [ones[0], ones[1]] + [None] * 6 + [ones[0], ones[1]] + [None] * 6
        + [ones[0], ones[1], ones[2], ones[2], twos[2], twos[0], twos[1]], 32
    )
    right = jnp.concatenate([basis, back], axis=1).astype(BF16)

    inside = [sum(chunk_rend[0, ch, seg] * rows[ch] for ch in range(3)) for seg in range(2)]
    at8 = iota((SUB, 256), 0)
    later = inside[0] + inside[1]
    later = jnp.where(at8 == SUB - 1, 0.0, pltpu.roll(later, SUB - 1, 0))
    for d in (1, 2, 4):
        later = later + jnp.where(at8 < SUB - d, pltpu.roll(later, SUB - d, 0), 0.0)
    behind = [later + inside[1] + inside[0], later + inside[1]]
    trans = [chunk_start[0, seg] for seg in range(2)]

    piece = 32
    order = [c // 2 + (c % 2) * (count // piece // 2) for c in range(count // piece)]
    for c in order:
        seg = 2 * c * piece // count
        field = jnp.dot(left_in[0, c * piece : (c + 1) * piece, :], right, preferred_element_type=F32)
        alpha = jnp.exp2(field[:, 0:256])
        ratio = alpha / (1.0 - alpha)
        parts = []
        for k in range(piece // SUB):
            span = slice(k * SUB, (k + 1) * SUB)
            weight = trans[seg] * alpha[span]
            trans[seg] = trans[seg] - weight
            shown = weight * field[span, 256:512]
            behind[seg] = behind[seg] - shown
            parts.append((shown - ratio[span] * behind[seg], weight))
        at = slice(c * piece, (c + 1) * piece)
        value = jnp.concatenate([p[0] for p in parts], axis=0)
        one = value.astype(BF16)
        halves[at, 0:256] = one
        halves[at, 256:512] = (value - one.astype(F32)).astype(BF16)
        halves[at, 512:768] = jnp.concatenate([p[1] for p in parts], axis=0).astype(BF16)

    base = stack_rows(basis_rows(256), 16)
    colours = stack_rows([None] * 6 + list(ones) + list(twos), 16)
    kernel = jnp.concatenate([base, base, colours], axis=1).astype(BF16)
    found = lax.dot_general(kernel, halves[...], NT, preferred_element_type=F32)
    low = found[8:16, :]
    at16 = iota(low.shape, 0)
    top = found[0:8, :] + jnp.where(at16 >= 6, pltpu.roll(low, 5, 0), 0.0)
    grads[tile, 0:8, :] = top
    grads[tile, 8:9, :] = low[0:1, :] + low[3:4, :]

    @pl.when(tile == tiles - 1)
    def _():
        slots[...] = jnp.zeros_like(slots)
        blocks = slots.shape[0] // (SUB + 1)
        per = 2

        def chunk(c, carry):
            each = [c * per + k for k in range(per)]
            idx = jnp.concatenate([jnp.maximum(lists[t], 0) for t in each], axis=1)
            eight = jnp.concatenate([grads[t, 0:8, :] for t in each], axis=1)
            ninth = jnp.concatenate([grads[t, 8:9, :] for t in each], axis=1)
            slots[...] = slots[...] + scatter_block(eight, ninth, idx, blocks)
            return carry

        lax.fori_loop(0, cots.shape[0] // per, chunk, 0)
        left = iota((SUB, LANE), 1) < 64
        top8 = jnp.where(iota((SUB, LANE), 0) == 0, 1.0, 0.0)
        for h in range(blocks):
            for half in range(2):
                span = slice(half * LANE, (half + 1) * LANE)
                acc = slots[h * SUB : (h + 1) * SUB, span]
                extra = jnp.broadcast_to(slots[blocks * SUB + h : blocks * SUB + h + 1, span], (SUB, LANE))
                owner = 4 * h + 2 * half
                out[owner] = jnp.where(left, acc, pltpu.roll(extra, 64, 1) * top8)
                out[owner + 1] = jnp.where(left, pltpu.roll(acc, 64, 1), extra * top8)


def home_kernel(back, send, centres, conic, rho, opacity, out, total, rows):
    lane = iota((SUB, LANE), 1)
    left = lane < 64
    pairs = back.shape[0] // 2
    per = 8
    blocks = centres.shape[1] // 256
    total[...] = jnp.zeros_like(total)

    def chunk(c, carry):
        eight, ninth = [], []
        for k in range(per):
            i = c * per + k
            even, odd = back[2 * i], back[2 * i + 1]
            eight.append(jnp.where(left, even, pltpu.roll(odd, 64, 1)))
            ninth.append(jnp.where(left, pltpu.roll(even, 64, 1), odd)[0:1, :])
        start = pl.multiple_of(c * per * LANE, per * LANE)
        idx = send[0:1, pl.ds(start, per * LANE)]
        total[...] = total[...] + scatter_block(
            jnp.concatenate(eight, axis=1), jnp.concatenate(ninth, axis=1), idx, blocks
        )
        return carry

    lax.fori_loop(0, pairs // per, chunk, 0)
    for h in range(blocks):
        span = slice(h * 256, (h + 1) * 256)
        rows[0:8, span] = total[h * SUB : (h + 1) * SUB, :]
        rows[8:9, span] = total[blocks * SUB + h : blocks * SUB + h + 1, :]
    m_uu, m_uv, m_vv, m_u, m_v, m_1 = (rows[p : p + 1, :] for p in range(6))
    cx, cy = centres[0:1, :], centres[1:2, :]
    a, c = conic[0:1, :], conic[1:2, :]
    r = rho[...]
    root = jnp.sqrt(a * c)
    b = r * root
    x1, y1 = m_u - cx * m_1, m_v - cy * m_1
    xx = m_uu - cx * (m_u + x1)
    yy = m_vv - cy * (m_v + y1)
    xy = m_uv - cx * m_v - cy * x1
    out[0:1, :] = a * x1 + b * y1
    out[1:2, :] = c * y1 + b * x1
    out[2:3, :] = -0.5 * xx - xy * (0.5 * r * (root / a))
    out[3:4, :] = -0.5 * yy - xy * (0.5 * r * (root / c))
    out[4:5, :] = -xy * root
    out[5:6, :] = m_1 / opacity[...]
    out[6:9, :] = rows[6:9, :]


def struct(*shape, dtype=F32):
    return jax.ShapeDtypeStruct(shape, dtype)


def shards(tile_lists, send_rows, centres, conic, rho, opacity, colors, target):
    devices = lax.axis_size("dev")
    owned = centres.shape[1]
    tiles, count = tile_lists.shape
    height, width = target.shape[1], target.shape[2]
    pixels = height * height
    params = pltpu.CompilerParams(vmem_limit_bytes=48 << 20)
    outgoing = pl.pallas_call(
        owner_kernel,
        out_shape=struct(devices, SUB, LANE),
        scratch_shapes=[pltpu.VMEM((SUB, owned), F32), pltpu.VMEM((owned // LANE, LANE), F32)],
        name="owner_gather",
    )(send_rows, centres, conic, rho, opacity, colors)
    lists = tile_lists.reshape(tiles, SUB, count // SUB).transpose(0, 2, 1).reshape(tiles, 1, count)
    incoming = exchange(outgoing, 0)
    whole = lambda *shape: pl.BlockSpec(shape, lambda t: (0,) * len(shape))
    per_tile = lambda *shape: pl.BlockSpec((1,) + shape, lambda t: (t,) + (0,) * len(shape))
    image, chunk_rend, chunk_start, left = pl.pallas_call(
        forward_kernel,
        grid=(tiles,),
        in_specs=[per_tile(1, count), whole(devices, SUB, LANE)],
        out_specs=[
            whole(3, height, width), per_tile(3, 2, SUB, pixels), per_tile(2, SUB, pixels), per_tile(count, 32)
        ],
        out_shape=[
            struct(3, height, width),
            struct(tiles, 3, 2, SUB, pixels),
            struct(tiles, 2, SUB, pixels),
            struct(tiles, count, 32, dtype=BF16),
        ],
        scratch_shapes=[
            pltpu.VMEM((devices // 2, SUB, LANE), F32),
            pltpu.VMEM((devices // 2, LANE), F32),
            pltpu.VMEM((count, LANE), F32),
            pltpu.VMEM((count, pixels), F32),
            pltpu.VMEM((3, tiles, pixels), F32),
        ],
        compiler_params=params,
        name="tile_forward",
    )(lists, incoming)

    up = [(i, i + 1) for i in range(devices - 1)]
    down = [(j, i) for i, j in up]
    me = lax.axis_index("dev")
    where = jnp.stack([me, devices * height]).astype(jnp.int32)
    pixel_grad = pl.pallas_call(
        loss_kernel,
        in_specs=[pl.BlockSpec(memory_space=pltpu.SMEM)] + [pl.BlockSpec(memory_space=pltpu.VMEM)] * 6,
        out_shape=struct(3, height, width),
        scratch_shapes=[pltpu.VMEM((5, 3 * height, width), F32), pltpu.VMEM((3, 2 * height, width), F32)],
        name="loss_gradient",
    )(
        where,
        lax.ppermute(image, "dev", up), image, lax.ppermute(image, "dev", down),
        lax.ppermute(target, "dev", up), target, lax.ppermute(target, "dev", down),
    )
    hi_blocks = devices * 64 // 256
    slot_grads = pl.pallas_call(
        backward_kernel,
        grid=(tiles,),
        in_specs=[
            whole(tiles, 1, count), per_tile(count, 32), whole(3, height, width),
            per_tile(3, 2, SUB, pixels), per_tile(2, SUB, pixels),
        ],
        out_specs=whole(devices, SUB, LANE),
        out_shape=struct(devices, SUB, LANE),
        scratch_shapes=[
            pltpu.VMEM((tiles, 3, pixels), F32),
            pltpu.VMEM((count, 3 * pixels), BF16),
            pltpu.VMEM((tiles, 16, count), F32),
            pltpu.VMEM((hi_blocks * (SUB + 1), 256), F32),
        ],
        compiler_params=params,
        name="tile_backward",
    )(lists, left, pixel_grad, chunk_rend, chunk_start)
    returned = exchange(slot_grads, 1)
    grads = pl.pallas_call(
        home_kernel,
        out_shape=struct(9, owned),
        scratch_shapes=[
            pltpu.VMEM((owned // 256 * (SUB + 1), 256), F32),
            pltpu.VMEM((16, owned), F32),
        ],
        name="owner_scatter",
    )(returned, send_rows, centres, conic, rho, opacity)
    return image, grads


def solution(mesh):
    return jax.shard_map(
        shards,
        mesh=mesh,
        in_specs=(
            P("dev", None),
            P("dev", None),
            P(None, "dev"),
            P(None, "dev"),
            P(None, "dev"),
            P(None, "dev"),
            P(None, "dev"),
            P(None, "dev", None),
        ),
        out_specs=(P(None, "dev", None), P(None, "dev")),
        check_vma=False,
    )
```

```python
import functools
import math

import jax
import jax.numpy as jnp
import numpy as np
from jax import lax
from jax.experimental import pallas as pl
from jax.experimental.pallas import tpu as pltpu
from jax.sharding import PartitionSpec as P

F32 = jnp.float32
BF16 = jnp.bfloat16
LOG2E = math.log2(math.e)
SUB, LANE = 8, 128
DEAD = -10000.0


def lane_pick(table, lanes):
    return jnp.take_along_axis(table, lanes, axis=1, mode="promise_in_bounds")


def iota(shape, dim):
    return lax.broadcasted_iota(jnp.int32, shape, dim)


def sub_sum(x):
    for d in (4, 2, 1):
        x = x + pltpu.roll(x, d, 0)
    return x


def split2(x):
    one = x.astype(BF16).astype(F32)
    return one, x - one


def coefficient_rows(cx, cy, a, c, rho, op):
    b = rho * jnp.sqrt(a * c)
    bx, by = a * cx + b * cy, c * cy + b * cx
    one = jnp.log(op) - 0.5 * (cx * bx + cy * by)
    return [LOG2E * k for k in (-0.5 * a, -b, -0.5 * c, bx, by, one)]


def pick_tree(parts, bits):
    if len(parts) == 1:
        return parts[0]()
    half = len(parts) // 2
    return jnp.where(bits[half], pick_tree(parts[half:], bits), pick_tree(parts[:half], bits))


def pick_nine(table, ninth, idx, row, blocks):
    hi, lo = lax.shift_right_logical(idx, 7), lax.bitwise_and(idx, 127)
    bits = {1 << k: lax.bitwise_and(hi, 1 << k) != 0 for k in range(blocks.bit_length() - 1)}
    eight = pick_tree([lambda h=h: lane_pick(table(h), lo) for h in range(blocks)], bits)
    coarse = {k // SUB: v for k, v in bits.items() if k >= SUB}
    last = pick_tree(
        [lambda v=v: lane_pick(ninth[v * SUB : (v + 1) * SUB, :], lo) for v in range(blocks // SUB)], coarse
    )
    return eight, sub_sum(jnp.where(lax.bitwise_and(hi, 7) == row, last, 0.0))


def owner_kernel(send, centres, conic, rho, opacity, colors, out, table, ninth):
    rows = coefficient_rows(
        centres[0:1, :], centres[1:2, :], conic[0:1, :], conic[1:2, :], rho[...], opacity[...]
    )
    for p, row in enumerate(rows + [colors[0:1, :], colors[1:2, :]]):
        table[p : p + 1, :] = row
    blocks = table.shape[1] // LANE
    for h in range(blocks):
        ninth[h : h + 1, :] = colors[2:3, h * LANE : (h + 1) * LANE]
    left = iota((SUB, LANE), 1) < 64
    row = iota((SUB, LANE), 0)
    step = 4

    def pairs(ii, carry):
        for k in range(step):
            i = ii * step + k
            start = pl.multiple_of(i * LANE, LANE)
            idx = jnp.broadcast_to(jnp.maximum(send[0:1, pl.ds(start, LANE)], 0), (SUB, LANE))
            eight, last = pick_nine(lambda h: table[:, h * LANE : (h + 1) * LANE], ninth, idx, row, blocks)
            out[2 * i], out[2 * i + 1] = pack_pair(eight, last, left, row)
        return carry

    lax.fori_loop(0, send.shape[1] // LANE // step, pairs, 0)


MESH = pl.DeviceIdType.MESH
USED = 5


def pack_pair(eight, last, left, row):
    low = pltpu.roll(eight, 4, 0)
    even = jnp.where(left, eight, pltpu.roll(low, 64, 1))
    odd = jnp.where(left, pltpu.roll(eight, 64, 1), low)
    return jnp.where(row < 4, even, last), jnp.where(row < 4, odd, pltpu.roll(last, 64, 1))


def unpack_pair(even, odd, left, row):
    high = jnp.where(left, even, pltpu.roll(odd, 64, 1))
    low = jnp.where(left, pltpu.roll(even, 64, 1), odd)
    return jnp.where(row < 4, high, pltpu.roll(low, 4, 0)), high[4:5, :]


def greet_all(n, me):
    barrier = pltpu.get_barrier_semaphore()

    def greet(k, carry):
        pl.semaphore_signal(barrier, inc=1, device_id=(lax.rem(me + k, n),), device_id_type=MESH)
        return carry

    lax.fori_loop(1, n, greet, 0)
    return barrier


def halo_copies(n, me, strip, before, after, send_sem, recv_sem):
    return [
        pltpu.make_async_remote_copy(
            src_ref=strip, dst_ref=to, send_sem=send_sem.at[k], recv_sem=recv_sem.at[k],
            device_id=(lax.rem(me + hop, n),), device_id_type=MESH,
        )
        for k, (hop, to) in enumerate(((1, before), (n - 1, after)))
    ]


def exchange_kernel(halo, *refs):
    if halo:
        x, strip, out, before, after, local_sem, send_sem, recv_sem, halo_send, halo_recv = refs
    else:
        x, out, local_sem, send_sem, recv_sem = refs
    me = lax.axis_index("dev")
    n = lax.axis_size("dev")
    rows = pl.ds(0, USED)
    barrier = greet_all(n, me)
    own = pltpu.make_async_copy(x.at[me, rows], out.at[me, rows], local_sem)
    own.start()
    pl.semaphore_wait(barrier, n - 1)

    def start(k, carry):
        peer = lax.rem(me + k, n)
        pltpu.make_async_remote_copy(
            src_ref=x.at[peer, rows], dst_ref=out.at[me, rows], send_sem=send_sem, recv_sem=recv_sem,
            device_id=(peer,), device_id_type=MESH,
        ).start()
        return carry

    lax.fori_loop(1, n, start, 0)
    copies = halo_copies(n, me, strip, before, after, halo_send, halo_recv) if halo else []
    for copy in copies:
        copy.start()
    own.wait()
    rest = pl.ds(0, n - 1)
    pltpu.make_async_copy(x.at[rest, rows], x.at[rest, rows], send_sem).wait()
    pltpu.make_async_copy(out.at[rest, rows], out.at[rest, rows], recv_sem).wait()
    for copy in copies:
        copy.wait()


def comm_params(number):
    return pltpu.CompilerParams(collective_id=number, has_side_effects=True, vmem_limit_bytes=4 << 20)


def exchange(x, number, strip=None):
    vmem = pl.BlockSpec(memory_space=pltpu.VMEM)
    halo = strip is not None
    like = lambda v: jax.ShapeDtypeStruct(v.shape, v.dtype)
    return pl.pallas_call(
        functools.partial(exchange_kernel, halo),
        out_shape=[like(x)] + [like(strip)] * 2 if halo else like(x),
        in_specs=[vmem] * (2 if halo else 1),
        out_specs=[vmem] * 3 if halo else vmem,
        scratch_shapes=[pltpu.SemaphoreType.DMA] * 3 + [pltpu.SemaphoreType.DMA((2,))] * (2 if halo else 0),
        compiler_params=comm_params(number),
        name="exchange",
    )(*([x, strip] if halo else [x]))


def halo_kernel(strip, before, after, send_sem, recv_sem):
    me = lax.axis_index("dev")
    n = lax.axis_size("dev")
    barrier = pltpu.get_barrier_semaphore()
    for hop in (1, n - 1):
        pl.semaphore_signal(barrier, inc=1, device_id=(lax.rem(me + hop, n),), device_id_type=MESH)
    pl.semaphore_wait(barrier, 2)
    copies = halo_copies(n, me, strip, before, after, send_sem, recv_sem)
    for copy in copies:
        copy.start()
    for copy in copies:
        copy.wait()


def halo_strips(strip, number):
    vmem = pl.BlockSpec(memory_space=pltpu.VMEM)
    return pl.pallas_call(
        halo_kernel,
        out_shape=[jax.ShapeDtypeStruct(strip.shape, strip.dtype)] * 2,
        in_specs=[vmem],
        out_specs=[vmem] * 2,
        scratch_shapes=[pltpu.SemaphoreType.DMA((2,))] * 2,
        compiler_params=comm_params(number),
        name="halo",
    )(strip)


def block_transpose(x):
    row = iota(x.shape, 0)
    block = lax.shift_right_logical(iota(x.shape, 1), 4)
    for d in (1, 2, 4):
        low_row = lax.bitwise_and(row, d) == 0
        low_block = lax.bitwise_and(block, d) == 0
        down = pltpu.roll(pltpu.roll(x, SUB - d, 0), 16 * d, 1)
        back = pltpu.roll(pltpu.roll(x, d, 0), LANE - 16 * d, 1)
        x = jnp.where(low_row == low_block, x, jnp.where(low_row, down, back))
    return x


def basis_rows(lanes):
    pixel = iota((1, lanes), 1)
    v = lax.shift_right_logical(pixel, 4).astype(F32) - 7.5
    u = lax.bitwise_and(pixel, 15).astype(F32) - 7.5
    return [u * u, u * v, v * v, u, v, jnp.ones_like(u)]


def stack_rows(rows, count):
    shape = (count, next(r for r in rows if r is not None).shape[1])
    at = iota(shape, 0)
    result = jnp.zeros(shape, F32)
    for p, row in enumerate(rows):
        if row is not None:
            result = jnp.where(at == p, jnp.broadcast_to(row, shape), result)
    return result


def scan_sub(x):
    at = iota(x.shape, 0)
    x = jnp.where(at == 0, 1.0, pltpu.roll(x, 1, 0))
    for d in (1, 2, 4):
        x = x * jnp.where(at >= d, pltpu.roll(x, d, 0), 1.0)
    return x


def segments(count):
    groups = count // SUB // 2
    return [(seg, j, (seg * groups + j) * SUB) for j in range(groups) for seg in range(2)]


def forward_kernel(lists, recv, image, chunk_rend, chunk_start, left_out, table, ninth, cols, alphas, rends):
    tile = pl.program_id(0)
    row = iota((SUB, LANE), 0)

    @pl.when(tile == 0)
    def _():
        def pair(h, carry):
            left = iota((SUB, LANE), 1) < 64
            table[h], ninth[pl.ds(h, 1), :] = unpack_pair(recv[2 * h], recv[2 * h + 1], left, row)
            return carry

        lax.fori_loop(0, recv.shape[0] // 2, pair, 0)

    blocks = table.shape[0]
    count = lists.shape[2]
    for q in range(count // LANE):
        span = slice(q * LANE, (q + 1) * LANE)
        raw = jnp.broadcast_to(lists[0, 0:1, span], (SUB, LANE))
        acc, last = pick_nine(lambda h: table[h], ninth, jnp.maximum(raw, 0), row, blocks)
        acc = jnp.where((row == 5) & (raw < 0), DEAD, acc)
        one, rest = split2(acc)
        two, three = split2(rest)
        b_one, b_two = split2(last)
        more = jnp.where(row == 1, b_two, jnp.where(row == 7, last, b_one))
        more = jnp.where((row == 3) | (row == 4), pltpu.roll(one, 5, 0), more)
        more = jnp.where((row == 5) | (row == 6), pltpu.roll(acc, 7, 0), more)
        stack = jnp.concatenate([one, two, three, more], axis=0)
        cols[span, :] = jnp.concatenate([stack, jnp.zeros((LANE - 32, LANE), F32)], axis=0).T

    basis = stack_rows((basis_rows(256) + [None, None]) * 3, 32).astype(BF16)
    ones = jnp.ones((SUB, 256), F32)
    product = [ones, ones]
    piece = 64
    for c in range(count // piece):
        span = slice(c * piece, (c + 1) * piece)
        left = cols[span, 0:32].astype(BF16)
        left_out[0, span, :] = left
        alpha = jnp.exp2(jnp.dot(left, basis, preferred_element_type=F32))
        alphas[span, :] = alpha
        rest = 1.0 - alpha
        parts = [rest[k * SUB : (k + 1) * SUB, :] for k in range(piece // SUB)]
        while len(parts) > 1:
            parts = [parts[k] * parts[k + 1] for k in range(0, len(parts), 2)]
        seg = 2 * c * piece // count
        product[seg] = product[seg] * parts[0]

    begin = scan_sub(product[0] * product[1])
    trans = [begin, begin * product[0]]
    zero = jnp.zeros((SUB, 256), F32)
    sums = [[zero] * 3, [zero] * 3]
    for seg in range(2):
        chunk_start[0, seg] = trans[seg]
    for seg, j, at in segments(count):
        weight = trans[seg] * alphas[at : at + SUB, :]
        trans[seg] = trans[seg] - weight
        color = cols[at : at + SUB, :]
        sums[seg] = [t + weight * color[:, 29 + ch : 30 + ch] for ch, t in enumerate(sums[seg])]
    for ch in range(3):
        for seg in range(2):
            chunk_rend[0, ch, seg] = sums[seg][ch]
        rends[ch, pl.ds(tile, 1), :] = sub_sum(sums[0][ch] + sums[1][ch])[0:1, :]

    @pl.when(tile == pl.num_programs(0) - 1)
    def _():
        for ch in range(3):
            for g in range(rends.shape[1] // SUB):
                for h in range(2):
                    image[ch, h * SUB : (h + 1) * SUB, g * LANE : (g + 1) * LANE] = block_transpose(
                        rends[ch, g * SUB : (g + 1) * SUB, h * LANE : (h + 1) * LANE]
                    )


def taps_of():
    offsets = np.arange(11, dtype=np.float32) - np.float32(5)
    taps = np.exp(-offsets * offsets / np.float32(4.5)).astype(np.float32)
    return [float(t) for t in taps / taps.sum(dtype=np.float32)]


TAPS = taps_of()


def blur_rows(read, start, count):
    total = TAPS[5] * read(start, count)
    for m in range(1, 6):
        total = total + TAPS[5 + m] * (read(start - m, count) + read(start + m, count))
    return total


def blur_lanes(x):
    rows, width = x.shape
    pad = jnp.zeros((rows, LANE), F32)
    wide = jnp.concatenate([x, pad], axis=1)
    total = TAPS[5] * x
    for m in range(1, 6):
        both = pltpu.roll(wide, m, 1) + pltpu.roll(wide, width + LANE - m, 1)
        total = total + TAPS[5 + m] * both[:, :width]
    return total


def loss_kernel(before, centre, after, t_before, t_centre, t_after, grad, pads, maps):
    height = centre.shape[1]
    mine = lax.axis_index("dev")
    total_rows = lax.axis_size("dev") * height
    width = centre.shape[2]
    at = iota((2 * height, width), 0) - height // 2 + mine * height
    inside = (at >= 0) & (at < total_rows)
    for ch in range(3):
        for i, (r, t) in enumerate(((before, t_before), (centre, t_centre), (after, t_after))):
            span = slice(i * height, (i + 1) * height)
            rr, tt = r[ch], t[ch]
            if i != 1:
                keep = mine > 0 if i == 0 else mine < total_rows // height - 1
                rr, tt = jnp.where(keep, rr, 0.0), jnp.where(keep, tt, 0.0)
            pads[0, span, :] = rr
            pads[1, span, :] = tt
            pads[2, span, :] = rr * rr
            pads[3, span, :] = tt * tt
            pads[4, span, :] = rr * tt

        def wide_blur(k):
            vertical = blur_rows(lambda s, n: pads[k, s : s + n, :], height // 2, 2 * height)
            return blur_lanes(vertical)

        mr, mt, rr, tt, rt = (wide_blur(k) for k in range(5))
        cv = rt - mr * mt
        top1 = 2.0 * mr * mt + 0.0001
        top2 = 2.0 * cv + 0.0009
        low1 = mr * mr + mt * mt + 0.0001
        low2 = (rr - mr * mr) + (tt - mt * mt) + 0.0009
        inv1, inv2 = 1.0 / low1, 1.0 / low2
        both = inv1 * inv2
        ssim = top1 * top2 * both
        d_rr = -ssim * inv2
        d_rt = 2.0 * top1 * both
        d_mr = 2.0 * (mt * (top2 - top1) * both + mr * ssim * (inv2 - inv1))
        for k, value in enumerate((d_mr, d_rr, d_rt)):
            maps[k] = jnp.where(inside, value, 0.0)

        def back_blur(k):
            vertical = blur_rows(lambda s, n: maps[k, s : s + n, :], height // 2, height)
            return blur_lanes(vertical)

        g_mr, g_rr, g_rt = (back_blur(k) for k in range(3))
        r, t = centre[ch], t_centre[ch]
        grad[ch] = 1.6 * (r - t) - 0.2 * (g_mr + 2.0 * r * g_rr + t * g_rt)


NT = (((1,), (1,)), ((), ()))


def onehot(lo, rows):
    return jnp.where(iota((rows, lo.shape[1]), 0) == lo, 1.0, 0.0).astype(BF16)


def spread(values, hi, blocks):
    masked = [jnp.where(hi == h, values, 0.0) for h in range(blocks)]
    return jnp.concatenate(masked, axis=0)


def scatter_block(eight, ninth, idx, blocks):
    span = idx.shape[1]
    hi, lo = lax.shift_right_arithmetic(idx, 8), lax.bitwise_and(idx, 255)
    hot = onehot(lo, 256)
    hi8 = jnp.broadcast_to(hi, (SUB, span))
    own = iota((blocks, span), 0) == hi
    left = []
    for values, extra in zip(split2(eight), split2(ninth)):
        left.append(spread(values, hi8, blocks))
        left.append(jnp.where(own, jnp.broadcast_to(extra, own.shape), 0.0))
    left = jnp.concatenate(left, axis=0).astype(BF16)
    both = lax.dot_general(left, hot, NT, preferred_element_type=F32)
    return both[: blocks * (SUB + 1), :] + both[blocks * (SUB + 1) :, :]


def backward_kernel(lists, left_in, grad, chunk_rend, chunk_start, out, cots, halves, grads, slots):
    tile = pl.program_id(0)
    tiles = pl.num_programs(0)
    count = left_in.shape[1]

    @pl.when(tile == 0)
    def _():
        for ch in range(3):
            for g in range(cots.shape[0] // SUB):
                for h in range(2):
                    span = slice(h * LANE, (h + 1) * LANE)
                    block = block_transpose(grad[ch, h * SUB : (h + 1) * SUB, g * LANE : (g + 1) * LANE])
                    for t in range(SUB):
                        cots[g * SUB + t, ch : ch + 1, span] = block[t : t + 1, :]

    rows = [cots[tile, ch : ch + 1, :] for ch in range(3)]
    ones, twos = zip(*(split2(r) for r in rows))
    basis = stack_rows((basis_rows(256) + [None, None]) * 3, 32)
    back = stack_rows(
        [None] * 6 + [ones[0], ones[1]] + [None] * 6 + [ones[0], ones[1]] + [None] * 6
        + [ones[0], ones[1], ones[2], ones[2], twos[2], twos[0], twos[1]], 32
    )
    right = jnp.concatenate([basis, back], axis=1).astype(BF16)

    inside = [sum(chunk_rend[0, ch, seg] * rows[ch] for ch in range(3)) for seg in range(2)]
    at8 = iota((SUB, 256), 0)
    later = inside[0] + inside[1]
    later = jnp.where(at8 == SUB - 1, 0.0, pltpu.roll(later, SUB - 1, 0))
    for d in (1, 2, 4):
        later = later + jnp.where(at8 < SUB - d, pltpu.roll(later, SUB - d, 0), 0.0)
    behind = [later + inside[1] + inside[0], later + inside[1]]
    trans = [chunk_start[0, seg] for seg in range(2)]

    piece = 32
    order = [c // 2 + (c % 2) * (count // piece // 2) for c in range(count // piece)]
    for c in order:
        seg = 2 * c * piece // count
        field = jnp.dot(left_in[0, c * piece : (c + 1) * piece, :], right, preferred_element_type=F32)
        alpha = jnp.exp2(field[:, 0:256])
        ratio = alpha / (1.0 - alpha)
        parts = []
        for k in range(piece // SUB):
            span = slice(k * SUB, (k + 1) * SUB)
            weight = trans[seg] * alpha[span]
            trans[seg] = trans[seg] - weight
            shown = weight * field[span, 256:512]
            behind[seg] = behind[seg] - shown
            parts.append((shown - ratio[span] * behind[seg], weight))
        at = slice(c * piece, (c + 1) * piece)
        value = jnp.concatenate([p[0] for p in parts], axis=0)
        one = value.astype(BF16)
        halves[at, 0:256] = one
        halves[at, 256:512] = (value - one.astype(F32)).astype(BF16)
        halves[at, 512:768] = jnp.concatenate([p[1] for p in parts], axis=0).astype(BF16)

    base = stack_rows(basis_rows(256), 16)
    colours = stack_rows([None] * 6 + list(ones) + list(twos), 16)
    kernel = jnp.concatenate([base, base, colours], axis=1).astype(BF16)
    found = lax.dot_general(kernel, halves[...], NT, preferred_element_type=F32)
    low = found[8:16, :]
    at16 = iota(low.shape, 0)
    top = found[0:8, :] + jnp.where(at16 >= 6, pltpu.roll(low, 5, 0), 0.0)
    grads[tile, 0:8, :] = top
    grads[tile, 8:9, :] = low[0:1, :] + low[3:4, :]

    @pl.when(tile == tiles - 1)
    def _():
        slots[...] = jnp.zeros_like(slots)
        blocks = slots.shape[0] // (SUB + 1)
        per = 2

        def chunk(c, carry):
            each = [c * per + k for k in range(per)]
            idx = jnp.concatenate([jnp.maximum(lists[t], 0) for t in each], axis=1)
            eight = jnp.concatenate([grads[t, 0:8, :] for t in each], axis=1)
            ninth = jnp.concatenate([grads[t, 8:9, :] for t in each], axis=1)
            slots[...] = slots[...] + scatter_block(eight, ninth, idx, blocks)
            return carry

        lax.fori_loop(0, cots.shape[0] // per, chunk, 0)
        left = iota((SUB, LANE), 1) < 64
        row = iota((SUB, LANE), 0)
        for h in range(blocks):
            for half in range(2):
                span = slice(half * LANE, (half + 1) * LANE)
                acc = slots[h * SUB : (h + 1) * SUB, span]
                extra = jnp.broadcast_to(slots[blocks * SUB + h : blocks * SUB + h + 1, span], (SUB, LANE))
                owner = 4 * h + 2 * half
                out[owner], out[owner + 1] = pack_pair(acc, extra, left, row)


def home_kernel(back, send, centres, conic, rho, opacity, out, total, rows):
    lane = iota((SUB, LANE), 1)
    left = lane < 64
    row = iota((SUB, LANE), 0)
    pairs = back.shape[0] // 2
    per = 8
    blocks = centres.shape[1] // 256
    total[...] = jnp.zeros_like(total)

    def chunk(c, carry):
        eight, ninth = [], []
        for k in range(per):
            i = c * per + k
            values, last = unpack_pair(back[2 * i], back[2 * i + 1], left, row)
            eight.append(values)
            ninth.append(last)
        start = pl.multiple_of(c * per * LANE, per * LANE)
        idx = send[0:1, pl.ds(start, per * LANE)]
        total[...] = total[...] + scatter_block(
            jnp.concatenate(eight, axis=1), jnp.concatenate(ninth, axis=1), idx, blocks
        )
        return carry

    lax.fori_loop(0, pairs // per, chunk, 0)
    for h in range(blocks):
        span = slice(h * 256, (h + 1) * 256)
        rows[0:8, span] = total[h * SUB : (h + 1) * SUB, :]
        rows[8:9, span] = total[blocks * SUB + h : blocks * SUB + h + 1, :]
    m_uu, m_uv, m_vv, m_u, m_v, m_1 = (rows[p : p + 1, :] for p in range(6))
    cx, cy = centres[0:1, :], centres[1:2, :]
    a, c = conic[0:1, :], conic[1:2, :]
    r = rho[...]
    root = jnp.sqrt(a * c)
    b = r * root
    x1, y1 = m_u - cx * m_1, m_v - cy * m_1
    xx = m_uu - cx * (m_u + x1)
    yy = m_vv - cy * (m_v + y1)
    xy = m_uv - cx * m_v - cy * x1
    out[0:1, :] = a * x1 + b * y1
    out[1:2, :] = c * y1 + b * x1
    out[2:3, :] = -0.5 * xx - xy * (0.5 * r * (root / a))
    out[3:4, :] = -0.5 * yy - xy * (0.5 * r * (root / c))
    out[4:5, :] = -xy * root
    out[5:6, :] = m_1 / opacity[...]
    out[6:9, :] = rows[6:9, :]


def struct(*shape, dtype=F32):
    return jax.ShapeDtypeStruct(shape, dtype)


def shards(tile_lists, send_rows, centres, conic, rho, opacity, colors, target):
    devices = lax.axis_size("dev")
    owned = centres.shape[1]
    tiles, count = tile_lists.shape
    height, width = target.shape[1], target.shape[2]
    pixels = height * height
    params = lambda mib: pltpu.CompilerParams(vmem_limit_bytes=mib << 20)
    outgoing = pl.pallas_call(
        owner_kernel,
        out_shape=struct(devices, SUB, LANE),
        scratch_shapes=[pltpu.VMEM((SUB, owned), F32), pltpu.VMEM((owned // LANE, LANE), F32)],
        compiler_params=params(8),
        name="owner_gather",
    )(send_rows, centres, conic, rho, opacity, colors)
    lists = tile_lists.reshape(tiles, SUB, count // SUB).transpose(0, 2, 1).reshape(tiles, 1, count)
    incoming, t_before, t_after = exchange(outgoing, 0, target)
    whole = lambda *shape: pl.BlockSpec(shape, lambda t: (0,) * len(shape))
    per_tile = lambda *shape: pl.BlockSpec((1,) + shape, lambda t: (t,) + (0,) * len(shape))
    image, chunk_rend, chunk_start, left = pl.pallas_call(
        forward_kernel,
        grid=(tiles,),
        in_specs=[per_tile(1, count), whole(devices, SUB, LANE)],
        out_specs=[
            whole(3, height, width), per_tile(3, 2, SUB, pixels), per_tile(2, SUB, pixels), per_tile(count, 32)
        ],
        out_shape=[
            struct(3, height, width),
            struct(tiles, 3, 2, SUB, pixels),
            struct(tiles, 2, SUB, pixels),
            struct(tiles, count, 32, dtype=BF16),
        ],
        scratch_shapes=[
            pltpu.VMEM((devices // 2, SUB, LANE), F32),
            pltpu.VMEM((devices // 2, LANE), F32),
            pltpu.VMEM((count, LANE), F32),
            pltpu.VMEM((count, pixels), F32),
            pltpu.VMEM((3, tiles, pixels), F32),
        ],
        compiler_params=params(16),
        name="tile_forward",
    )(lists, incoming)

    before, after = halo_strips(image, 1)
    pixel_grad = pl.pallas_call(
        loss_kernel,
        out_shape=struct(3, height, width),
        scratch_shapes=[pltpu.VMEM((5, 3 * height, width), F32), pltpu.VMEM((3, 2 * height, width), F32)],
        compiler_params=params(8),
        name="loss_gradient",
    )(before, image, after, t_before, target, t_after)

    hi_blocks = devices * 64 // 256
    slot_grads = pl.pallas_call(
        backward_kernel,
        grid=(tiles,),
        in_specs=[
            whole(tiles, 1, count), per_tile(count, 32), whole(3, height, width),
            per_tile(3, 2, SUB, pixels), per_tile(2, SUB, pixels),
        ],
        out_specs=whole(devices, SUB, LANE),
        out_shape=struct(devices, SUB, LANE),
        scratch_shapes=[
            pltpu.VMEM((tiles, 3, pixels), F32),
            pltpu.VMEM((count, 3 * pixels), BF16),
            pltpu.VMEM((tiles, 16, count), F32),
            pltpu.VMEM((hi_blocks * (SUB + 1), 256), F32),
        ],
        compiler_params=params(20),
        name="tile_backward",
    )(lists, left, pixel_grad, chunk_rend, chunk_start)
    returned = exchange(slot_grads, 2)
    grads = pl.pallas_call(
        home_kernel,
        out_shape=struct(9, owned),
        scratch_shapes=[
            pltpu.VMEM((owned // 256 * (SUB + 1), 256), F32),
            pltpu.VMEM((16, owned), F32),
        ],
        compiler_params=params(16),
        name="owner_scatter",
    )(returned, send_rows, centres, conic, rho, opacity)
    return image, grads


def solution(mesh):
    return jax.shard_map(
        shards,
        mesh=mesh,
        in_specs=(
            P("dev", None),
            P("dev", None),
            P(None, "dev"),
            P(None, "dev"),
            P(None, "dev"),
            P(None, "dev"),
            P(None, "dev"),
            P(None, "dev", None),
        ),
        out_specs=(P(None, "dev", None), P(None, "dev")),
        check_vma=False,
    )
```

```python
import functools
import math

import jax
import jax.numpy as jnp
import numpy as np
from jax import lax
from jax.experimental import pallas as pl
from jax.experimental.pallas import tpu as pltpu
from jax.sharding import PartitionSpec as P

F32 = jnp.float32
BF16 = jnp.bfloat16
LOG2E = math.log2(math.e)
SUB, LANE = 8, 128
DEAD = -10000.0


def lane_pick(table, lanes):
    return jnp.take_along_axis(table, lanes, axis=1, mode="promise_in_bounds")


def iota(shape, dim):
    return lax.broadcasted_iota(jnp.int32, shape, dim)


def sub_sum(x):
    for d in (4, 2, 1):
        x = x + pltpu.roll(x, d, 0)
    return x


def split2(x):
    one = x.astype(BF16).astype(F32)
    return one, x - one


def coefficient_rows(cx, cy, a, c, rho, op):
    b = rho * jnp.sqrt(a * c)
    bx, by = a * cx + b * cy, c * cy + b * cx
    one = jnp.log(op) - 0.5 * (cx * bx + cy * by)
    return [LOG2E * k for k in (-0.5 * a, -b, -0.5 * c, bx, by, one)]


def pick_tree(parts, bits):
    if len(parts) == 1:
        return parts[0]()
    half = len(parts) // 2
    return jnp.where(bits[half], pick_tree(parts[half:], bits), pick_tree(parts[:half], bits))


def pick_nine(table, ninth, idx, row, blocks):
    hi, lo = lax.shift_right_logical(idx, 7), lax.bitwise_and(idx, 127)
    bits = {1 << k: lax.bitwise_and(hi, 1 << k) != 0 for k in range(blocks.bit_length() - 1)}
    eight = pick_tree([lambda h=h: lane_pick(table(h), lo) for h in range(blocks)], bits)
    coarse = {k // SUB: v for k, v in bits.items() if k >= SUB}
    last = pick_tree(
        [lambda v=v: lane_pick(ninth[v * SUB : (v + 1) * SUB, :], lo) for v in range(blocks // SUB)], coarse
    )
    return eight, sub_sum(jnp.where(lax.bitwise_and(hi, 7) == row, last, 0.0))


def owner_kernel(*refs):
    sources, (out, table, ninth), places, sems = refs[:6], refs[6:9], refs[9:15], refs[15]
    copies = [pltpu.make_async_copy(a, b, sems.at[k]) for k, (a, b) in enumerate(zip(sources, places))]
    for copy in copies:
        copy.start()
    for copy in copies:
        copy.wait()
    send, centres, conic, rho, opacity, colors = places
    rows = coefficient_rows(
        centres[0:1, :], centres[1:2, :], conic[0:1, :], conic[1:2, :], rho[...], opacity[...]
    )
    for p, row in enumerate(rows + [colors[0:1, :], colors[1:2, :]]):
        table[p : p + 1, :] = row
    blocks = table.shape[1] // LANE
    for h in range(blocks):
        ninth[h : h + 1, :] = colors[2:3, h * LANE : (h + 1) * LANE]
    left = iota((SUB, LANE), 1) < 64
    row = iota((SUB, LANE), 0)
    step = 4

    def pairs(ii, carry):
        for k in range(step):
            i = ii * step + k
            start = pl.multiple_of(i * LANE, LANE)
            idx = jnp.broadcast_to(jnp.maximum(send[0:1, pl.ds(start, LANE)], 0), (SUB, LANE))
            eight, last = pick_nine(lambda h: table[:, h * LANE : (h + 1) * LANE], ninth, idx, row, blocks)
            out[2 * i], out[2 * i + 1] = pack_pair(eight, last, left, row)
        return carry

    lax.fori_loop(0, send.shape[1] // LANE // step, pairs, 0)


MESH = pl.DeviceIdType.MESH
USED = 5


def pack_pair(eight, last, left, row):
    low = pltpu.roll(eight, 4, 0)
    even = jnp.where(left, eight, pltpu.roll(low, 64, 1))
    odd = jnp.where(left, pltpu.roll(eight, 64, 1), low)
    return jnp.where(row < 4, even, last), jnp.where(row < 4, odd, pltpu.roll(last, 64, 1))


def unpack_pair(even, odd, left, row):
    high = jnp.where(left, even, pltpu.roll(odd, 64, 1))
    low = jnp.where(left, pltpu.roll(even, 64, 1), odd)
    return jnp.where(row < 4, high, pltpu.roll(low, 4, 0)), high[4:5, :]


def greet_all(n, me):
    barrier = pltpu.get_barrier_semaphore()

    def greet(k, carry):
        pl.semaphore_signal(barrier, inc=1, device_id=(lax.rem(me + k, n),), device_id_type=MESH)
        return carry

    lax.fori_loop(1, n, greet, 0)
    return barrier


def halo_copies(n, me, strip, before, after, send_sem, recv_sem):
    return [
        pltpu.make_async_remote_copy(
            src_ref=strip, dst_ref=to, send_sem=send_sem.at[k], recv_sem=recv_sem.at[k],
            device_id=(lax.rem(me + hop, n),), device_id_type=MESH,
        )
        for k, (hop, to) in enumerate(((1, before), (n - 1, after)))
    ]


def exchange_kernel(halo, *refs):
    if halo:
        x, strip, out, before, centre, after, local_sem, send_sem, recv_sem, halo_send, halo_recv = refs
    else:
        x, out, local_sem, send_sem, recv_sem = refs
    me = lax.axis_index("dev")
    n = lax.axis_size("dev")
    rows = pl.ds(0, USED)
    barrier = greet_all(n, me)
    own = pltpu.make_async_copy(x.at[me, rows], out.at[me, rows], local_sem)
    own.start()
    pl.semaphore_wait(barrier, n - 1)

    def start(k, carry):
        peer = lax.rem(me + k, n)
        pltpu.make_async_remote_copy(
            src_ref=x.at[peer, rows], dst_ref=out.at[me, rows], send_sem=send_sem, recv_sem=recv_sem,
            device_id=(peer,), device_id_type=MESH,
        ).start()
        return carry

    lax.fori_loop(1, n, start, 0)
    copies = []
    if halo:
        copies = halo_copies(n, me, strip, before, after, halo_send, halo_recv)
        copies.append(pltpu.make_async_copy(strip, centre, halo_recv.at[2]))
    for copy in copies:
        copy.start()
    own.wait()
    rest = pl.ds(0, n - 1)
    pltpu.make_async_copy(x.at[rest, rows], x.at[rest, rows], send_sem).wait()
    pltpu.make_async_copy(out.at[rest, rows], out.at[rest, rows], recv_sem).wait()
    for copy in copies:
        copy.wait()


def comm_params(number):
    return pltpu.CompilerParams(collective_id=number, has_side_effects=True, vmem_limit_bytes=4 << 20)


def exchange(x, number, strip=None):
    vmem = pl.BlockSpec(memory_space=pltpu.VMEM)
    halo = strip is not None
    like = lambda v: jax.ShapeDtypeStruct(v.shape, v.dtype)
    return pl.pallas_call(
        functools.partial(exchange_kernel, halo),
        out_shape=[like(x)] + [like(strip)] * 3 if halo else like(x),
        in_specs=[vmem] + [pl.BlockSpec(memory_space=pltpu.HBM)] * halo,
        out_specs=[vmem] * 4 if halo else vmem,
        scratch_shapes=[pltpu.SemaphoreType.DMA] * 3 + [pltpu.SemaphoreType.DMA((3,))] * (2 if halo else 0),
        compiler_params=comm_params(number),
        name="exchange",
    )(*([x, strip] if halo else [x]))


def halo_kernel(strip, before, after, send_sem, recv_sem):
    me = lax.axis_index("dev")
    n = lax.axis_size("dev")
    barrier = pltpu.get_barrier_semaphore()
    for hop in (1, n - 1):
        pl.semaphore_signal(barrier, inc=1, device_id=(lax.rem(me + hop, n),), device_id_type=MESH)
    pl.semaphore_wait(barrier, 2)
    copies = halo_copies(n, me, strip, before, after, send_sem, recv_sem)
    for copy in copies:
        copy.start()
    for copy in copies:
        copy.wait()


def halo_strips(strip, number):
    vmem = pl.BlockSpec(memory_space=pltpu.VMEM)
    return pl.pallas_call(
        halo_kernel,
        out_shape=[jax.ShapeDtypeStruct(strip.shape, strip.dtype)] * 2,
        in_specs=[vmem],
        out_specs=[vmem] * 2,
        scratch_shapes=[pltpu.SemaphoreType.DMA((2,))] * 2,
        compiler_params=comm_params(number),
        name="halo",
    )(strip)


def block_transpose(x):
    row = iota(x.shape, 0)
    block = lax.shift_right_logical(iota(x.shape, 1), 4)
    for d in (1, 2, 4):
        low_row = lax.bitwise_and(row, d) == 0
        low_block = lax.bitwise_and(block, d) == 0
        down = pltpu.roll(pltpu.roll(x, SUB - d, 0), 16 * d, 1)
        back = pltpu.roll(pltpu.roll(x, d, 0), LANE - 16 * d, 1)
        x = jnp.where(low_row == low_block, x, jnp.where(low_row, down, back))
    return x


def basis_rows(lanes):
    pixel = iota((1, lanes), 1)
    v = lax.shift_right_logical(pixel, 4).astype(F32) - 7.5
    u = lax.bitwise_and(pixel, 15).astype(F32) - 7.5
    return [u * u, u * v, v * v, u, v, jnp.ones_like(u)]


def stack_rows(rows, count):
    shape = (count, next(r for r in rows if r is not None).shape[1])
    at = iota(shape, 0)
    result = jnp.zeros(shape, F32)
    for p, row in enumerate(rows):
        if row is not None:
            result = jnp.where(at == p, jnp.broadcast_to(row, shape), result)
    return result


def scan_sub(x):
    at = iota(x.shape, 0)
    x = jnp.where(at == 0, 1.0, pltpu.roll(x, 1, 0))
    for d in (1, 2, 4):
        x = x * jnp.where(at >= d, pltpu.roll(x, d, 0), 1.0)
    return x


def segments(count):
    groups = count // SUB // 2
    return [(seg, j, (seg * groups + j) * SUB) for j in range(groups) for seg in range(2)]


def split3(x):
    one, rest = split2(x)
    two, three = split2(rest)
    return one, two, three


def gather_columns(lists, flat, cols, slot):
    count = lists.shape[2]
    raw = lists[slot, 0:1, :]
    idx = jnp.maximum(raw, 0)
    hi, lo = lax.shift_right_logical(idx, 8), lax.bitwise_and(idx, 255)
    blocks = flat.shape[0] // (SUB + 1)
    hot = onehot(lo, 256)
    found = jnp.dot(flat[...], jnp.concatenate([hot] * 3, axis=0), preferred_element_type=F32)
    row = iota((SUB, LANE), 0)
    for q in range(count // LANE):
        span = slice(q * LANE, (q + 1) * LANE)
        hq = jnp.broadcast_to(hi[:, span], (SUB, LANE))
        bits = {1 << k: lax.bitwise_and(hq, 1 << k) != 0 for k in range(blocks.bit_length() - 1)}
        acc = pick_tree([lambda h=h: found[h * SUB : (h + 1) * SUB, span] for h in range(blocks)], bits)
        coarse = {k // SUB: v for k, v in bits.items() if k >= SUB}
        base = blocks * SUB
        last = pick_tree(
            [lambda v=v: found[base + v * SUB : base + (v + 1) * SUB, span] for v in range(blocks // SUB)], coarse
        )
        last = sub_sum(jnp.where(lax.bitwise_and(hq, 7) == row, last, 0.0))
        acc = jnp.where((row == 5) & (jnp.broadcast_to(raw[:, span], (SUB, LANE)) < 0), DEAD, acc)
        one, two, three = split3(acc)
        b_one, b_two = split2(last)
        more = jnp.where(row == 1, b_two, jnp.where(row == 7, last, b_one))
        more = jnp.where((row == 3) | (row == 4), pltpu.roll(one, 5, 0), more)
        more = jnp.where((row == 5) | (row == 6), pltpu.roll(acc, 7, 0), more)
        stack = jnp.concatenate([one, two, three, more], axis=0)
        cols[slot, span, :] = jnp.concatenate([stack, jnp.zeros((LANE - 32, LANE), F32)], axis=0).T


def draw_tile(slot, tile, basis, chunk_rend, chunk_start, left_out, cols, alphas, rends):
    count = cols.shape[1]
    ones = jnp.ones((SUB, 256), F32)
    product = [ones, ones]
    piece = 64
    for c in range(count // piece):
        span = slice(c * piece, (c + 1) * piece)
        left = cols[slot, span, 0:32].astype(BF16)
        left_out[slot, span, :] = left
        alpha = jnp.exp2(jnp.dot(left, basis, preferred_element_type=F32))
        alphas[slot, span, :] = alpha
        rest = 1.0 - alpha
        parts = [rest[k * SUB : (k + 1) * SUB, :] for k in range(piece // SUB)]
        while len(parts) > 1:
            parts = [parts[k] * parts[k + 1] for k in range(0, len(parts), 2)]
        seg = 2 * c * piece // count
        product[seg] = product[seg] * parts[0]

    begin = scan_sub(product[0] * product[1])
    trans = [begin, begin * product[0]]
    zero = jnp.zeros((SUB, 256), F32)
    sums = [[zero] * 3, [zero] * 3]
    for seg in range(2):
        chunk_start[slot, seg] = trans[seg]
    for seg, j, at in segments(count):
        weight = trans[seg] * alphas[slot, at : at + SUB, :]
        trans[seg] = trans[seg] - weight
        color = cols[slot, at : at + SUB, :]
        sums[seg] = [t + weight * color[:, 29 + ch : 30 + ch] for ch, t in enumerate(sums[seg])]
    for ch in range(3):
        for seg in range(2):
            chunk_rend[slot, ch, seg] = sums[seg][ch]
        rends[ch, pl.ds(tile, 1), :] = sub_sum(sums[0][ch] + sums[1][ch])[0:1, :]


def forward_kernel(
    lists, recv, image, image_too, chunk_rend, chunk_start, left_out, pieces, ninth, flat, cols, alphas, rends
):
    step = pl.program_id(0)
    per = lists.shape[0]
    row = iota((SUB, LANE), 0)

    @pl.when(step == 0)
    def _():
        blocks = pieces.shape[0] // SUB
        left = iota((SUB, LANE), 1) < 64

        def block(h, carry):
            lasts = []
            for half in range(2):
                owner = 4 * h + 2 * half
                eight, last = unpack_pair(recv[owner], recv[owner + 1], left, row)
                pieces[pl.ds(pl.multiple_of(h * SUB, SUB), SUB), half * LANE : (half + 1) * LANE] = eight
                lasts.append(last)
            ninth[pl.ds(h, 1), :] = jnp.concatenate(lasts, axis=1)
            return carry

        lax.fori_loop(0, blocks, block, 0)
        for rows, source in ((slice(0, blocks * SUB), pieces), (slice(blocks * SUB, None), ninth)):
            for k, part in enumerate(split3(source[...])):
                flat[rows, k * 256 : (k + 1) * 256] = part.astype(BF16)

    basis = stack_rows((basis_rows(256) + [None, None]) * 3, 32).astype(BF16)
    for slot in range(per):
        gather_columns(lists, flat, cols, slot)
    for slot in range(per):
        draw_tile(slot, step * per + slot, basis, chunk_rend, chunk_start, left_out, cols, alphas, rends)

    @pl.when(step == pl.num_programs(0) - 1)
    def _():
        for ch in range(3):
            for g in range(rends.shape[1] // SUB):
                for h in range(2):
                    block = block_transpose(rends[ch, g * SUB : (g + 1) * SUB, h * LANE : (h + 1) * LANE])
                    for to in (image, image_too):
                        to[ch, h * SUB : (h + 1) * SUB, g * LANE : (g + 1) * LANE] = block


def taps_of():
    offsets = np.arange(11, dtype=np.float32) - np.float32(5)
    taps = np.exp(-offsets * offsets / np.float32(4.5)).astype(np.float32)
    return [float(t) for t in taps / taps.sum(dtype=np.float32)]


TAPS = taps_of()


def blur_rows(read, start, count):
    total = TAPS[5] * read(start, count)
    for m in range(1, 6):
        total = total + TAPS[5 + m] * (read(start - m, count) + read(start + m, count))
    return total


def blur_lanes(x):
    rows, width = x.shape
    pad = jnp.zeros((rows, LANE), F32)
    wide = jnp.concatenate([x, pad], axis=1)
    total = TAPS[5] * x
    for m in range(1, 6):
        both = pltpu.roll(wide, m, 1) + pltpu.roll(wide, width + LANE - m, 1)
        total = total + TAPS[5 + m] * both[:, :width]
    return total


def loss_kernel(before, centre, after, t_before, t_centre, t_after, grad, pads, maps):
    height = centre.shape[1]
    mine = lax.axis_index("dev")
    total_rows = lax.axis_size("dev") * height
    width = centre.shape[2]
    at = iota((2 * height, width), 0) - height // 2 + mine * height
    inside = (at >= 0) & (at < total_rows)
    for ch in range(3):
        for i, (r, t) in enumerate(((before, t_before), (centre, t_centre), (after, t_after))):
            span = slice(i * height, (i + 1) * height)
            rr, tt = r[ch], t[ch]
            if i != 1:
                keep = mine > 0 if i == 0 else mine < total_rows // height - 1
                rr, tt = jnp.where(keep, rr, 0.0), jnp.where(keep, tt, 0.0)
            pads[0, span, :] = rr
            pads[1, span, :] = tt
            pads[2, span, :] = rr * rr
            pads[3, span, :] = tt * tt
            pads[4, span, :] = rr * tt

        def wide_blur(k):
            vertical = blur_rows(lambda s, n: pads[k, s : s + n, :], height // 2, 2 * height)
            return blur_lanes(vertical)

        mr, mt, rr, tt, rt = (wide_blur(k) for k in range(5))
        cv = rt - mr * mt
        top1 = 2.0 * mr * mt + 0.0001
        top2 = 2.0 * cv + 0.0009
        low1 = mr * mr + mt * mt + 0.0001
        low2 = (rr - mr * mr) + (tt - mt * mt) + 0.0009
        inv1, inv2 = 1.0 / low1, 1.0 / low2
        both = inv1 * inv2
        ssim = top1 * top2 * both
        d_rr = -ssim * inv2
        d_rt = 2.0 * top1 * both
        d_mr = 2.0 * (mt * (top2 - top1) * both + mr * ssim * (inv2 - inv1))
        for k, value in enumerate((d_mr, d_rr, d_rt)):
            maps[k] = jnp.where(inside, value, 0.0)

        def back_blur(k):
            vertical = blur_rows(lambda s, n: maps[k, s : s + n, :], height // 2, height)
            return blur_lanes(vertical)

        g_mr, g_rr, g_rt = (back_blur(k) for k in range(3))
        r, t = centre[ch], t_centre[ch]
        grad[ch] = 1.6 * (r - t) - 0.2 * (g_mr + 2.0 * r * g_rr + t * g_rt)


NT = (((1,), (1,)), ((), ()))


def onehot(lo, rows):
    return jnp.where(iota((rows, lo.shape[1]), 0) == lo, 1.0, 0.0).astype(BF16)


def spread(values, hi, blocks):
    masked = [jnp.where(hi == h, values, 0.0) for h in range(blocks)]
    return jnp.concatenate(masked, axis=0)


def scatter_block(eight, ninth, idx, blocks):
    span = idx.shape[1]
    hi, lo = lax.shift_right_arithmetic(idx, 8), lax.bitwise_and(idx, 255)
    hot = onehot(lo, 256)
    hi8 = jnp.broadcast_to(hi, (SUB, span))
    own = iota((blocks, span), 0) == hi
    left = []
    for values, extra in zip(split2(eight), split2(ninth)):
        left.append(spread(values, hi8, blocks))
        left.append(jnp.where(own, jnp.broadcast_to(extra, own.shape), 0.0))
    left = jnp.concatenate(left, axis=0).astype(BF16)
    both = lax.dot_general(left, hot, NT, preferred_element_type=F32)
    return both[: blocks * (SUB + 1), :] + both[blocks * (SUB + 1) :, :]


def shade_tile(slot, tile, left_in, chunk_rend, chunk_start, cots, halves, grads):
    count = left_in.shape[1]
    rows = [cots[tile, ch : ch + 1, :] for ch in range(3)]
    ones, twos = zip(*(split2(r) for r in rows))
    basis = stack_rows((basis_rows(256) + [None, None]) * 3, 32)
    back = stack_rows(
        [None] * 6 + [ones[0], ones[1]] + [None] * 6 + [ones[0], ones[1]] + [None] * 6
        + [ones[0], ones[1], ones[2], ones[2], twos[2], twos[0], twos[1]], 32
    )
    right = jnp.concatenate([basis, back], axis=1).astype(BF16)

    inside = [sum(chunk_rend[slot, ch, seg] * rows[ch] for ch in range(3)) for seg in range(2)]
    at8 = iota((SUB, 256), 0)
    later = inside[0] + inside[1]
    later = jnp.where(at8 == SUB - 1, 0.0, pltpu.roll(later, SUB - 1, 0))
    for d in (1, 2, 4):
        later = later + jnp.where(at8 < SUB - d, pltpu.roll(later, SUB - d, 0), 0.0)
    behind = [later + inside[1] + inside[0], later + inside[1]]
    trans = [chunk_start[slot, seg] for seg in range(2)]

    piece = 32
    order = [c // 2 + (c % 2) * (count // piece // 2) for c in range(count // piece)]
    for c in order:
        seg = 2 * c * piece // count
        field = jnp.dot(left_in[slot, c * piece : (c + 1) * piece, :], right, preferred_element_type=F32)
        alpha = jnp.exp2(field[:, 0:256])
        ratio = alpha / (1.0 - alpha)
        parts = []
        for k in range(piece // SUB):
            span = slice(k * SUB, (k + 1) * SUB)
            weight = trans[seg] * alpha[span]
            trans[seg] = trans[seg] - weight
            shown = weight * field[span, 256:512]
            behind[seg] = behind[seg] - shown
            parts.append((shown - ratio[span] * behind[seg], weight))
        at = slice(c * piece, (c + 1) * piece)
        value = jnp.concatenate([p[0] for p in parts], axis=0)
        one = value.astype(BF16)
        halves[slot, at, 0:256] = one
        halves[slot, at, 256:512] = (value - one.astype(F32)).astype(BF16)
        halves[slot, at, 512:768] = jnp.concatenate([p[1] for p in parts], axis=0).astype(BF16)

    base = stack_rows(basis_rows(256), 16)
    colours = stack_rows([None] * 6 + list(ones) + list(twos), 16)
    kernel = jnp.concatenate([base, base, colours], axis=1).astype(BF16)
    found = lax.dot_general(kernel, halves[slot], NT, preferred_element_type=F32)
    low = found[8:16, :]
    at16 = iota(low.shape, 0)
    top = found[0:8, :] + jnp.where(at16 >= 6, pltpu.roll(low, 5, 0), 0.0)
    grads[tile, 0:8, :] = top
    grads[tile, 8:9, :] = low[0:1, :] + low[3:4, :]


def backward_kernel(lists, left_in, grad, chunk_rend, chunk_start, out, cots, halves, grads, slots):
    step = pl.program_id(0)
    steps = pl.num_programs(0)

    @pl.when(step == 0)
    def _():
        for ch in range(3):
            for g in range(cots.shape[0] // SUB):
                for h in range(2):
                    span = slice(h * LANE, (h + 1) * LANE)
                    block = block_transpose(grad[ch, h * SUB : (h + 1) * SUB, g * LANE : (g + 1) * LANE])
                    for t in range(SUB):
                        cots[g * SUB + t, ch : ch + 1, span] = block[t : t + 1, :]

    per = left_in.shape[0]
    for slot in range(per):
        shade_tile(slot, step * per + slot, left_in, chunk_rend, chunk_start, cots, halves, grads)

    @pl.when(step == steps - 1)
    def _():
        slots[...] = jnp.zeros_like(slots)
        blocks = slots.shape[0] // (SUB + 1)
        group = 2

        def chunk(c, carry):
            each = [c * group + k for k in range(group)]
            idx = jnp.concatenate([jnp.maximum(lists[t], 0) for t in each], axis=1)
            eight = jnp.concatenate([grads[t, 0:8, :] for t in each], axis=1)
            ninth = jnp.concatenate([grads[t, 8:9, :] for t in each], axis=1)
            slots[...] = slots[...] + scatter_block(eight, ninth, idx, blocks)
            return carry

        lax.fori_loop(0, cots.shape[0] // group, chunk, 0)
        left = iota((SUB, LANE), 1) < 64
        row = iota((SUB, LANE), 0)
        for h in range(blocks):
            for half in range(2):
                span = slice(half * LANE, (half + 1) * LANE)
                acc = slots[h * SUB : (h + 1) * SUB, span]
                extra = jnp.broadcast_to(slots[blocks * SUB + h : blocks * SUB + h + 1, span], (SUB, LANE))
                owner = 4 * h + 2 * half
                out[owner], out[owner + 1] = pack_pair(acc, extra, left, row)


def home_kernel(back, send, centres, conic, rho, opacity, out, total, rows):
    lane = iota((SUB, LANE), 1)
    left = lane < 64
    row = iota((SUB, LANE), 0)
    pairs = back.shape[0] // 2
    per = 8
    blocks = centres.shape[1] // 256
    total[...] = jnp.zeros_like(total)

    def chunk(c, carry):
        eight, ninth = [], []
        for k in range(per):
            i = c * per + k
            values, last = unpack_pair(back[2 * i], back[2 * i + 1], left, row)
            eight.append(values)
            ninth.append(last)
        start = pl.multiple_of(c * per * LANE, per * LANE)
        idx = send[0:1, pl.ds(start, per * LANE)]
        total[...] = total[...] + scatter_block(
            jnp.concatenate(eight, axis=1), jnp.concatenate(ninth, axis=1), idx, blocks
        )
        return carry

    lax.fori_loop(0, pairs // per, chunk, 0)
    for h in range(blocks):
        span = slice(h * 256, (h + 1) * 256)
        rows[0:8, span] = total[h * SUB : (h + 1) * SUB, :]
        rows[8:9, span] = total[blocks * SUB + h : blocks * SUB + h + 1, :]
    m_uu, m_uv, m_vv, m_u, m_v, m_1 = (rows[p : p + 1, :] for p in range(6))
    cx, cy = centres[0:1, :], centres[1:2, :]
    a, c = conic[0:1, :], conic[1:2, :]
    r = rho[...]
    root = jnp.sqrt(a * c)
    b = r * root
    x1, y1 = m_u - cx * m_1, m_v - cy * m_1
    xx = m_uu - cx * (m_u + x1)
    yy = m_vv - cy * (m_v + y1)
    xy = m_uv - cx * m_v - cy * x1
    out[0:1, :] = a * x1 + b * y1
    out[1:2, :] = c * y1 + b * x1
    out[2:3, :] = -0.5 * xx - xy * (0.5 * r * (root / a))
    out[3:4, :] = -0.5 * yy - xy * (0.5 * r * (root / c))
    out[4:5, :] = -xy * root
    out[5:6, :] = m_1 / opacity[...]
    out[6:9, :] = rows[6:9, :]


def struct(*shape, dtype=F32):
    return jax.ShapeDtypeStruct(shape, dtype)


def shards(tile_lists, send_rows, centres, conic, rho, opacity, colors, target):
    devices = lax.axis_size("dev")
    owned = centres.shape[1]
    tiles, count = tile_lists.shape
    height, width = target.shape[1], target.shape[2]
    pixels = height * height
    params = lambda mib: pltpu.CompilerParams(vmem_limit_bytes=mib << 20)
    sources = (send_rows, centres, conic, rho, opacity, colors)
    outgoing = pl.pallas_call(
        owner_kernel,
        in_specs=[pl.BlockSpec(memory_space=pltpu.HBM)] * 6,
        out_shape=struct(devices, SUB, LANE),
        scratch_shapes=[pltpu.VMEM((SUB, owned), F32), pltpu.VMEM((owned // LANE, LANE), F32)]
        + [pltpu.VMEM(v.shape, v.dtype) for v in sources]
        + [pltpu.SemaphoreType.DMA((6,))],
        compiler_params=params(8),
        name="owner_gather",
    )(*sources)

    lists = tile_lists.reshape(tiles, SUB, count // SUB).transpose(0, 2, 1).reshape(tiles, 1, count)
    incoming, t_before, t_centre, t_after = exchange(outgoing, 0, target)
    whole = lambda *shape: pl.BlockSpec(shape, lambda t: (0,) * len(shape))
    per = 2
    per_tile = lambda *shape: pl.BlockSpec((per,) + shape, lambda t: (t,) + (0,) * len(shape))
    hi_blocks = devices * 64 // 256
    image, image_too, chunk_rend, chunk_start, left = pl.pallas_call(
        forward_kernel,
        grid=(tiles // per,),
        in_specs=[per_tile(1, count), whole(devices, SUB, LANE)],
        out_specs=[
            whole(3, height, width), whole(3, height, width),
            per_tile(3, 2, SUB, pixels), per_tile(2, SUB, pixels), per_tile(count, 32),
        ],
        out_shape=[
            struct(3, height, width),
            struct(3, height, width),
            struct(tiles, 3, 2, SUB, pixels),
            struct(tiles, 2, SUB, pixels),
            struct(tiles, count, 32, dtype=BF16),
        ],
        scratch_shapes=[
            pltpu.VMEM((hi_blocks * SUB, 256), F32),
            pltpu.VMEM((hi_blocks, 256), F32),
            pltpu.VMEM((hi_blocks * (SUB + 1), 3 * 256), BF16),
            pltpu.VMEM((per, count, LANE), F32),
            pltpu.VMEM((per, count, pixels), F32),
            pltpu.VMEM((3, tiles, pixels), F32),
        ],
        compiler_params=params(16),
        name="tile_forward",
    )(lists, incoming)

    before, after = halo_strips(image_too, 1)
    pixel_grad = pl.pallas_call(
        loss_kernel,
        out_shape=struct(3, height, width),
        scratch_shapes=[pltpu.VMEM((5, 3 * height, width), F32), pltpu.VMEM((3, 2 * height, width), F32)],
        compiler_params=params(8),
        name="loss_gradient",
    )(before, image_too, after, t_before, t_centre, t_after)

    slot_grads = pl.pallas_call(
        backward_kernel,
        grid=(tiles // per,),
        in_specs=[
            whole(tiles, 1, count), per_tile(count, 32), whole(3, height, width),
            per_tile(3, 2, SUB, pixels), per_tile(2, SUB, pixels),
        ],
        out_specs=whole(devices, SUB, LANE),
        out_shape=struct(devices, SUB, LANE),
        scratch_shapes=[
            pltpu.VMEM((tiles, 3, pixels), F32),
            pltpu.VMEM((per, count, 3 * pixels), BF16),
            pltpu.VMEM((tiles, 16, count), F32),
            pltpu.VMEM((hi_blocks * (SUB + 1), 256), F32),
        ],
        compiler_params=params(20),
        name="tile_backward",
    )(lists, left, pixel_grad, chunk_rend, chunk_start)
    returned = exchange(slot_grads, 2)
    grads = pl.pallas_call(
        home_kernel,
        out_shape=struct(9, owned),
        scratch_shapes=[
            pltpu.VMEM((owned // 256 * (SUB + 1), 256), F32),
            pltpu.VMEM((16, owned), F32),
        ],
        compiler_params=params(16),
        name="owner_scatter",
    )(returned, send_rows, centres, conic, rho, opacity)
    return image, grads


def solution(mesh):
    return jax.shard_map(
        shards,
        mesh=mesh,
        in_specs=(
            P("dev", None),
            P("dev", None),
            P(None, "dev"),
            P(None, "dev"),
            P(None, "dev"),
            P(None, "dev"),
            P(None, "dev"),
            P(None, "dev", None),
        ),
        out_specs=(P(None, "dev", None), P(None, "dev")),
        check_vma=False,
    )
```

```python
import functools
import math

import jax
import jax.numpy as jnp
import numpy as np
from jax import lax
from jax.experimental import pallas as pl
from jax.experimental.pallas import tpu as pltpu
from jax.sharding import PartitionSpec as P

F32 = jnp.float32
BF16 = jnp.bfloat16
LOG2E = math.log2(math.e)
SUB, LANE = 8, 128
DEAD = -10000.0


def lane_pick(table, lanes):
    return jnp.take_along_axis(table, lanes, axis=1, mode="promise_in_bounds")


def iota(shape, dim):
    return lax.broadcasted_iota(jnp.int32, shape, dim)


def sub_sum(x):
    for d in (4, 2, 1):
        x = x + pltpu.roll(x, d, 0)
    return x


def split2(x):
    one = x.astype(BF16).astype(F32)
    return one, x - one


def coefficient_rows(cx, cy, a, c, rho, op):
    b = rho * jnp.sqrt(a * c)
    bx, by = a * cx + b * cy, c * cy + b * cx
    one = jnp.log(op) - 0.5 * (cx * bx + cy * by)
    return [LOG2E * k for k in (-0.5 * a, -b, -0.5 * c, bx, by, one)]


def pick_tree(parts, bits):
    if len(parts) == 1:
        return parts[0]()
    half = len(parts) // 2
    return jnp.where(bits[half], pick_tree(parts[half:], bits), pick_tree(parts[:half], bits))


def pick_nine(table, ninth, idx, row, blocks):
    hi, lo = lax.shift_right_logical(idx, 7), lax.bitwise_and(idx, 127)
    bits = {1 << k: lax.bitwise_and(hi, 1 << k) != 0 for k in range(blocks.bit_length() - 1)}
    eight = pick_tree([lambda h=h: lane_pick(table(h), lo) for h in range(blocks)], bits)
    coarse = {k // SUB: v for k, v in bits.items() if k >= SUB}
    last = pick_tree(
        [lambda v=v: lane_pick(ninth[v * SUB : (v + 1) * SUB, :], lo) for v in range(blocks // SUB)], coarse
    )
    return eight, sub_sum(jnp.where(lax.bitwise_and(hi, 7) == row, last, 0.0))


def owner_kernel(*refs):
    sources, (out, table, ninth), places, sems = refs[:6], refs[6:9], refs[9:15], refs[15]
    copies = [pltpu.make_async_copy(a, b, sems.at[k]) for k, (a, b) in enumerate(zip(sources, places))]
    for copy in copies:
        copy.start()
    for copy in copies:
        copy.wait()
    send, centres, conic, rho, opacity, colors = places
    rows = coefficient_rows(
        centres[0:1, :], centres[1:2, :], conic[0:1, :], conic[1:2, :], rho[...], opacity[...]
    )
    for p, row in enumerate(rows + [colors[0:1, :], colors[1:2, :]]):
        table[p : p + 1, :] = row
    blocks = table.shape[1] // LANE
    for h in range(blocks):
        ninth[h : h + 1, :] = colors[2:3, h * LANE : (h + 1) * LANE]
    left = iota((SUB, LANE), 1) < 64
    row = iota((SUB, LANE), 0)
    step = 4

    def pairs(ii, carry):
        for k in range(step):
            i = ii * step + k
            start = pl.multiple_of(i * LANE, LANE)
            idx = jnp.broadcast_to(jnp.maximum(send[0:1, pl.ds(start, LANE)], 0), (SUB, LANE))
            eight, last = pick_nine(lambda h: table[:, h * LANE : (h + 1) * LANE], ninth, idx, row, blocks)
            out[2 * i], out[2 * i + 1] = pack_pair(eight, last, left, row)
        return carry

    lax.fori_loop(0, send.shape[1] // LANE // step, pairs, 0)


MESH = pl.DeviceIdType.MESH
USED = 5


def pack_pair(eight, last, left, row):
    low = pltpu.roll(eight, 4, 0)
    even = jnp.where(left, eight, pltpu.roll(low, 64, 1))
    odd = jnp.where(left, pltpu.roll(eight, 64, 1), low)
    return jnp.where(row < 4, even, last), jnp.where(row < 4, odd, pltpu.roll(last, 64, 1))


def unpack_pair(even, odd, left, row):
    high = jnp.where(left, even, pltpu.roll(odd, 64, 1))
    low = jnp.where(left, pltpu.roll(even, 64, 1), odd)
    return jnp.where(row < 4, high, pltpu.roll(low, 4, 0)), high[4:5, :]


def greet_all(n, me):
    barrier = pltpu.get_barrier_semaphore()

    def greet(k, carry):
        pl.semaphore_signal(barrier, inc=1, device_id=(lax.rem(me + k, n),), device_id_type=MESH)
        return carry

    lax.fori_loop(1, n, greet, 0)
    return barrier


def halo_copies(n, me, strip, before, after, send_sem, recv_sem):
    return [
        pltpu.make_async_remote_copy(
            src_ref=strip, dst_ref=to, send_sem=send_sem.at[k], recv_sem=recv_sem.at[k],
            device_id=(lax.rem(me + hop, n),), device_id_type=MESH,
        )
        for k, (hop, to) in enumerate(((1, before), (n - 1, after)))
    ]


def exchange_kernel(halo, *refs):
    if halo:
        x, strip, out, before, centre, after, local_sem, send_sem, recv_sem, halo_send, halo_recv = refs
    else:
        x, out, local_sem, send_sem, recv_sem = refs
    me = lax.axis_index("dev")
    n = lax.axis_size("dev")
    rows = pl.ds(0, USED)
    barrier = greet_all(n, me)
    own = pltpu.make_async_copy(x.at[me, rows], out.at[me, rows], local_sem)
    own.start()
    pl.semaphore_wait(barrier, n - 1)

    def start(k, carry):
        peer = lax.rem(me + k, n)
        pltpu.make_async_remote_copy(
            src_ref=x.at[peer, rows], dst_ref=out.at[me, rows], send_sem=send_sem, recv_sem=recv_sem,
            device_id=(peer,), device_id_type=MESH,
        ).start()
        return carry

    lax.fori_loop(1, n, start, 0)
    copies = []
    if halo:
        copies = halo_copies(n, me, strip, before, after, halo_send, halo_recv)
        copies.append(pltpu.make_async_copy(strip, centre, halo_recv.at[2]))
    for copy in copies:
        copy.start()
    own.wait()
    rest = pl.ds(0, n - 1)
    pltpu.make_async_copy(x.at[rest, rows], x.at[rest, rows], send_sem).wait()
    pltpu.make_async_copy(out.at[rest, rows], out.at[rest, rows], recv_sem).wait()
    for copy in copies:
        copy.wait()


def comm_params(number):
    return pltpu.CompilerParams(collective_id=number, has_side_effects=True, vmem_limit_bytes=4 << 20)


def exchange(x, number, strip=None):
    vmem = pl.BlockSpec(memory_space=pltpu.VMEM)
    halo = strip is not None
    like = lambda v: jax.ShapeDtypeStruct(v.shape, v.dtype)
    return pl.pallas_call(
        functools.partial(exchange_kernel, halo),
        out_shape=[like(x)] + [like(strip)] * 3 if halo else like(x),
        in_specs=[vmem] + [pl.BlockSpec(memory_space=pltpu.HBM)] * halo,
        out_specs=[vmem] * 4 if halo else vmem,
        scratch_shapes=[pltpu.SemaphoreType.DMA] * 3 + [pltpu.SemaphoreType.DMA((3,))] * (2 if halo else 0),
        compiler_params=comm_params(number),
        name="exchange",
    )(*([x, strip] if halo else [x]))


def halo_kernel(strip, before, after, send_sem, recv_sem):
    me = lax.axis_index("dev")
    n = lax.axis_size("dev")
    barrier = pltpu.get_barrier_semaphore()
    for hop in (1, n - 1):
        pl.semaphore_signal(barrier, inc=1, device_id=(lax.rem(me + hop, n),), device_id_type=MESH)
    pl.semaphore_wait(barrier, 2)
    copies = halo_copies(n, me, strip, before, after, send_sem, recv_sem)
    for copy in copies:
        copy.start()
    for copy in copies:
        copy.wait()


def halo_strips(strip, number):
    vmem = pl.BlockSpec(memory_space=pltpu.VMEM)
    return pl.pallas_call(
        halo_kernel,
        out_shape=[jax.ShapeDtypeStruct(strip.shape, strip.dtype)] * 2,
        in_specs=[vmem],
        out_specs=[vmem] * 2,
        scratch_shapes=[pltpu.SemaphoreType.DMA((2,))] * 2,
        compiler_params=comm_params(number),
        name="halo",
    )(strip)


def block_transpose(x):
    row = iota(x.shape, 0)
    block = lax.shift_right_logical(iota(x.shape, 1), 4)
    for d in (1, 2, 4):
        low_row = lax.bitwise_and(row, d) == 0
        low_block = lax.bitwise_and(block, d) == 0
        down = pltpu.roll(pltpu.roll(x, SUB - d, 0), 16 * d, 1)
        back = pltpu.roll(pltpu.roll(x, d, 0), LANE - 16 * d, 1)
        x = jnp.where(low_row == low_block, x, jnp.where(low_row, down, back))
    return x


def basis_rows(lanes):
    pixel = iota((1, lanes), 1)
    v = lax.shift_right_logical(pixel, 4).astype(F32) - 7.5
    u = lax.bitwise_and(pixel, 15).astype(F32) - 7.5
    return [u * u, u * v, v * v, u, v, jnp.ones_like(u)]


def stack_rows(rows, count):
    shape = (count, next(r for r in rows if r is not None).shape[1])
    at = iota(shape, 0)
    result = jnp.zeros(shape, F32)
    for p, row in enumerate(rows):
        if row is not None:
            result = jnp.where(at == p, jnp.broadcast_to(row, shape), result)
    return result


def scan_sub(x):
    at = iota(x.shape, 0)
    x = jnp.where(at == 0, 1.0, pltpu.roll(x, 1, 0))
    for d in (1, 2, 4):
        x = x * jnp.where(at >= d, pltpu.roll(x, d, 0), 1.0)
    return x


def take_turns(order, **workers):
    for name in order:
        next(workers[name], None)
    for worker in workers.values():
        for _ in worker:
            pass


def segments(count):
    groups = count // SUB // 2
    return [(seg, j, (seg * groups + j) * SUB) for j in range(groups) for seg in range(2)]


def split3(x):
    one, rest = split2(x)
    two, three = split2(rest)
    return one, two, three


def gather_columns(raw, flat, cols, slot):
    count = raw.shape[1]
    blocks = flat.shape[0] // (SUB + 1)
    row = iota((SUB, LANE), 0)
    wide = 2 * LANE
    founds = []
    for n in range(count // wide):
        idx = jnp.maximum(raw[:, n * wide : (n + 1) * wide], 0)
        hi, lo = lax.shift_right_logical(idx, 8), lax.bitwise_and(idx, 255)
        hot = onehot(lo, 256)
        found = jnp.dot(flat[...], jnp.concatenate([hot] * 2, axis=0), preferred_element_type=F32)
        founds.append((hi, found))
        yield
    for q in range(count // LANE):
        hi, found = founds[q // 2]
        span = slice((q % 2) * LANE, (q % 2 + 1) * LANE)
        out = slice(q * LANE, (q + 1) * LANE)
        hq = jnp.broadcast_to(hi[:, span], (SUB, LANE))
        bits = {1 << k: lax.bitwise_and(hq, 1 << k) != 0 for k in range(blocks.bit_length() - 1)}
        acc = pick_tree([lambda h=h: found[h * SUB : (h + 1) * SUB, span] for h in range(blocks)], bits)
        coarse = {k // SUB: v for k, v in bits.items() if k >= SUB}
        base = blocks * SUB
        last = pick_tree(
            [lambda v=v: found[base + v * SUB : base + (v + 1) * SUB, span] for v in range(blocks // SUB)], coarse
        )
        last = sub_sum(jnp.where(lax.bitwise_and(hq, 7) == row, last, 0.0))
        yield
        acc = jnp.where((row == 5) & (jnp.broadcast_to(raw[:, out], (SUB, LANE)) < 0), DEAD, acc)
        one, two, three = split3(acc)
        b_one, b_two = split2(last)
        more = jnp.where(row == 1, b_two, jnp.where(row == 7, last, b_one))
        more = jnp.where((row == 3) | (row == 4), pltpu.roll(one, 5, 0), more)
        more = jnp.where((row == 5) | (row == 6), pltpu.roll(acc, 7, 0), more)
        stack = jnp.concatenate([one, two, three, more], axis=0)
        cols[slot, out, :] = jnp.concatenate([stack, jnp.zeros((LANE - 32, LANE), F32)], axis=0).T
        yield


TURNS = "d" * 8 + "g" + "d" * 6 + "g" + "d" * 2 + "gg" + "d" * 2 + "gg" + "d" * 2 + "gg" + "d" * 4 + "gg"


def draw_tile(slot, tile, basis, chunk_rend, chunk_start, left_out, cols, alphas, rends):
    count = cols.shape[1]
    ones = jnp.ones((SUB, 256), F32)
    product = [ones, ones]
    piece = 64
    for c in range(count // piece):
        span = slice(c * piece, (c + 1) * piece)
        left = cols[slot, span, 0:32].astype(BF16)
        left_out[slot, span, :] = left
        alpha = jnp.exp2(jnp.dot(left, basis, preferred_element_type=F32))
        alphas[slot, span, :] = alpha
        rest = 1.0 - alpha
        parts = [rest[k * SUB : (k + 1) * SUB, :] for k in range(piece // SUB)]
        while len(parts) > 1:
            parts = [parts[k] * parts[k + 1] for k in range(0, len(parts), 2)]
        seg = 2 * c * piece // count
        product[seg] = product[seg] * parts[0]
        yield

    begin = scan_sub(product[0] * product[1])
    trans = [begin, begin * product[0]]
    zero = jnp.zeros((SUB, 256), F32)
    sums = [[zero] * 3, [zero] * 3]
    for seg in range(2):
        chunk_start[slot, seg] = trans[seg]
    for seg, j, at in segments(count):
        weight = trans[seg] * alphas[slot, at : at + SUB, :]
        trans[seg] = trans[seg] - weight
        color = cols[slot, at : at + SUB, :]
        sums[seg] = [t + weight * color[:, 29 + ch : 30 + ch] for ch, t in enumerate(sums[seg])]
        if seg == 1 and j % 2 == 1:
            yield
    for ch in range(3):
        for seg in range(2):
            chunk_rend[slot, ch, seg] = sums[seg][ch]
        rends[ch, pl.ds(tile, 1), :] = sub_sum(sums[0][ch] + sums[1][ch])[0:1, :]


def forward_kernel(
    lists, recv, image, image_too, chunk_rend, chunk_start, left_out, pieces, ninth, flat, cols, alphas, rends
):
    step = pl.program_id(0)
    row = iota((SUB, LANE), 0)

    @pl.when(step == 0)
    def _():
        blocks = pieces.shape[0] // SUB
        left = iota((SUB, LANE), 1) < 64

        def block(h, carry):
            lasts = []
            for half in range(2):
                owner = 4 * h + 2 * half
                eight, last = unpack_pair(recv[owner], recv[owner + 1], left, row)
                pieces[pl.ds(pl.multiple_of(h * SUB, SUB), SUB), half * LANE : (half + 1) * LANE] = eight
                lasts.append(last)
            ninth[pl.ds(h, 1), :] = jnp.concatenate(lasts, axis=1)
            return carry

        lax.fori_loop(0, blocks, block, 0)
        for rows, source in ((slice(0, blocks * SUB), pieces), (slice(blocks * SUB, None), ninth)):
            for k, part in enumerate(split2(source[...])):
                flat[rows, k * 256 : (k + 1) * 256] = part.astype(BF16)
        for _ in gather_columns(lists[0], flat, cols, 0):
            pass

    basis = stack_rows((basis_rows(256) + [None, None]) * 3, 32).astype(BF16)
    for slot in range(2):
        tile = 2 * step + slot
        later = jnp.minimum(tile + 1, lists.shape[0] - 1)
        take_turns(
            TURNS,
            g=gather_columns(lists[later], flat, cols, 1 - slot),
            d=draw_tile(slot, tile, basis, chunk_rend, chunk_start, left_out, cols, alphas, rends),
        )

    @pl.when(step == pl.num_programs(0) - 1)
    def _():
        for ch in range(3):
            for g in range(rends.shape[1] // SUB):
                for h in range(2):
                    block = block_transpose(rends[ch, g * SUB : (g + 1) * SUB, h * LANE : (h + 1) * LANE])
                    for to in (image, image_too):
                        to[ch, h * SUB : (h + 1) * SUB, g * LANE : (g + 1) * LANE] = block


def taps_of():
    offsets = np.arange(11, dtype=np.float32) - np.float32(5)
    taps = np.exp(-offsets * offsets / np.float32(4.5)).astype(np.float32)
    return [float(t) for t in taps / taps.sum(dtype=np.float32)]


TAPS = taps_of()


def blur_rows(read, start, count):
    total = TAPS[5] * read(start, count)
    for m in range(1, 6):
        total = total + TAPS[5 + m] * (read(start - m, count) + read(start + m, count))
    return total


def blur_lanes(x):
    rows, width = x.shape
    pad = jnp.zeros((rows, LANE), F32)
    wide = jnp.concatenate([x, pad], axis=1)
    total = TAPS[5] * x
    for m in range(1, 6):
        both = pltpu.roll(wide, m, 1) + pltpu.roll(wide, width + LANE - m, 1)
        total = total + TAPS[5 + m] * both[:, :width]
    return total


def loss_kernel(before, centre, after, t_before, t_centre, t_after, grad, pads, maps):
    height = centre.shape[1]
    mine = lax.axis_index("dev")
    total_rows = lax.axis_size("dev") * height
    width = centre.shape[2]
    at = iota((2 * height, width), 0) - height // 2 + mine * height
    inside = (at >= 0) & (at < total_rows)
    for ch in range(3):
        for i, (r, t) in enumerate(((before, t_before), (centre, t_centre), (after, t_after))):
            span = slice(i * height, (i + 1) * height)
            rr, tt = r[ch], t[ch]
            if i != 1:
                keep = mine > 0 if i == 0 else mine < total_rows // height - 1
                rr, tt = jnp.where(keep, rr, 0.0), jnp.where(keep, tt, 0.0)
            pads[0, span, :] = rr
            pads[1, span, :] = tt
            pads[2, span, :] = rr * rr
            pads[3, span, :] = tt * tt
            pads[4, span, :] = rr * tt

        def wide_blur(k):
            vertical = blur_rows(lambda s, n: pads[k, s : s + n, :], height // 2, 2 * height)
            return blur_lanes(vertical)

        mr, mt, rr, tt, rt = (wide_blur(k) for k in range(5))
        cv = rt - mr * mt
        top1 = 2.0 * mr * mt + 0.0001
        top2 = 2.0 * cv + 0.0009
        low1 = mr * mr + mt * mt + 0.0001
        low2 = (rr - mr * mr) + (tt - mt * mt) + 0.0009
        inv1, inv2 = 1.0 / low1, 1.0 / low2
        both = inv1 * inv2
        ssim = top1 * top2 * both
        d_rr = -ssim * inv2
        d_rt = 2.0 * top1 * both
        d_mr = 2.0 * (mt * (top2 - top1) * both + mr * ssim * (inv2 - inv1))
        for k, value in enumerate((d_mr, d_rr, d_rt)):
            maps[k] = jnp.where(inside, value, 0.0)

        def back_blur(k):
            vertical = blur_rows(lambda s, n: maps[k, s : s + n, :], height // 2, height)
            return blur_lanes(vertical)

        g_mr, g_rr, g_rt = (back_blur(k) for k in range(3))
        r, t = centre[ch], t_centre[ch]
        grad[ch] = 1.6 * (r - t) - 0.2 * (g_mr + 2.0 * r * g_rr + t * g_rt)


NT = (((1,), (1,)), ((), ()))


def onehot(lo, rows):
    return jnp.where(iota((rows, lo.shape[1]), 0) == lo, 1.0, 0.0).astype(BF16)


def spread(values, hi, blocks):
    masked = [jnp.where(hi == h, values, 0.0) for h in range(blocks)]
    return jnp.concatenate(masked, axis=0)


def scatter_block(eight, ninth, idx, blocks):
    span = idx.shape[1]
    hi, lo = lax.shift_right_arithmetic(idx, 8), lax.bitwise_and(idx, 255)
    hot = onehot(lo, 256)
    hi8 = jnp.broadcast_to(hi, (SUB, span))
    own = iota((blocks, span), 0) == hi
    left = []
    for values, extra in zip(split2(eight), split2(ninth)):
        left.append(spread(values, hi8, blocks))
        left.append(jnp.where(own, jnp.broadcast_to(extra, own.shape), 0.0))
    left = jnp.concatenate(left, axis=0).astype(BF16)
    both = lax.dot_general(left, hot, NT, preferred_element_type=F32)
    return both[: blocks * (SUB + 1), :] + both[blocks * (SUB + 1) :, :]


def shade_tile(slot, tile, left_in, chunk_rend, chunk_start, cots, halves):
    count = left_in.shape[1]
    rows = [cots[tile, ch : ch + 1, :] for ch in range(3)]
    ones, twos = zip(*(split2(r) for r in rows))
    basis = stack_rows((basis_rows(256) + [None, None]) * 3, 32)
    back = stack_rows(
        [None] * 6 + [ones[0], ones[1]] + [None] * 6 + [ones[0], ones[1]] + [None] * 6
        + [ones[0], ones[1], ones[2], ones[2], twos[2], twos[0], twos[1]], 32
    )
    right = jnp.concatenate([basis, back], axis=1).astype(BF16)

    inside = [sum(chunk_rend[slot, ch, seg] * rows[ch] for ch in range(3)) for seg in range(2)]
    at8 = iota((SUB, 256), 0)
    later = inside[0] + inside[1]
    later = jnp.where(at8 == SUB - 1, 0.0, pltpu.roll(later, SUB - 1, 0))
    for d in (1, 2, 4):
        later = later + jnp.where(at8 < SUB - d, pltpu.roll(later, SUB - d, 0), 0.0)
    behind = [later + inside[1] + inside[0], later + inside[1]]
    trans = [chunk_start[slot, seg] for seg in range(2)]

    piece = 64
    order = [c // 2 + (c % 2) * (count // piece // 2) for c in range(count // piece)]

    def field_of(c):
        return jnp.dot(left_in[slot, c * piece : (c + 1) * piece, :], right, preferred_element_type=F32)

    ahead = 1
    fields = [field_of(c) for c in order[:ahead]]
    for n, c in enumerate(order):
        if n + ahead < len(order):
            fields.append(field_of(order[n + ahead]))
        seg = 2 * c * piece // count
        field = fields[n]
        alpha = jnp.exp2(field[:, 0:256])
        ratio = alpha / (1.0 - alpha)
        parts = []
        for k in range(piece // SUB):
            span = slice(k * SUB, (k + 1) * SUB)
            weight = trans[seg] * alpha[span]
            trans[seg] = trans[seg] - weight
            shown = weight * field[span, 256:512]
            behind[seg] = behind[seg] - shown
            parts.append((shown - ratio[span] * behind[seg], weight))
        at = slice(c * piece, (c + 1) * piece)
        value = jnp.concatenate([p[0] for p in parts], axis=0)
        one = value.astype(BF16)
        halves[slot, at, 0:256] = one
        halves[slot, at, 256:512] = (value - one.astype(F32)).astype(BF16)
        halves[slot, at, 512:768] = jnp.concatenate([p[1] for p in parts], axis=0).astype(BF16)
        yield


BACK_TURNS = "fss" * 4


def find_moments(slot, tile, cots, halves, grads):
    rows = [cots[tile, ch : ch + 1, :] for ch in range(3)]
    ones, twos = zip(*(split2(r) for r in rows))
    base = stack_rows(basis_rows(256), 16)
    colours = stack_rows([None] * 6 + list(ones) + list(twos), 16)
    kernel = jnp.concatenate([base, base, colours], axis=1).astype(BF16)
    wide = 128
    for n in range(halves.shape[1] // wide):
        at = slice(n * wide, (n + 1) * wide)
        found = lax.dot_general(kernel, halves[slot, at, :], NT, preferred_element_type=F32)
        low = found[8:16, :]
        at16 = iota(low.shape, 0)
        top = found[0:8, :] + jnp.where(at16 >= 6, pltpu.roll(low, 5, 0), 0.0)
        grads[tile, 0:8, at] = top
        grads[tile, 8:9, at] = low[0:1, :] + low[3:4, :]
        yield


def backward_kernel(lists, left_in, grad, chunk_rend, chunk_start, out, cots, halves, grads, slots):
    step = pl.program_id(0)
    steps = pl.num_programs(0)

    @pl.when(step == 0)
    def _():
        for ch in range(3):
            for g in range(cots.shape[0] // SUB):
                for h in range(2):
                    span = slice(h * LANE, (h + 1) * LANE)
                    block = block_transpose(grad[ch, h * SUB : (h + 1) * SUB, g * LANE : (g + 1) * LANE])
                    for t in range(SUB):
                        cots[g * SUB + t, ch : ch + 1, span] = block[t : t + 1, :]

    for slot in range(2):
        tile = 2 * step + slot
        past = jnp.maximum(tile - 1, 0)
        take_turns(
            BACK_TURNS,
            f=find_moments(1 - slot, past, cots, halves, grads),
            s=shade_tile(slot, tile, left_in, chunk_rend, chunk_start, cots, halves),
        )

    @pl.when(step == steps - 1)
    def _():
        for _ in find_moments(1, 2 * step + 1, cots, halves, grads):
            pass
        slots[...] = jnp.zeros_like(slots)
        blocks = slots.shape[0] // (SUB + 1)
        group = 2

        def chunk(c, carry):
            each = [c * group + k for k in range(group)]
            idx = jnp.concatenate([jnp.maximum(lists[t], 0) for t in each], axis=1)
            eight = jnp.concatenate([grads[t, 0:8, :] for t in each], axis=1)
            ninth = jnp.concatenate([grads[t, 8:9, :] for t in each], axis=1)
            slots[...] = slots[...] + scatter_block(eight, ninth, idx, blocks)
            return carry

        lax.fori_loop(0, cots.shape[0] // group, chunk, 0)
        left = iota((SUB, LANE), 1) < 64
        row = iota((SUB, LANE), 0)
        for h in range(blocks):
            for half in range(2):
                span = slice(half * LANE, (half + 1) * LANE)
                acc = slots[h * SUB : (h + 1) * SUB, span]
                extra = jnp.broadcast_to(slots[blocks * SUB + h : blocks * SUB + h + 1, span], (SUB, LANE))
                owner = 4 * h + 2 * half
                out[owner], out[owner + 1] = pack_pair(acc, extra, left, row)


def home_kernel(back, send, centres, conic, rho, opacity, out, total, rows):
    lane = iota((SUB, LANE), 1)
    left = lane < 64
    row = iota((SUB, LANE), 0)
    pairs = back.shape[0] // 2
    per = 8
    blocks = centres.shape[1] // 256
    total[...] = jnp.zeros_like(total)

    def chunk(c, carry):
        eight, ninth = [], []
        for k in range(per):
            i = c * per + k
            values, last = unpack_pair(back[2 * i], back[2 * i + 1], left, row)
            eight.append(values)
            ninth.append(last)
        start = pl.multiple_of(c * per * LANE, per * LANE)
        idx = send[0:1, pl.ds(start, per * LANE)]
        total[...] = total[...] + scatter_block(
            jnp.concatenate(eight, axis=1), jnp.concatenate(ninth, axis=1), idx, blocks
        )
        return carry

    lax.fori_loop(0, pairs // per, chunk, 0)
    for h in range(blocks):
        span = slice(h * 256, (h + 1) * 256)
        rows[0:8, span] = total[h * SUB : (h + 1) * SUB, :]
        rows[8:9, span] = total[blocks * SUB + h : blocks * SUB + h + 1, :]
    m_uu, m_uv, m_vv, m_u, m_v, m_1 = (rows[p : p + 1, :] for p in range(6))
    cx, cy = centres[0:1, :], centres[1:2, :]
    a, c = conic[0:1, :], conic[1:2, :]
    r = rho[...]
    root = jnp.sqrt(a * c)
    b = r * root
    x1, y1 = m_u - cx * m_1, m_v - cy * m_1
    xx = m_uu - cx * (m_u + x1)
    yy = m_vv - cy * (m_v + y1)
    xy = m_uv - cx * m_v - cy * x1
    out[0:1, :] = a * x1 + b * y1
    out[1:2, :] = c * y1 + b * x1
    out[2:3, :] = -0.5 * xx - xy * (0.5 * r * (root / a))
    out[3:4, :] = -0.5 * yy - xy * (0.5 * r * (root / c))
    out[4:5, :] = -xy * root
    out[5:6, :] = m_1 / opacity[...]
    out[6:9, :] = rows[6:9, :]


def struct(*shape, dtype=F32):
    return jax.ShapeDtypeStruct(shape, dtype)


def shards(tile_lists, send_rows, centres, conic, rho, opacity, colors, target):
    devices = lax.axis_size("dev")
    owned = centres.shape[1]
    tiles, count = tile_lists.shape
    height, width = target.shape[1], target.shape[2]
    pixels = height * height
    params = lambda mib: pltpu.CompilerParams(vmem_limit_bytes=mib << 20)
    sources = (send_rows, centres, conic, rho, opacity, colors)
    outgoing = pl.pallas_call(
        owner_kernel,
        in_specs=[pl.BlockSpec(memory_space=pltpu.HBM)] * 6,
        out_shape=struct(devices, SUB, LANE),
        scratch_shapes=[pltpu.VMEM((SUB, owned), F32), pltpu.VMEM((owned // LANE, LANE), F32)]
        + [pltpu.VMEM(v.shape, v.dtype) for v in sources]
        + [pltpu.SemaphoreType.DMA((6,))],
        compiler_params=params(8),
        name="owner_gather",
    )(*sources)

    lists = tile_lists.reshape(tiles, SUB, count // SUB).transpose(0, 2, 1).reshape(tiles, 1, count)
    incoming, t_before, t_centre, t_after = exchange(outgoing, 0, target)
    whole = lambda *shape: pl.BlockSpec(shape, lambda t: (0,) * len(shape))
    per = 2
    per_tile = lambda *shape: pl.BlockSpec((per,) + shape, lambda t: (t,) + (0,) * len(shape))
    hi_blocks = devices * 64 // 256
    image, image_too, chunk_rend, chunk_start, left = pl.pallas_call(
        forward_kernel,
        grid=(tiles // per,),
        in_specs=[whole(tiles, 1, count), whole(devices, SUB, LANE)],
        out_specs=[
            whole(3, height, width), whole(3, height, width),
            per_tile(3, 2, SUB, pixels), per_tile(2, SUB, pixels), per_tile(count, 32),
        ],
        out_shape=[
            struct(3, height, width),
            struct(3, height, width),
            struct(tiles, 3, 2, SUB, pixels),
            struct(tiles, 2, SUB, pixels),
            struct(tiles, count, 32, dtype=BF16),
        ],
        scratch_shapes=[
            pltpu.VMEM((hi_blocks * SUB, 256), F32),
            pltpu.VMEM((hi_blocks, 256), F32),
            pltpu.VMEM((hi_blocks * (SUB + 1), 2 * 256), BF16),
            pltpu.VMEM((per, count, LANE), F32),
            pltpu.VMEM((per, count, pixels), F32),
            pltpu.VMEM((3, tiles, pixels), F32),
        ],
        compiler_params=params(16),
        name="tile_forward",
    )(lists, incoming)

    before, after = halo_strips(image_too, 1)
    pixel_grad = pl.pallas_call(
        loss_kernel,
        out_shape=struct(3, height, width),
        scratch_shapes=[pltpu.VMEM((5, 3 * height, width), F32), pltpu.VMEM((3, 2 * height, width), F32)],
        compiler_params=params(8),
        name="loss_gradient",
    )(before, image_too, after, t_before, t_centre, t_after)

    slot_grads = pl.pallas_call(
        backward_kernel,
        grid=(tiles // per,),
        in_specs=[
            whole(tiles, 1, count), per_tile(count, 32), whole(3, height, width),
            per_tile(3, 2, SUB, pixels), per_tile(2, SUB, pixels),
        ],
        out_specs=whole(devices, SUB, LANE),
        out_shape=struct(devices, SUB, LANE),
        scratch_shapes=[
            pltpu.VMEM((tiles, 3, pixels), F32),
            pltpu.VMEM((per, count, 3 * pixels), BF16),
            pltpu.VMEM((tiles, 16, count), F32),
            pltpu.VMEM((hi_blocks * (SUB + 1), 256), F32),
        ],
        compiler_params=params(20),
        name="tile_backward",
    )(lists, left, pixel_grad, chunk_rend, chunk_start)
    returned = exchange(slot_grads, 2)
    grads = pl.pallas_call(
        home_kernel,
        out_shape=struct(9, owned),
        scratch_shapes=[
            pltpu.VMEM((owned // 256 * (SUB + 1), 256), F32),
            pltpu.VMEM((16, owned), F32),
        ],
        compiler_params=params(16),
        name="owner_scatter",
    )(returned, send_rows, centres, conic, rho, opacity)
    return image, grads


def solution(mesh):
    return jax.shard_map(
        shards,
        mesh=mesh,
        in_specs=(
            P("dev", None),
            P("dev", None),
            P(None, "dev"),
            P(None, "dev"),
            P(None, "dev"),
            P(None, "dev"),
            P(None, "dev"),
            P(None, "dev", None),
        ),
        out_specs=(P(None, "dev", None), P(None, "dev")),
        check_vma=False,
    )
```

```python
import functools
import math

import jax
import jax.numpy as jnp
import numpy as np
from jax import lax
from jax.experimental import pallas as pl
from jax.experimental.pallas import tpu as pltpu
from jax.sharding import PartitionSpec as P

F32 = jnp.float32
BF16 = jnp.bfloat16
LOG2E = math.log2(math.e)
SUB, LANE = 8, 128
DEAD = -10000.0


def lane_pick(table, lanes):
    return jnp.take_along_axis(table, lanes, axis=1, mode="promise_in_bounds")


def iota(shape, dim):
    return lax.broadcasted_iota(jnp.int32, shape, dim)


def sub_sum(x):
    for d in (4, 2, 1):
        x = x + pltpu.roll(x, d, 0)
    return x


def split2(x):
    one = x.astype(BF16).astype(F32)
    return one, x - one


def coefficient_rows(cx, cy, a, c, rho, op):
    b = rho * jnp.sqrt(a * c)
    bx, by = a * cx + b * cy, c * cy + b * cx
    one = jnp.log(op) - 0.5 * (cx * bx + cy * by)
    return [LOG2E * k for k in (-0.5 * a, -b, -0.5 * c, bx, by, one)]


def pick_tree(parts, bits):
    if len(parts) == 1:
        return parts[0]()
    half = len(parts) // 2
    return jnp.where(bits[half], pick_tree(parts[half:], bits), pick_tree(parts[:half], bits))


def pick_nine(table, ninth, idx, row, blocks):
    hi, lo = lax.shift_right_logical(idx, 7), lax.bitwise_and(idx, 127)
    bits = {1 << k: lax.bitwise_and(hi, 1 << k) != 0 for k in range(blocks.bit_length() - 1)}
    eight = pick_tree([lambda h=h: lane_pick(table(h), lo) for h in range(blocks)], bits)
    coarse = {k // SUB: v for k, v in bits.items() if k >= SUB}
    last = pick_tree(
        [lambda v=v: lane_pick(ninth[v * SUB : (v + 1) * SUB, :], lo) for v in range(blocks // SUB)], coarse
    )
    return eight, sub_sum(jnp.where(lax.bitwise_and(hi, 7) == row, last, 0.0))


MESH = pl.DeviceIdType.MESH
USED = 5


def pack_pair(eight, last, left, row):
    low = pltpu.roll(eight, 4, 0)
    even = jnp.where(left, eight, pltpu.roll(low, 64, 1))
    odd = jnp.where(left, pltpu.roll(eight, 64, 1), low)
    return jnp.where(row < 4, even, last), jnp.where(row < 4, odd, pltpu.roll(last, 64, 1))


def unpack_pair(even, odd, left, row):
    high = jnp.where(left, even, pltpu.roll(odd, 64, 1))
    low = jnp.where(left, pltpu.roll(even, 64, 1), odd)
    return jnp.where(row < 4, high, pltpu.roll(low, 4, 0)), high[4:5, :]


def greet_all(n, me):
    barrier = pltpu.get_barrier_semaphore()

    def greet(k, carry):
        pl.semaphore_signal(barrier, inc=1, device_id=(lax.rem(me + k, n),), device_id_type=MESH)
        return carry

    lax.fori_loop(1, n, greet, 0)
    return barrier


def halo_copies(n, me, strip, before, after, send_sem, recv_sem):
    return [
        pltpu.make_async_remote_copy(
            src_ref=strip, dst_ref=to, send_sem=send_sem.at[k], recv_sem=recv_sem.at[k],
            device_id=(lax.rem(me + hop, n),), device_id_type=MESH,
        )
        for k, (hop, to) in enumerate(((1, before), (n - 1, after)))
    ]


def send_owned_kernel(*refs):
    sources, strip, (out, before, centre, after), x, table, ninth = refs[:6], refs[6], refs[7:11], *refs[11:14]
    places, (local_sem, send_sem, recv_sem, halo_send, halo_recv) = refs[14:20], refs[20:25]
    me = lax.axis_index("dev")
    n = lax.axis_size("dev")
    fetched = [pltpu.make_async_copy(a, b, local_sem.at[k]) for k, (a, b) in enumerate(zip(sources, places))]
    for copy in fetched:
        copy.start()
    barrier = greet_all(n, me)
    for copy in fetched:
        copy.wait()
    send, centres, conic, rho, opacity, colors = places
    rows = coefficient_rows(
        centres[0:1, :], centres[1:2, :], conic[0:1, :], conic[1:2, :], rho[...], opacity[...]
    )
    for p, value in enumerate(rows + [colors[0:1, :], colors[1:2, :]]):
        table[p : p + 1, :] = value
    blocks = table.shape[1] // LANE
    for h in range(blocks):
        ninth[h : h + 1, :] = colors[2:3, h * LANE : (h + 1) * LANE]
    left = iota((SUB, LANE), 1) < 64
    row = iota((SUB, LANE), 0)
    pairs = n // 2
    mine = me // 2
    used = pl.ds(0, USED)
    step = 4

    def fill(group):
        for k in range(step):
            i = lax.rem(mine + group * step + k, pairs)
            start = pl.multiple_of(i * LANE, LANE)
            idx = jnp.broadcast_to(jnp.maximum(send[0:1, pl.ds(start, LANE)], 0), (SUB, LANE))
            eight, last = pick_nine(lambda h: table[:, h * LANE : (h + 1) * LANE], ninth, idx, row, blocks)
            x[2 * i], x[2 * i + 1] = pack_pair(eight, last, left, row)

    def ship(k):
        for core in range(2):
            peer = 2 * lax.rem(mine + k, pairs) + core
            pltpu.make_async_remote_copy(
                src_ref=x.at[peer, used], dst_ref=out.at[me, used], send_sem=send_sem, recv_sem=recv_sem,
                device_id=(peer,), device_id_type=MESH,
            ).start()

    copies = halo_copies(n, me, strip, before, after, halo_send, halo_recv)
    copies.append(pltpu.make_async_copy(strip, centre, halo_recv.at[2]))
    early = 5

    def first(group, carry):
        fill(group)
        return carry

    lax.fori_loop(0, early, first, 0)
    pl.semaphore_wait(barrier, n - 1)
    for copy in copies:
        copy.start()
    partner = me + 1 - 2 * lax.rem(me, 2)
    own = pltpu.make_async_copy(x.at[me, used], out.at[me, used], local_sem.at[6])
    own.start()
    pltpu.make_async_remote_copy(
        src_ref=x.at[partner, used], dst_ref=out.at[me, used], send_sem=send_sem, recv_sem=recv_sem,
        device_id=(partner,), device_id_type=MESH,
    ).start()

    def ship_one(k, carry):
        ship(k)
        return carry

    lax.fori_loop(1, (early - 1) * step, ship_one, 0)

    def both(group, carry):
        for k in range(step):
            ship((group - 1) * step + k)
        fill(group)
        return carry

    lax.fori_loop(early, pairs // step, both, 0)
    lax.fori_loop(pairs - step, pairs, ship_one, 0)
    own.wait()
    rest = pl.ds(0, n - 1)
    pltpu.make_async_copy(x.at[rest, used], x.at[rest, used], send_sem).wait()
    pltpu.make_async_copy(out.at[rest, used], out.at[rest, used], recv_sem).wait()
    for copy in copies:
        copy.wait()


def send_owned(sources, strip, number):
    devices, owned = lax.axis_size("dev"), sources[1].shape[1]
    vmem, hbm = pl.BlockSpec(memory_space=pltpu.VMEM), pl.BlockSpec(memory_space=pltpu.HBM)
    return pl.pallas_call(
        send_owned_kernel,
        out_shape=[struct(devices, SUB, LANE)] + [struct(*strip.shape)] * 3,
        in_specs=[hbm] * 7,
        out_specs=[hbm] * 4,
        scratch_shapes=[
            pltpu.VMEM((devices, SUB, LANE), F32),
            pltpu.VMEM((SUB, owned), F32),
            pltpu.VMEM((owned // LANE, LANE), F32),
        ]
        + [pltpu.VMEM(v.shape, v.dtype) for v in sources]
        + [pltpu.SemaphoreType.DMA((7,))]
        + [pltpu.SemaphoreType.DMA] * 2
        + [pltpu.SemaphoreType.DMA((3,))] * 2,
        compiler_params=pltpu.CompilerParams(
            collective_id=number, has_side_effects=True, vmem_limit_bytes=60 * 1024 * 1024
        ),
        name="owner_send",
    )(*sources, strip)


def exchange_kernel(x, out, local_sem, send_sem, recv_sem):
    me = lax.axis_index("dev")
    n = lax.axis_size("dev")
    rows = pl.ds(0, USED)
    barrier = greet_all(n, me)
    own = pltpu.make_async_copy(x.at[me, rows], out.at[me, rows], local_sem)
    own.start()
    pl.semaphore_wait(barrier, n - 1)

    def start(k, carry):
        peer = lax.rem(me + k, n)
        pltpu.make_async_remote_copy(
            src_ref=x.at[peer, rows], dst_ref=out.at[me, rows], send_sem=send_sem, recv_sem=recv_sem,
            device_id=(peer,), device_id_type=MESH,
        ).start()
        return carry

    lax.fori_loop(1, n, start, 0)
    own.wait()
    rest = pl.ds(0, n - 1)
    pltpu.make_async_copy(x.at[rest, rows], x.at[rest, rows], send_sem).wait()
    pltpu.make_async_copy(out.at[rest, rows], out.at[rest, rows], recv_sem).wait()


def comm_params(number):
    return pltpu.CompilerParams(collective_id=number, has_side_effects=True, vmem_limit_bytes=4 << 20)


def exchange(x, number):
    vmem = pl.BlockSpec(memory_space=pltpu.VMEM)
    return pl.pallas_call(
        exchange_kernel,
        out_shape=jax.ShapeDtypeStruct(x.shape, x.dtype),
        in_specs=[vmem],
        out_specs=vmem,
        scratch_shapes=[pltpu.SemaphoreType.DMA] * 3,
        compiler_params=comm_params(number),
        name="exchange",
    )(x)


def halo_kernel(strip, before, after, send_sem, recv_sem):
    me = lax.axis_index("dev")
    n = lax.axis_size("dev")
    barrier = pltpu.get_barrier_semaphore()
    for hop in (1, n - 1):
        pl.semaphore_signal(barrier, inc=1, device_id=(lax.rem(me + hop, n),), device_id_type=MESH)
    pl.semaphore_wait(barrier, 2)
    copies = halo_copies(n, me, strip, before, after, send_sem, recv_sem)
    for copy in copies:
        copy.start()
    for copy in copies:
        copy.wait()


def halo_strips(strip, number):
    vmem = pl.BlockSpec(memory_space=pltpu.VMEM)
    return pl.pallas_call(
        halo_kernel,
        out_shape=[jax.ShapeDtypeStruct(strip.shape, strip.dtype)] * 2,
        in_specs=[vmem],
        out_specs=[vmem] * 2,
        scratch_shapes=[pltpu.SemaphoreType.DMA((2,))] * 2,
        compiler_params=comm_params(number),
        name="halo",
    )(strip)


def block_transpose(x):
    row = iota(x.shape, 0)
    block = lax.shift_right_logical(iota(x.shape, 1), 4)
    for d in (1, 2, 4):
        low_row = lax.bitwise_and(row, d) == 0
        low_block = lax.bitwise_and(block, d) == 0
        down = pltpu.roll(pltpu.roll(x, SUB - d, 0), 16 * d, 1)
        back = pltpu.roll(pltpu.roll(x, d, 0), LANE - 16 * d, 1)
        x = jnp.where(low_row == low_block, x, jnp.where(low_row, down, back))
    return x


def basis_rows(lanes):
    pixel = iota((1, lanes), 1)
    v = lax.shift_right_logical(pixel, 4).astype(F32) - 7.5
    u = lax.bitwise_and(pixel, 15).astype(F32) - 7.5
    return [u * u, u * v, v * v, u, v, jnp.ones_like(u)]


def stack_rows(rows, count):
    shape = (count, next(r for r in rows if r is not None).shape[1])
    at = iota(shape, 0)
    result = jnp.zeros(shape, F32)
    for p, row in enumerate(rows):
        if row is not None:
            result = jnp.where(at == p, jnp.broadcast_to(row, shape), result)
    return result


def scan_sub(x):
    at = iota(x.shape, 0)
    x = jnp.where(at == 0, 1.0, pltpu.roll(x, 1, 0))
    for d in (1, 2, 4):
        x = x * jnp.where(at >= d, pltpu.roll(x, d, 0), 1.0)
    return x


def take_turns(order, **workers):
    for name in order:
        next(workers[name], None)
    for worker in workers.values():
        for _ in worker:
            pass


def segments(count):
    groups = count // SUB // 2
    return [(seg, j, (seg * groups + j) * SUB) for j in range(groups) for seg in range(2)]


def split3(x):
    one, rest = split2(x)
    two, three = split2(rest)
    return one, two, three


def gather_columns(raw, flat, cols, slot):
    count = raw.shape[1]
    blocks = flat.shape[0] // (SUB + 1)
    row = iota((SUB, LANE), 0)
    wide = 2 * LANE
    founds = []
    for n in range(count // wide):
        idx = jnp.maximum(raw[:, n * wide : (n + 1) * wide], 0)
        hi, lo = lax.shift_right_logical(idx, 8), lax.bitwise_and(idx, 255)
        hot = onehot(lo, 256)
        found = jnp.dot(flat[...], jnp.concatenate([hot] * 2, axis=0), preferred_element_type=F32)
        founds.append((hi, found))
        yield
    for q in range(count // LANE):
        hi, found = founds[q // 2]
        span = slice((q % 2) * LANE, (q % 2 + 1) * LANE)
        out = slice(q * LANE, (q + 1) * LANE)
        hq = jnp.broadcast_to(hi[:, span], (SUB, LANE))
        bits = {1 << k: lax.bitwise_and(hq, 1 << k) != 0 for k in range(blocks.bit_length() - 1)}
        acc = pick_tree([lambda h=h: found[h * SUB : (h + 1) * SUB, span] for h in range(blocks)], bits)
        coarse = {k // SUB: v for k, v in bits.items() if k >= SUB}
        base = blocks * SUB
        last = pick_tree(
            [lambda v=v: found[base + v * SUB : base + (v + 1) * SUB, span] for v in range(blocks // SUB)], coarse
        )
        last = sub_sum(jnp.where(lax.bitwise_and(hq, 7) == row, last, 0.0))
        yield
        acc = jnp.where((row == 5) & (jnp.broadcast_to(raw[:, out], (SUB, LANE)) < 0), DEAD, acc)
        one, two, three = split3(acc)
        b_one, b_two = split2(last)
        more = jnp.where(row == 1, b_two, jnp.where(row == 7, last, b_one))
        more = jnp.where((row == 3) | (row == 4), pltpu.roll(one, 5, 0), more)
        more = jnp.where((row == 5) | (row == 6), pltpu.roll(acc, 7, 0), more)
        stack = jnp.concatenate([one, two, three, more], axis=0)
        cols[slot, out, :] = jnp.concatenate([stack, jnp.zeros((LANE - 32, LANE), F32)], axis=0).T
        yield


TURNS = "d" * 8 + "g" + "d" * 6 + "g" + "d" * 2 + "gg" + "d" * 2 + "gg" + "d" * 2 + "gg" + "d" * 4 + "gg"


def draw_tile(slot, tile, basis, chunk_rend, chunk_start, left_out, cols, alphas, rends):
    count = cols.shape[1]
    ones = jnp.ones((SUB, 256), F32)
    product = [ones, ones]
    piece = 64
    for c in range(count // piece):
        span = slice(c * piece, (c + 1) * piece)
        left = cols[slot, span, 0:32].astype(BF16)
        left_out[slot, span, :] = left
        alpha = jnp.exp2(jnp.dot(left, basis, preferred_element_type=F32))
        alphas[slot, span, :] = alpha
        rest = 1.0 - alpha
        parts = [rest[k * SUB : (k + 1) * SUB, :] for k in range(piece // SUB)]
        while len(parts) > 1:
            parts = [parts[k] * parts[k + 1] for k in range(0, len(parts), 2)]
        seg = 2 * c * piece // count
        product[seg] = product[seg] * parts[0]
        yield

    begin = scan_sub(product[0] * product[1])
    trans = [begin, begin * product[0]]
    zero = jnp.zeros((SUB, 256), F32)
    sums = [[zero] * 3, [zero] * 3]
    for seg in range(2):
        chunk_start[slot, seg] = trans[seg]
    for seg, j, at in segments(count):
        weight = trans[seg] * alphas[slot, at : at + SUB, :]
        trans[seg] = trans[seg] - weight
        color = cols[slot, at : at + SUB, :]
        sums[seg] = [t + weight * color[:, 29 + ch : 30 + ch] for ch, t in enumerate(sums[seg])]
        if seg == 1 and j % 2 == 1:
            yield
    for ch in range(3):
        for seg in range(2):
            chunk_rend[slot, ch, seg] = sums[seg][ch]
        rends[ch, pl.ds(tile, 1), :] = sub_sum(sums[0][ch] + sums[1][ch])[0:1, :]


def forward_kernel(
    lists, recv, image, image_too, chunk_rend, chunk_start, left_out, pieces, ninth, flat, cols, alphas, rends
):
    step = pl.program_id(0)
    row = iota((SUB, LANE), 0)

    @pl.when(step == 0)
    def _():
        blocks = pieces.shape[0] // SUB
        left = iota((SUB, LANE), 1) < 64

        def block(h, carry):
            lasts = []
            for half in range(2):
                owner = 4 * h + 2 * half
                eight, last = unpack_pair(recv[owner], recv[owner + 1], left, row)
                pieces[pl.ds(pl.multiple_of(h * SUB, SUB), SUB), half * LANE : (half + 1) * LANE] = eight
                lasts.append(last)
            ninth[pl.ds(h, 1), :] = jnp.concatenate(lasts, axis=1)
            return carry

        lax.fori_loop(0, blocks, block, 0)
        for rows, source in ((slice(0, blocks * SUB), pieces), (slice(blocks * SUB, None), ninth)):
            for k, part in enumerate(split2(source[...])):
                flat[rows, k * 256 : (k + 1) * 256] = part.astype(BF16)
        for _ in gather_columns(lists[0], flat, cols, 0):
            pass

    basis = stack_rows((basis_rows(256) + [None, None]) * 3, 32).astype(BF16)
    for slot in range(2):
        tile = 2 * step + slot
        later = jnp.minimum(tile + 1, lists.shape[0] - 1)
        take_turns(
            TURNS,
            g=gather_columns(lists[later], flat, cols, 1 - slot),
            d=draw_tile(slot, tile, basis, chunk_rend, chunk_start, left_out, cols, alphas, rends),
        )

    @pl.when(step == pl.num_programs(0) - 1)
    def _():
        for ch in range(3):
            for g in range(rends.shape[1] // SUB):
                for h in range(2):
                    block = block_transpose(rends[ch, g * SUB : (g + 1) * SUB, h * LANE : (h + 1) * LANE])
                    for to in (image, image_too):
                        to[ch, h * SUB : (h + 1) * SUB, g * LANE : (g + 1) * LANE] = block


def taps_of():
    offsets = np.arange(11, dtype=np.float32) - np.float32(5)
    taps = np.exp(-offsets * offsets / np.float32(4.5)).astype(np.float32)
    return [float(t) for t in taps / taps.sum(dtype=np.float32)]


TAPS = taps_of()


def blur_rows(read, start, count):
    total = TAPS[5] * read(start, count)
    for m in range(1, 6):
        total = total + TAPS[5 + m] * (read(start - m, count) + read(start + m, count))
    return total


def blur_lanes(x):
    rows, width = x.shape
    pad = jnp.zeros((rows, LANE), F32)
    wide = jnp.concatenate([x, pad], axis=1)
    total = TAPS[5] * x
    for m in range(1, 6):
        both = pltpu.roll(wide, m, 1) + pltpu.roll(wide, width + LANE - m, 1)
        total = total + TAPS[5 + m] * both[:, :width]
    return total


def loss_kernel(before, centre, after, t_before, t_centre, t_after, grad, pads, maps):
    height = centre.shape[1]
    mine = lax.axis_index("dev")
    total_rows = lax.axis_size("dev") * height
    width = centre.shape[2]
    at = iota((2 * height, width), 0) - height // 2 + mine * height
    inside = (at >= 0) & (at < total_rows)
    for ch in range(3):
        for i, (r, t) in enumerate(((before, t_before), (centre, t_centre), (after, t_after))):
            span = slice(i * height, (i + 1) * height)
            rr, tt = r[ch], t[ch]
            if i != 1:
                keep = mine > 0 if i == 0 else mine < total_rows // height - 1
                rr, tt = jnp.where(keep, rr, 0.0), jnp.where(keep, tt, 0.0)
            pads[0, span, :] = rr
            pads[1, span, :] = tt
            pads[2, span, :] = rr * rr
            pads[3, span, :] = tt * tt
            pads[4, span, :] = rr * tt

        def wide_blur(k):
            vertical = blur_rows(lambda s, n: pads[k, s : s + n, :], height // 2, 2 * height)
            return blur_lanes(vertical)

        mr, mt, rr, tt, rt = (wide_blur(k) for k in range(5))
        cv = rt - mr * mt
        top1 = 2.0 * mr * mt + 0.0001
        top2 = 2.0 * cv + 0.0009
        low1 = mr * mr + mt * mt + 0.0001
        low2 = (rr - mr * mr) + (tt - mt * mt) + 0.0009
        inv1, inv2 = 1.0 / low1, 1.0 / low2
        both = inv1 * inv2
        ssim = top1 * top2 * both
        d_rr = -ssim * inv2
        d_rt = 2.0 * top1 * both
        d_mr = 2.0 * (mt * (top2 - top1) * both + mr * ssim * (inv2 - inv1))
        for k, value in enumerate((d_mr, d_rr, d_rt)):
            maps[k] = jnp.where(inside, value, 0.0)

        def back_blur(k):
            vertical = blur_rows(lambda s, n: maps[k, s : s + n, :], height // 2, height)
            return blur_lanes(vertical)

        g_mr, g_rr, g_rt = (back_blur(k) for k in range(3))
        r, t = centre[ch], t_centre[ch]
        grad[ch] = 1.6 * (r - t) - 0.2 * (g_mr + 2.0 * r * g_rr + t * g_rt)


NT = (((1,), (1,)), ((), ()))


def onehot(lo, rows):
    return jnp.where(iota((rows, lo.shape[1]), 0) == lo, 1.0, 0.0).astype(BF16)


def spread(values, hi, blocks):
    masked = [jnp.where(hi == h, values, 0.0) for h in range(blocks)]
    return jnp.concatenate(masked, axis=0)


def scatter_block(eight, ninth, idx, blocks):
    span = idx.shape[1]
    hi, lo = lax.shift_right_arithmetic(idx, 8), lax.bitwise_and(idx, 255)
    hot = onehot(lo, 256)
    hi8 = jnp.broadcast_to(hi, (SUB, span))
    own = iota((blocks, span), 0) == hi
    left = []
    for values, extra in zip(split2(eight), split2(ninth)):
        left.append(spread(values, hi8, blocks))
        left.append(jnp.where(own, jnp.broadcast_to(extra, own.shape), 0.0))
    left = jnp.concatenate(left, axis=0).astype(BF16)
    both = lax.dot_general(left, hot, NT, preferred_element_type=F32)
    return both[: blocks * (SUB + 1), :] + both[blocks * (SUB + 1) :, :]


def shade_tile(slot, tile, left_in, chunk_rend, chunk_start, cots, halves):
    count = left_in.shape[1]
    rows = [cots[tile, ch : ch + 1, :] for ch in range(3)]
    ones, twos = zip(*(split2(r) for r in rows))
    basis = stack_rows((basis_rows(256) + [None, None]) * 3, 32)
    back = stack_rows(
        [None] * 6 + [ones[0], ones[1]] + [None] * 6 + [ones[0], ones[1]] + [None] * 6
        + [ones[0], ones[1], ones[2], ones[2], twos[2], twos[0], twos[1]], 32
    )
    right = jnp.concatenate([basis, back], axis=1).astype(BF16)

    inside = [sum(chunk_rend[slot, ch, seg] * rows[ch] for ch in range(3)) for seg in range(2)]
    at8 = iota((SUB, 256), 0)
    later = inside[0] + inside[1]
    later = jnp.where(at8 == SUB - 1, 0.0, pltpu.roll(later, SUB - 1, 0))
    for d in (1, 2, 4):
        later = later + jnp.where(at8 < SUB - d, pltpu.roll(later, SUB - d, 0), 0.0)
    behind = [later + inside[1] + inside[0], later + inside[1]]
    trans = [chunk_start[slot, seg] for seg in range(2)]

    piece = 64
    order = [c // 2 + (c % 2) * (count // piece // 2) for c in range(count // piece)]

    def field_of(c):
        return jnp.dot(left_in[slot, c * piece : (c + 1) * piece, :], right, preferred_element_type=F32)

    ahead = 1
    fields = [field_of(c) for c in order[:ahead]]
    for n, c in enumerate(order):
        if n + ahead < len(order):
            fields.append(field_of(order[n + ahead]))
        seg = 2 * c * piece // count
        field = fields[n]
        alpha = jnp.exp2(field[:, 0:256])
        ratio = alpha / (1.0 - alpha)
        parts = []
        for k in range(piece // SUB):
            span = slice(k * SUB, (k + 1) * SUB)
            weight = trans[seg] * alpha[span]
            trans[seg] = trans[seg] - weight
            shown = weight * field[span, 256:512]
            behind[seg] = behind[seg] - shown
            parts.append((shown - ratio[span] * behind[seg], weight))
        at = slice(c * piece, (c + 1) * piece)
        value = jnp.concatenate([p[0] for p in parts], axis=0)
        one = value.astype(BF16)
        halves[slot, at, 0:256] = one
        halves[slot, at, 256:512] = (value - one.astype(F32)).astype(BF16)
        halves[slot, at, 512:768] = jnp.concatenate([p[1] for p in parts], axis=0).astype(BF16)
        yield


BACK_TURNS = "fss" * 4


def find_moments(slot, tile, cots, halves, grads):
    rows = [cots[tile, ch : ch + 1, :] for ch in range(3)]
    ones, twos = zip(*(split2(r) for r in rows))
    base = stack_rows(basis_rows(256), 16)
    colours = stack_rows([None] * 6 + list(ones) + list(twos), 16)
    kernel = jnp.concatenate([base, base, colours], axis=1).astype(BF16)
    wide = 128
    for n in range(halves.shape[1] // wide):
        at = slice(n * wide, (n + 1) * wide)
        found = lax.dot_general(kernel, halves[slot, at, :], NT, preferred_element_type=F32)
        low = found[8:16, :]
        at16 = iota(low.shape, 0)
        top = found[0:8, :] + jnp.where(at16 >= 6, pltpu.roll(low, 5, 0), 0.0)
        grads[tile, 0:8, at] = top
        grads[tile, 8:9, at] = low[0:1, :] + low[3:4, :]
        yield


def backward_kernel(lists, left_in, grad, chunk_rend, chunk_start, out, cots, halves, grads, slots):
    step = pl.program_id(0)
    steps = pl.num_programs(0)

    @pl.when(step == 0)
    def _():
        for ch in range(3):
            for g in range(cots.shape[0] // SUB):
                for h in range(2):
                    span = slice(h * LANE, (h + 1) * LANE)
                    block = block_transpose(grad[ch, h * SUB : (h + 1) * SUB, g * LANE : (g + 1) * LANE])
                    for t in range(SUB):
                        cots[g * SUB + t, ch : ch + 1, span] = block[t : t + 1, :]

    for slot in range(2):
        tile = 2 * step + slot
        past = jnp.maximum(tile - 1, 0)
        take_turns(
            BACK_TURNS,
            f=find_moments(1 - slot, past, cots, halves, grads),
            s=shade_tile(slot, tile, left_in, chunk_rend, chunk_start, cots, halves),
        )

    @pl.when(step == steps - 1)
    def _():
        for _ in find_moments(1, 2 * step + 1, cots, halves, grads):
            pass
        slots[...] = jnp.zeros_like(slots)
        blocks = slots.shape[0] // (SUB + 1)
        group = 2

        def chunk(c, carry):
            each = [c * group + k for k in range(group)]
            idx = jnp.concatenate([jnp.maximum(lists[t], 0) for t in each], axis=1)
            eight = jnp.concatenate([grads[t, 0:8, :] for t in each], axis=1)
            ninth = jnp.concatenate([grads[t, 8:9, :] for t in each], axis=1)
            slots[...] = slots[...] + scatter_block(eight, ninth, idx, blocks)
            return carry

        lax.fori_loop(0, cots.shape[0] // group, chunk, 0)
        left = iota((SUB, LANE), 1) < 64
        row = iota((SUB, LANE), 0)
        for h in range(blocks):
            for half in range(2):
                span = slice(half * LANE, (half + 1) * LANE)
                acc = slots[h * SUB : (h + 1) * SUB, span]
                extra = jnp.broadcast_to(slots[blocks * SUB + h : blocks * SUB + h + 1, span], (SUB, LANE))
                owner = 4 * h + 2 * half
                out[owner], out[owner + 1] = pack_pair(acc, extra, left, row)


def home_kernel(back, send, centres, conic, rho, opacity, out, total, rows):
    lane = iota((SUB, LANE), 1)
    left = lane < 64
    row = iota((SUB, LANE), 0)
    pairs = back.shape[0] // 2
    per = 8
    blocks = centres.shape[1] // 256
    total[...] = jnp.zeros_like(total)

    def chunk(c, carry):
        eight, ninth = [], []
        for k in range(per):
            i = c * per + k
            values, last = unpack_pair(back[2 * i], back[2 * i + 1], left, row)
            eight.append(values)
            ninth.append(last)
        start = pl.multiple_of(c * per * LANE, per * LANE)
        idx = send[0:1, pl.ds(start, per * LANE)]
        total[...] = total[...] + scatter_block(
            jnp.concatenate(eight, axis=1), jnp.concatenate(ninth, axis=1), idx, blocks
        )
        return carry

    lax.fori_loop(0, pairs // per, chunk, 0)
    for h in range(blocks):
        span = slice(h * 256, (h + 1) * 256)
        rows[0:8, span] = total[h * SUB : (h + 1) * SUB, :]
        rows[8:9, span] = total[blocks * SUB + h : blocks * SUB + h + 1, :]
    m_uu, m_uv, m_vv, m_u, m_v, m_1 = (rows[p : p + 1, :] for p in range(6))
    cx, cy = centres[0:1, :], centres[1:2, :]
    a, c = conic[0:1, :], conic[1:2, :]
    r = rho[...]
    root = jnp.sqrt(a * c)
    b = r * root
    x1, y1 = m_u - cx * m_1, m_v - cy * m_1
    xx = m_uu - cx * (m_u + x1)
    yy = m_vv - cy * (m_v + y1)
    xy = m_uv - cx * m_v - cy * x1
    out[0:1, :] = a * x1 + b * y1
    out[1:2, :] = c * y1 + b * x1
    out[2:3, :] = -0.5 * xx - xy * (0.5 * r * (root / a))
    out[3:4, :] = -0.5 * yy - xy * (0.5 * r * (root / c))
    out[4:5, :] = -xy * root
    out[5:6, :] = m_1 / opacity[...]
    out[6:9, :] = rows[6:9, :]


def struct(*shape, dtype=F32):
    return jax.ShapeDtypeStruct(shape, dtype)


def shards(tile_lists, send_rows, centres, conic, rho, opacity, colors, target):
    devices = lax.axis_size("dev")
    owned = centres.shape[1]
    tiles, count = tile_lists.shape
    height, width = target.shape[1], target.shape[2]
    pixels = height * height
    params = lambda mib: pltpu.CompilerParams(vmem_limit_bytes=mib << 20)
    sources = (send_rows, centres, conic, rho, opacity, colors)
    lists = tile_lists.reshape(tiles, SUB, count // SUB).transpose(0, 2, 1).reshape(tiles, 1, count)
    incoming, t_before, t_centre, t_after = send_owned(sources, target, 0)
    whole = lambda *shape: pl.BlockSpec(shape, lambda t: (0,) * len(shape))
    per = 2
    per_tile = lambda *shape: pl.BlockSpec((per,) + shape, lambda t: (t,) + (0,) * len(shape))
    hi_blocks = devices * 64 // 256
    image, image_too, chunk_rend, chunk_start, left = pl.pallas_call(
        forward_kernel,
        grid=(tiles // per,),
        in_specs=[whole(tiles, 1, count), whole(devices, SUB, LANE)],
        out_specs=[
            whole(3, height, width), whole(3, height, width),
            per_tile(3, 2, SUB, pixels), per_tile(2, SUB, pixels), per_tile(count, 32),
        ],
        out_shape=[
            struct(3, height, width),
            struct(3, height, width),
            struct(tiles, 3, 2, SUB, pixels),
            struct(tiles, 2, SUB, pixels),
            struct(tiles, count, 32, dtype=BF16),
        ],
        scratch_shapes=[
            pltpu.VMEM((hi_blocks * SUB, 256), F32),
            pltpu.VMEM((hi_blocks, 256), F32),
            pltpu.VMEM((hi_blocks * (SUB + 1), 2 * 256), BF16),
            pltpu.VMEM((per, count, LANE), F32),
            pltpu.VMEM((per, count, pixels), F32),
            pltpu.VMEM((3, tiles, pixels), F32),
        ],
        compiler_params=params(16),
        name="tile_forward",
    )(lists, incoming)

    before, after = halo_strips(image_too, 1)
    pixel_grad = pl.pallas_call(
        loss_kernel,
        out_shape=struct(3, height, width),
        scratch_shapes=[pltpu.VMEM((5, 3 * height, width), F32), pltpu.VMEM((3, 2 * height, width), F32)],
        compiler_params=params(8),
        name="loss_gradient",
    )(before, image_too, after, t_before, t_centre, t_after)

    slot_grads = pl.pallas_call(
        backward_kernel,
        grid=(tiles // per,),
        in_specs=[
            whole(tiles, 1, count), per_tile(count, 32), whole(3, height, width),
            per_tile(3, 2, SUB, pixels), per_tile(2, SUB, pixels),
        ],
        out_specs=whole(devices, SUB, LANE),
        out_shape=struct(devices, SUB, LANE),
        scratch_shapes=[
            pltpu.VMEM((tiles, 3, pixels), F32),
            pltpu.VMEM((per, count, 3 * pixels), BF16),
            pltpu.VMEM((tiles, 16, count), F32),
            pltpu.VMEM((hi_blocks * (SUB + 1), 256), F32),
        ],
        compiler_params=params(20),
        name="tile_backward",
    )(lists, left, pixel_grad, chunk_rend, chunk_start)
    returned = exchange(slot_grads, 2)
    grads = pl.pallas_call(
        home_kernel,
        out_shape=struct(9, owned),
        scratch_shapes=[
            pltpu.VMEM((owned // 256 * (SUB + 1), 256), F32),
            pltpu.VMEM((16, owned), F32),
        ],
        compiler_params=params(16),
        name="owner_scatter",
    )(returned, send_rows, centres, conic, rho, opacity)
    return image, grads


def solution(mesh):
    return jax.shard_map(
        shards,
        mesh=mesh,
        in_specs=(
            P("dev", None),
            P("dev", None),
            P(None, "dev"),
            P(None, "dev"),
            P(None, "dev"),
            P(None, "dev"),
            P(None, "dev"),
            P(None, "dev", None),
        ),
        out_specs=(P(None, "dev", None), P(None, "dev")),
        check_vma=False,
    )
```

```python
import functools
import math

import jax
import jax.numpy as jnp
import numpy as np
from jax import lax
from jax.experimental import pallas as pl
from jax.experimental.pallas import tpu as pltpu
from jax.sharding import PartitionSpec as P

F32 = jnp.float32
BF16 = jnp.bfloat16
LOG2E = math.log2(math.e)
SUB, LANE = 8, 128
DEAD = -10000.0


def lane_pick(table, lanes):
    return jnp.take_along_axis(table, lanes, axis=1, mode="promise_in_bounds")


def iota(shape, dim):
    return lax.broadcasted_iota(jnp.int32, shape, dim)


def sub_sum(x):
    for d in (4, 2, 1):
        x = x + pltpu.roll(x, d, 0)
    return x


def split2(x):
    one = x.astype(BF16).astype(F32)
    return one, x - one


def coefficient_rows(cx, cy, a, c, rho, op):
    b = rho * jnp.sqrt(a * c)
    bx, by = a * cx + b * cy, c * cy + b * cx
    one = jnp.log(op) - 0.5 * (cx * bx + cy * by)
    return [LOG2E * k for k in (-0.5 * a, -b, -0.5 * c, bx, by, one)]


def pick_tree(parts, bits):
    if len(parts) == 1:
        return parts[0]()
    half = len(parts) // 2
    return jnp.where(bits[half], pick_tree(parts[half:], bits), pick_tree(parts[:half], bits))


def pick_nine(table, ninth, idx, row, blocks):
    hi, lo = lax.shift_right_logical(idx, 7), lax.bitwise_and(idx, 127)
    bits = {1 << k: lax.bitwise_and(hi, 1 << k) != 0 for k in range(blocks.bit_length() - 1)}
    eight = pick_tree([lambda h=h: lane_pick(table(h), lo) for h in range(blocks)], bits)
    coarse = {k // SUB: v for k, v in bits.items() if k >= SUB}
    last = pick_tree(
        [lambda v=v: lane_pick(ninth[v * SUB : (v + 1) * SUB, :], lo) for v in range(blocks // SUB)], coarse
    )
    return eight, sub_sum(jnp.where(lax.bitwise_and(hi, 7) == row, last, 0.0))


MESH = pl.DeviceIdType.MESH
USED = 5
RIM = 10
RIMS = 32


def pack_pair(eight, last, left, row):
    low = pltpu.roll(eight, 4, 0)
    even = jnp.where(left, eight, pltpu.roll(low, 64, 1))
    odd = jnp.where(left, pltpu.roll(eight, 64, 1), low)
    return jnp.where(row < 4, even, last), jnp.where(row < 4, odd, pltpu.roll(last, 64, 1))


def unpack_pair(even, odd, left, row):
    high = jnp.where(left, even, pltpu.roll(odd, 64, 1))
    low = jnp.where(left, pltpu.roll(even, 64, 1), odd)
    return jnp.where(row < 4, high, pltpu.roll(low, 4, 0)), high[4:5, :]


def greet_all(n, me):
    barrier = pltpu.get_barrier_semaphore()

    def greet(k, carry):
        pl.semaphore_signal(barrier, inc=1, device_id=(lax.rem(me + k, n),), device_id_type=MESH)
        return carry

    lax.fori_loop(1, n, greet, 0)
    return barrier


def halo_copies(n, me, strip, before, after, send_sem, recv_sem):
    return [
        pltpu.make_async_remote_copy(
            src_ref=strip, dst_ref=to, send_sem=send_sem.at[k], recv_sem=recv_sem.at[k],
            device_id=(lax.rem(me + hop, n),), device_id_type=MESH,
        )
        for k, (hop, to) in enumerate(((1, before), (n - 1, after)))
    ]


def send_owned_kernel(*refs):
    sources, strip, (out, strips), x, table, ninth = refs[:6], refs[6], refs[7:9], *refs[9:12]
    places, (local_sem, send_sem, recv_sem, halo_send, halo_recv) = refs[12:18], refs[18:23]
    me = lax.axis_index("dev")
    n = lax.axis_size("dev")
    fetched = [pltpu.make_async_copy(a, b, local_sem.at[k]) for k, (a, b) in enumerate(zip(sources, places))]
    for copy in fetched:
        copy.start()
    barrier = greet_all(n, me)
    for copy in fetched:
        copy.wait()
    send, centres, conic, rho, opacity, colors = places
    rows = coefficient_rows(
        centres[0:1, :], centres[1:2, :], conic[0:1, :], conic[1:2, :], rho[...], opacity[...]
    )
    for p, value in enumerate(rows + [colors[0:1, :], colors[1:2, :]]):
        table[p : p + 1, :] = value
    blocks = table.shape[1] // LANE
    for h in range(blocks):
        ninth[h : h + 1, :] = colors[2:3, h * LANE : (h + 1) * LANE]
    left = iota((SUB, LANE), 1) < 64
    row = iota((SUB, LANE), 0)
    pairs = n // 2
    mine = me // 2
    used = pl.ds(0, USED)
    step = 4

    def fill(group):
        for k in range(step):
            i = lax.rem(mine + group * step + k, pairs)
            start = pl.multiple_of(i * LANE, LANE)
            idx = jnp.broadcast_to(jnp.maximum(send[0:1, pl.ds(start, LANE)], 0), (SUB, LANE))
            eight, last = pick_nine(lambda h: table[:, h * LANE : (h + 1) * LANE], ninth, idx, row, blocks)
            x[2 * i], x[2 * i + 1] = pack_pair(eight, last, left, row)

    def ship(k):
        for core in range(2):
            peer = 2 * lax.rem(mine + k, pairs) + core
            pltpu.make_async_remote_copy(
                src_ref=x.at[peer, used], dst_ref=out.at[me, used], send_sem=send_sem, recv_sem=recv_sem,
                device_id=(peer,), device_id_type=MESH,
            ).start()

    copies = halo_copies(n, me, strip, strips.at[0], strips.at[2], halo_send, halo_recv)
    copies.append(pltpu.make_async_copy(strip, strips.at[1], halo_recv.at[2]))
    early = 5

    def first(group, carry):
        fill(group)
        return carry

    lax.fori_loop(0, early, first, 0)
    pl.semaphore_wait(barrier, n - 1)
    for copy in copies:
        copy.start()
    partner = me + 1 - 2 * lax.rem(me, 2)
    own = pltpu.make_async_copy(x.at[me, used], out.at[me, used], local_sem.at[6])
    own.start()
    pltpu.make_async_remote_copy(
        src_ref=x.at[partner, used], dst_ref=out.at[me, used], send_sem=send_sem, recv_sem=recv_sem,
        device_id=(partner,), device_id_type=MESH,
    ).start()

    def ship_one(k, carry):
        ship(k)
        return carry

    lax.fori_loop(1, (early - 1) * step, ship_one, 0)

    def both(group, carry):
        for k in range(step):
            ship((group - 1) * step + k)
        fill(group)
        return carry

    lax.fori_loop(early, pairs // step, both, 0)
    lax.fori_loop(pairs - step, pairs, ship_one, 0)
    own.wait()
    rest = pl.ds(0, n - 1)
    pltpu.make_async_copy(x.at[rest, used], x.at[rest, used], send_sem).wait()
    pltpu.make_async_copy(out.at[rest, used], out.at[rest, used], recv_sem).wait()
    for copy in copies:
        copy.wait()


def send_owned(sources, strip, number):
    devices, owned = lax.axis_size("dev"), sources[1].shape[1]
    vmem, hbm = pl.BlockSpec(memory_space=pltpu.VMEM), pl.BlockSpec(memory_space=pltpu.HBM)
    return pl.pallas_call(
        send_owned_kernel,
        out_shape=[struct(devices, SUB, LANE), struct(3, *strip.shape)],
        in_specs=[hbm] * 7,
        out_specs=[hbm] * 2,
        scratch_shapes=[
            pltpu.VMEM((devices, SUB, LANE), F32),
            pltpu.VMEM((SUB, owned), F32),
            pltpu.VMEM((owned // LANE, LANE), F32),
        ]
        + [pltpu.VMEM(v.shape, v.dtype) for v in sources]
        + [pltpu.SemaphoreType.DMA((7,))]
        + [pltpu.SemaphoreType.DMA] * 2
        + [pltpu.SemaphoreType.DMA((3,))] * 2,
        compiler_params=pltpu.CompilerParams(
            collective_id=number, has_side_effects=True, vmem_limit_bytes=60 * 1024 * 1024
        ),
        name="owner_send",
    )(*sources, strip)


def exchange_kernel(x, out, local_sem, send_sem, recv_sem):
    me = lax.axis_index("dev")
    n = lax.axis_size("dev")
    rows = pl.ds(0, USED)
    barrier = greet_all(n, me)
    own = pltpu.make_async_copy(x.at[me, rows], out.at[me, rows], local_sem)
    own.start()
    pl.semaphore_wait(barrier, n - 1)

    def start(k, carry):
        peer = lax.rem(me + k, n)
        pltpu.make_async_remote_copy(
            src_ref=x.at[peer, rows], dst_ref=out.at[me, rows], send_sem=send_sem, recv_sem=recv_sem,
            device_id=(peer,), device_id_type=MESH,
        ).start()
        return carry

    lax.fori_loop(1, n, start, 0)
    own.wait()
    rest = pl.ds(0, n - 1)
    pltpu.make_async_copy(x.at[rest, rows], x.at[rest, rows], send_sem).wait()
    pltpu.make_async_copy(out.at[rest, rows], out.at[rest, rows], recv_sem).wait()


def comm_params(number):
    return pltpu.CompilerParams(collective_id=number, has_side_effects=True, vmem_limit_bytes=4 << 20)


def exchange(x, number):
    vmem = pl.BlockSpec(memory_space=pltpu.VMEM)
    return pl.pallas_call(
        exchange_kernel,
        out_shape=jax.ShapeDtypeStruct(x.shape, x.dtype),
        in_specs=[vmem],
        out_specs=vmem,
        scratch_shapes=[pltpu.SemaphoreType.DMA] * 3,
        compiler_params=comm_params(number),
        name="exchange",
    )(x)


def block_transpose(x):
    row = iota(x.shape, 0)
    block = lax.shift_right_logical(iota(x.shape, 1), 4)
    for d in (1, 2, 4):
        low_row = lax.bitwise_and(row, d) == 0
        low_block = lax.bitwise_and(block, d) == 0
        down = pltpu.roll(pltpu.roll(x, SUB - d, 0), 16 * d, 1)
        back = pltpu.roll(pltpu.roll(x, d, 0), LANE - 16 * d, 1)
        x = jnp.where(low_row == low_block, x, jnp.where(low_row, down, back))
    return x


def basis_rows(lanes):
    pixel = iota((1, lanes), 1)
    v = lax.shift_right_logical(pixel, 4).astype(F32) - 7.5
    u = lax.bitwise_and(pixel, 15).astype(F32) - 7.5
    return [u * u, u * v, v * v, u, v, jnp.ones_like(u)]


def stack_rows(rows, count):
    shape = (count, next(r for r in rows if r is not None).shape[1])
    at = iota(shape, 0)
    result = jnp.zeros(shape, F32)
    for p, row in enumerate(rows):
        if row is not None:
            result = jnp.where(at == p, jnp.broadcast_to(row, shape), result)
    return result


def scan_sub(x):
    at = iota(x.shape, 0)
    x = jnp.where(at == 0, 1.0, pltpu.roll(x, 1, 0))
    for d in (1, 2, 4):
        x = x * jnp.where(at >= d, pltpu.roll(x, d, 0), 1.0)
    return x


def take_turns(order, **workers):
    for name in order:
        next(workers[name], None)
    for worker in workers.values():
        for _ in worker:
            pass


def segments(count):
    groups = count // SUB // 2
    return [(seg, j, (seg * groups + j) * SUB) for j in range(groups) for seg in range(2)]


def split3(x):
    one, rest = split2(x)
    two, three = split2(rest)
    return one, two, three


def gather_columns(raw, flat, cols, slot):
    count = raw.shape[1]
    blocks = flat.shape[0] // (SUB + 1)
    row = iota((SUB, LANE), 0)
    wide = 2 * LANE
    founds = []
    for n in range(count // wide):
        idx = jnp.maximum(raw[:, n * wide : (n + 1) * wide], 0)
        hi, lo = lax.shift_right_logical(idx, 8), lax.bitwise_and(idx, 255)
        hot = onehot(lo, 256)
        found = jnp.dot(flat[...], jnp.concatenate([hot] * 2, axis=0), preferred_element_type=F32)
        founds.append((hi, found))
        yield
    for q in range(count // LANE):
        hi, found = founds[q // 2]
        span = slice((q % 2) * LANE, (q % 2 + 1) * LANE)
        out = slice(q * LANE, (q + 1) * LANE)
        hq = jnp.broadcast_to(hi[:, span], (SUB, LANE))
        bits = {1 << k: lax.bitwise_and(hq, 1 << k) != 0 for k in range(blocks.bit_length() - 1)}
        acc = pick_tree([lambda h=h: found[h * SUB : (h + 1) * SUB, span] for h in range(blocks)], bits)
        coarse = {k // SUB: v for k, v in bits.items() if k >= SUB}
        base = blocks * SUB
        last = pick_tree(
            [lambda v=v: found[base + v * SUB : base + (v + 1) * SUB, span] for v in range(blocks // SUB)], coarse
        )
        last = sub_sum(jnp.where(lax.bitwise_and(hq, 7) == row, last, 0.0))
        yield
        acc = jnp.where((row == 5) & (jnp.broadcast_to(raw[:, out], (SUB, LANE)) < 0), DEAD, acc)
        one, two, three = split3(acc)
        b_one, b_two = split2(last)
        more = jnp.where(row == 1, b_two, jnp.where(row == 7, last, b_one))
        more = jnp.where((row == 3) | (row == 4), pltpu.roll(one, 5, 0), more)
        more = jnp.where((row == 5) | (row == 6), pltpu.roll(acc, 7, 0), more)
        stack = jnp.concatenate([one, two, three, more], axis=0)
        cols[slot, out, :] = jnp.concatenate([stack, jnp.zeros((LANE - 32, LANE), F32)], axis=0).T
        yield


TURNS = "d" * 8 + "g" + "d" * 6 + "g" + "d" * 2 + "gg" + "d" * 2 + "gg" + "d" * 2 + "gg" + "d" * 4 + "gg"


def draw_tile(slot, tile, basis, chunk_rend, chunk_start, left_out, cols, alphas, rends):
    count = cols.shape[1]
    ones = jnp.ones((SUB, 256), F32)
    product = [ones, ones]
    piece = 64
    for c in range(count // piece):
        span = slice(c * piece, (c + 1) * piece)
        left = cols[slot, span, 0:32].astype(BF16)
        left_out[slot, span, :] = left
        alpha = jnp.exp2(jnp.dot(left, basis, preferred_element_type=F32))
        alphas[slot, span, :] = alpha
        rest = 1.0 - alpha
        parts = [rest[k * SUB : (k + 1) * SUB, :] for k in range(piece // SUB)]
        while len(parts) > 1:
            parts = [parts[k] * parts[k + 1] for k in range(0, len(parts), 2)]
        seg = 2 * c * piece // count
        product[seg] = product[seg] * parts[0]
        yield

    begin = scan_sub(product[0] * product[1])
    trans = [begin, begin * product[0]]
    zero = jnp.zeros((SUB, 256), F32)
    sums = [[zero] * 3, [zero] * 3]
    for seg in range(2):
        chunk_start[slot, seg] = trans[seg]
    for seg, j, at in segments(count):
        weight = trans[seg] * alphas[slot, at : at + SUB, :]
        trans[seg] = trans[seg] - weight
        color = cols[slot, at : at + SUB, :]
        sums[seg] = [t + weight * color[:, 29 + ch : 30 + ch] for ch, t in enumerate(sums[seg])]
        if seg == 1 and j % 2 == 1:
            yield
    for ch in range(3):
        for seg in range(2):
            chunk_rend[slot, ch, seg] = sums[seg][ch]
        rends[ch, pl.ds(tile, 1), :] = sub_sum(sums[0][ch] + sums[1][ch])[0:1, :]


def forward_kernel(
    lists, recv, image, image_too, head, tail, chunk_rend, chunk_start, left_out, pieces, ninth, flat, cols, alphas, rends
):
    step = pl.program_id(0)
    row = iota((SUB, LANE), 0)

    @pl.when(step == 0)
    def _():
        blocks = pieces.shape[0] // SUB
        left = iota((SUB, LANE), 1) < 64

        def block(h, carry):
            lasts = []
            for half in range(2):
                owner = 4 * h + 2 * half
                eight, last = unpack_pair(recv[owner], recv[owner + 1], left, row)
                pieces[pl.ds(pl.multiple_of(h * SUB, SUB), SUB), half * LANE : (half + 1) * LANE] = eight
                lasts.append(last)
            ninth[pl.ds(h, 1), :] = jnp.concatenate(lasts, axis=1)
            return carry

        lax.fori_loop(0, blocks, block, 0)
        for rows, source in ((slice(0, blocks * SUB), pieces), (slice(blocks * SUB, None), ninth)):
            for k, part in enumerate(split2(source[...])):
                flat[rows, k * 256 : (k + 1) * 256] = part.astype(BF16)
        for _ in gather_columns(lists[0], flat, cols, 0):
            pass

    basis = stack_rows((basis_rows(256) + [None, None]) * 3, 32).astype(BF16)
    for slot in range(2):
        tile = 2 * step + slot
        later = jnp.minimum(tile + 1, lists.shape[0] - 1)
        take_turns(
            TURNS,
            g=gather_columns(lists[later], flat, cols, 1 - slot),
            d=draw_tile(slot, tile, basis, chunk_rend, chunk_start, left_out, cols, alphas, rends),
        )

    @pl.when(step == pl.num_programs(0) - 1)
    def _():
        for ch in range(3):
            for g in range(rends.shape[1] // SUB):
                for h in range(2):
                    block = block_transpose(rends[ch, g * SUB : (g + 1) * SUB, h * LANE : (h + 1) * LANE])
                    span = slice(g * LANE, (g + 1) * LANE)
                    for to in (image, image_too):
                        to[ch, h * SUB : (h + 1) * SUB, span] = block
                    at = RIM * ch
                    if h == 0:
                        head[at : at + SUB, span] = block
                        tail[at : at + 2, span] = block[6:8, :]
                    else:
                        head[at + SUB : at + RIM, span] = block[0:2, :]
                        tail[at + 2 : at + RIM, span] = block


def taps_of():
    offsets = np.arange(11, dtype=np.float32) - np.float32(5)
    taps = np.exp(-offsets * offsets / np.float32(4.5)).astype(np.float32)
    return [float(t) for t in taps / taps.sum(dtype=np.float32)]


TAPS = taps_of()


def blur_rows(read, start, count):
    total = TAPS[5] * read(start, count)
    for m in range(1, 6):
        total = total + TAPS[5 + m] * (read(start - m, count) + read(start + m, count))
    return total


def blur_lanes(x):
    rows, width = x.shape
    pad = jnp.zeros((rows, LANE), F32)
    wide = jnp.concatenate([x, pad], axis=1)
    total = TAPS[5] * x
    for m in range(1, 6):
        both = pltpu.roll(wide, m, 1) + pltpu.roll(wide, width + LANE - m, 1)
        total = total + TAPS[5 + m] * both[:, :width]
    return total


def loss_kernel(
    centre, head, tail, target, grad, before, after, pads, maps, blurred, send_sem, recv_sem
):
    height, width = centre.shape[1:]
    me = lax.axis_index("dev")
    n = lax.axis_size("dev")
    barrier = pltpu.get_barrier_semaphore()
    for hop in (1, n - 1):
        pl.semaphore_signal(barrier, inc=1, device_id=(lax.rem(me + hop, n),), device_id_type=MESH)
    rim = RIM
    copies = []
    for part in range(RIMS // SUB):
        rows = pl.ds(part * SUB, SUB)
        for k, (hop, source, to) in enumerate(((1, tail, before), (n - 1, head, after))):
            copies.append(
                pltpu.make_async_remote_copy(
                    src_ref=source.at[rows], dst_ref=to.at[rows],
                    send_sem=send_sem.at[2 * part + k], recv_sem=recv_sem.at[2 * part + k],
                    device_id=(lax.rem(me + hop, n),), device_id_type=MESH,
                )
            )
    t_before, t_centre, t_after = target.at[0], target.at[1], target.at[2]
    pl.semaphore_wait(barrier, 2)
    for copy in copies:
        copy.start()

    at = iota((2 * height, width), 0) - height // 2 + me * height
    inside = (at >= 0) & (at < n * height)

    def wide_blur(k):
        vertical = blur_rows(lambda s, c: pads[k, s : s + c, :], height // 2, 2 * height)
        return blur_lanes(vertical)

    edge = height - rim
    for k in range(5):
        pads[k, 0:edge, :] = jnp.zeros((edge, width), F32)
        pads[k, 3 * height - edge :, :] = jnp.zeros((edge, width), F32)
    for ch in range(3):
        first = jnp.where(me > 0, t_before[ch, edge:height, :], 0.0)
        last = jnp.where(me < n - 1, t_after[ch, 0:rim, :], 0.0)
        for rows, tt in (
            (slice(edge, height), first), (slice(height, 2 * height), t_centre[ch]),
            (slice(2 * height, 2 * height + rim), last),
        ):
            pads[1, rows, :] = tt
            pads[3, rows, :] = tt * tt
        blurred[ch, 0] = wide_blur(1)
        blurred[ch, 1] = wide_blur(3)

    for ch in range(3):
        for copy in copies[:4] if ch == 0 else copies[2 * ch + 2 : 2 * ch + 4]:
            copy.wait_recv()
        for rows, keep, r, t in (
            (slice(edge, height), me > 0, before[rim * ch : rim * (ch + 1), :], t_before[ch, edge:height, :]),
            (slice(height, 2 * height), None, centre[ch], t_centre[ch]),
            (slice(2 * height, 2 * height + rim), me < n - 1, after[rim * ch : rim * (ch + 1), :], t_after[ch, 0:rim, :]),
        ):
            if keep is not None:
                r, t = jnp.where(keep, r, 0.0), jnp.where(keep, t, 0.0)
            pads[0, rows, :] = r
            pads[2, rows, :] = r * r
            pads[4, rows, :] = r * t
        mr, rr, rt = wide_blur(0), wide_blur(2), wide_blur(4)
        mt, tt = blurred[ch, 0], blurred[ch, 1]
        cv = rt - mr * mt
        top1 = 2.0 * mr * mt + 0.0001
        top2 = 2.0 * cv + 0.0009
        low1 = mr * mr + mt * mt + 0.0001
        low2 = (rr - mr * mr) + (tt - mt * mt) + 0.0009
        inv1, inv2 = 1.0 / low1, 1.0 / low2
        both = inv1 * inv2
        ssim = top1 * top2 * both
        d_rr = -ssim * inv2
        d_rt = 2.0 * top1 * both
        d_mr = 2.0 * (mt * (top2 - top1) * both + mr * ssim * (inv2 - inv1))
        for k, value in enumerate((d_mr, d_rr, d_rt)):
            maps[k] = jnp.where(inside, value, 0.0)

        def back_blur(k):
            vertical = blur_rows(lambda s, c: maps[k, s : s + c, :], height // 2, height)
            return blur_lanes(vertical)

        g_mr, g_rr, g_rt = (back_blur(k) for k in range(3))
        r, t = centre[ch], t_centre[ch]
        grad[ch] = 1.6 * (r - t) - 0.2 * (g_mr + 2.0 * r * g_rr + t * g_rt)
    for copy in copies:
        copy.wait_send()


NT = (((1,), (1,)), ((), ()))


def onehot(lo, rows):
    return jnp.where(iota((rows, lo.shape[1]), 0) == lo, 1.0, 0.0).astype(BF16)


def spread(values, hi, blocks):
    masked = [jnp.where(hi == h, values, 0.0) for h in range(blocks)]
    return jnp.concatenate(masked, axis=0)


def scatter_block(eight, ninth, idx, blocks):
    span = idx.shape[1]
    hi, lo = lax.shift_right_arithmetic(idx, 8), lax.bitwise_and(idx, 255)
    hot = onehot(lo, 256)
    hi8 = jnp.broadcast_to(hi, (SUB, span))
    own = iota((blocks, span), 0) == hi
    left = []
    for values, extra in zip(split2(eight), split2(ninth)):
        left.append(spread(values, hi8, blocks))
        left.append(jnp.where(own, jnp.broadcast_to(extra, own.shape), 0.0))
    left = jnp.concatenate(left, axis=0).astype(BF16)
    both = lax.dot_general(left, hot, NT, preferred_element_type=F32)
    return both[: blocks * (SUB + 1), :] + both[blocks * (SUB + 1) :, :]


def shade_tile(slot, tile, left_in, chunk_rend, chunk_start, cots, halves):
    count = left_in.shape[1]
    rows = [cots[tile, ch : ch + 1, :] for ch in range(3)]
    ones, twos = zip(*(split2(r) for r in rows))
    basis = stack_rows((basis_rows(256) + [None, None]) * 3, 32)
    back = stack_rows(
        [None] * 6 + [ones[0], ones[1]] + [None] * 6 + [ones[0], ones[1]] + [None] * 6
        + [ones[0], ones[1], ones[2], ones[2], twos[2], twos[0], twos[1]], 32
    )
    right = jnp.concatenate([basis, back], axis=1).astype(BF16)

    inside = [sum(chunk_rend[slot, ch, seg] * rows[ch] for ch in range(3)) for seg in range(2)]
    at8 = iota((SUB, 256), 0)
    later = inside[0] + inside[1]
    later = jnp.where(at8 == SUB - 1, 0.0, pltpu.roll(later, SUB - 1, 0))
    for d in (1, 2, 4):
        later = later + jnp.where(at8 < SUB - d, pltpu.roll(later, SUB - d, 0), 0.0)
    behind = [later + inside[1] + inside[0], later + inside[1]]
    trans = [chunk_start[slot, seg] for seg in range(2)]

    piece = 64
    order = [c // 2 + (c % 2) * (count // piece // 2) for c in range(count // piece)]

    def field_of(c):
        return jnp.dot(left_in[slot, c * piece : (c + 1) * piece, :], right, preferred_element_type=F32)

    ahead = 1
    fields = [field_of(c) for c in order[:ahead]]
    for n, c in enumerate(order):
        if n + ahead < len(order):
            fields.append(field_of(order[n + ahead]))
        seg = 2 * c * piece // count
        field = fields[n]
        alpha = jnp.exp2(field[:, 0:256])
        ratio = alpha / (1.0 - alpha)
        parts = []
        for k in range(piece // SUB):
            span = slice(k * SUB, (k + 1) * SUB)
            weight = trans[seg] * alpha[span]
            trans[seg] = trans[seg] - weight
            shown = weight * field[span, 256:512]
            behind[seg] = behind[seg] - shown
            parts.append((shown - ratio[span] * behind[seg], weight))
        at = slice(c * piece, (c + 1) * piece)
        value = jnp.concatenate([p[0] for p in parts], axis=0)
        one = value.astype(BF16)
        halves[slot, at, 0:256] = one
        halves[slot, at, 256:512] = (value - one.astype(F32)).astype(BF16)
        halves[slot, at, 512:768] = jnp.concatenate([p[1] for p in parts], axis=0).astype(BF16)
        yield


BACK_TURNS = "fss" * 4


def find_moments(slot, tile, cots, halves, grads):
    rows = [cots[tile, ch : ch + 1, :] for ch in range(3)]
    ones, twos = zip(*(split2(r) for r in rows))
    base = stack_rows(basis_rows(256), 16)
    colours = stack_rows([None] * 6 + list(ones) + list(twos), 16)
    kernel = jnp.concatenate([base, base, colours], axis=1).astype(BF16)
    wide = 128
    for n in range(halves.shape[1] // wide):
        at = slice(n * wide, (n + 1) * wide)
        found = lax.dot_general(kernel, halves[slot, at, :], NT, preferred_element_type=F32)
        low = found[8:16, :]
        at16 = iota(low.shape, 0)
        top = found[0:8, :] + jnp.where(at16 >= 6, pltpu.roll(low, 5, 0), 0.0)
        grads[tile, 0:8, at] = top
        grads[tile, 8:9, at] = low[0:1, :] + low[3:4, :]
        yield


def backward_kernel(lists, left_in, grad, chunk_rend, chunk_start, out, cots, halves, grads, slots):
    step = pl.program_id(0)
    steps = pl.num_programs(0)

    @pl.when(step == 0)
    def _():
        for ch in range(3):
            for g in range(cots.shape[0] // SUB):
                for h in range(2):
                    span = slice(h * LANE, (h + 1) * LANE)
                    block = block_transpose(grad[ch, h * SUB : (h + 1) * SUB, g * LANE : (g + 1) * LANE])
                    for t in range(SUB):
                        cots[g * SUB + t, ch : ch + 1, span] = block[t : t + 1, :]

    for slot in range(2):
        tile = 2 * step + slot
        past = jnp.maximum(tile - 1, 0)
        take_turns(
            BACK_TURNS,
            f=find_moments(1 - slot, past, cots, halves, grads),
            s=shade_tile(slot, tile, left_in, chunk_rend, chunk_start, cots, halves),
        )

    @pl.when(step == steps - 1)
    def _():
        for _ in find_moments(1, 2 * step + 1, cots, halves, grads):
            pass
        slots[...] = jnp.zeros_like(slots)
        blocks = slots.shape[0] // (SUB + 1)
        group = 2

        def chunk(c, carry):
            each = [c * group + k for k in range(group)]
            idx = jnp.concatenate([jnp.maximum(lists[t], 0) for t in each], axis=1)
            eight = jnp.concatenate([grads[t, 0:8, :] for t in each], axis=1)
            ninth = jnp.concatenate([grads[t, 8:9, :] for t in each], axis=1)
            slots[...] = slots[...] + scatter_block(eight, ninth, idx, blocks)
            return carry

        lax.fori_loop(0, cots.shape[0] // group, chunk, 0)
        left = iota((SUB, LANE), 1) < 64
        row = iota((SUB, LANE), 0)
        for h in range(blocks):
            for half in range(2):
                span = slice(half * LANE, (half + 1) * LANE)
                acc = slots[h * SUB : (h + 1) * SUB, span]
                extra = jnp.broadcast_to(slots[blocks * SUB + h : blocks * SUB + h + 1, span], (SUB, LANE))
                owner = 4 * h + 2 * half
                out[owner], out[owner + 1] = pack_pair(acc, extra, left, row)


def home_kernel(back, send, centres, conic, rho, opacity, out, total, rows):
    lane = iota((SUB, LANE), 1)
    left = lane < 64
    row = iota((SUB, LANE), 0)
    pairs = back.shape[0] // 2
    per = 8
    blocks = centres.shape[1] // 256
    total[...] = jnp.zeros_like(total)

    def chunk(c, carry):
        eight, ninth = [], []
        for k in range(per):
            i = c * per + k
            values, last = unpack_pair(back[2 * i], back[2 * i + 1], left, row)
            eight.append(values)
            ninth.append(last)
        start = pl.multiple_of(c * per * LANE, per * LANE)
        idx = send[0:1, pl.ds(start, per * LANE)]
        total[...] = total[...] + scatter_block(
            jnp.concatenate(eight, axis=1), jnp.concatenate(ninth, axis=1), idx, blocks
        )
        return carry

    lax.fori_loop(0, pairs // per, chunk, 0)
    for h in range(blocks):
        span = slice(h * 256, (h + 1) * 256)
        rows[0:8, span] = total[h * SUB : (h + 1) * SUB, :]
        rows[8:9, span] = total[blocks * SUB + h : blocks * SUB + h + 1, :]
    m_uu, m_uv, m_vv, m_u, m_v, m_1 = (rows[p : p + 1, :] for p in range(6))
    cx, cy = centres[0:1, :], centres[1:2, :]
    a, c = conic[0:1, :], conic[1:2, :]
    r = rho[...]
    root = jnp.sqrt(a * c)
    b = r * root
    x1, y1 = m_u - cx * m_1, m_v - cy * m_1
    xx = m_uu - cx * (m_u + x1)
    yy = m_vv - cy * (m_v + y1)
    xy = m_uv - cx * m_v - cy * x1
    out[0:1, :] = a * x1 + b * y1
    out[1:2, :] = c * y1 + b * x1
    out[2:3, :] = -0.5 * xx - xy * (0.5 * r * (root / a))
    out[3:4, :] = -0.5 * yy - xy * (0.5 * r * (root / c))
    out[4:5, :] = -xy * root
    out[5:6, :] = m_1 / opacity[...]
    out[6:9, :] = rows[6:9, :]


def struct(*shape, dtype=F32):
    return jax.ShapeDtypeStruct(shape, dtype)


def shards(tile_lists, send_rows, centres, conic, rho, opacity, colors, target):
    devices = lax.axis_size("dev")
    owned = centres.shape[1]
    tiles, count = tile_lists.shape
    height, width = target.shape[1], target.shape[2]
    pixels = height * height
    params = lambda mib: pltpu.CompilerParams(vmem_limit_bytes=mib << 20)
    sources = (send_rows, centres, conic, rho, opacity, colors)
    lists = tile_lists.reshape(tiles, SUB, count // SUB).transpose(0, 2, 1).reshape(tiles, 1, count)
    incoming, t_strips = send_owned(sources, target, 0)
    whole = lambda *shape: pl.BlockSpec(shape, lambda t: (0,) * len(shape))
    per = 2
    per_tile = lambda *shape: pl.BlockSpec((per,) + shape, lambda t: (t,) + (0,) * len(shape))
    hi_blocks = devices * 64 // 256
    image, image_too, head, tail, chunk_rend, chunk_start, left = pl.pallas_call(
        forward_kernel,
        grid=(tiles // per,),
        in_specs=[whole(tiles, 1, count), whole(devices, SUB, LANE)],
        out_specs=[
            whole(3, height, width), whole(3, height, width), whole(RIMS, width), whole(RIMS, width),
            per_tile(3, 2, SUB, pixels), per_tile(2, SUB, pixels), per_tile(count, 32),
        ],
        out_shape=[
            struct(3, height, width),
            struct(3, height, width),
            struct(RIMS, width),
            struct(RIMS, width),
            struct(tiles, 3, 2, SUB, pixels),
            struct(tiles, 2, SUB, pixels),
            struct(tiles, count, 32, dtype=BF16),
        ],
        scratch_shapes=[
            pltpu.VMEM((hi_blocks * SUB, 256), F32),
            pltpu.VMEM((hi_blocks, 256), F32),
            pltpu.VMEM((hi_blocks * (SUB + 1), 2 * 256), BF16),
            pltpu.VMEM((per, count, LANE), F32),
            pltpu.VMEM((per, count, pixels), F32),
            pltpu.VMEM((3, tiles, pixels), F32),
        ],
        compiler_params=params(16),
        name="tile_forward",
    )(lists, incoming)

    pixel_grad = pl.pallas_call(
        loss_kernel,
        out_shape=struct(3, height, width),
        scratch_shapes=[pltpu.VMEM((RIMS, width), F32)] * 2
        + [
            pltpu.VMEM((5, 3 * height, width), F32),
            pltpu.VMEM((3, 2 * height, width), F32),
            pltpu.VMEM((3, 2, 2 * height, width), F32),
        ]
        + [pltpu.SemaphoreType.DMA((8,))] * 2,
        compiler_params=pltpu.CompilerParams(collective_id=1, has_side_effects=True, vmem_limit_bytes=8 << 20),
        name="loss_gradient",
    )(image_too, head, tail, t_strips)

    slot_grads = pl.pallas_call(
        backward_kernel,
        grid=(tiles // per,),
        in_specs=[
            whole(tiles, 1, count), per_tile(count, 32), whole(3, height, width),
            per_tile(3, 2, SUB, pixels), per_tile(2, SUB, pixels),
        ],
        out_specs=whole(devices, SUB, LANE),
        out_shape=struct(devices, SUB, LANE),
        scratch_shapes=[
            pltpu.VMEM((tiles, 3, pixels), F32),
            pltpu.VMEM((per, count, 3 * pixels), BF16),
            pltpu.VMEM((tiles, 16, count), F32),
            pltpu.VMEM((hi_blocks * (SUB + 1), 256), F32),
        ],
        compiler_params=params(20),
        name="tile_backward",
    )(lists, left, pixel_grad, chunk_rend, chunk_start)
    returned = exchange(slot_grads, 2)
    grads = pl.pallas_call(
        home_kernel,
        out_shape=struct(9, owned),
        scratch_shapes=[
            pltpu.VMEM((owned // 256 * (SUB + 1), 256), F32),
            pltpu.VMEM((16, owned), F32),
        ],
        compiler_params=params(16),
        name="owner_scatter",
    )(returned, send_rows, centres, conic, rho, opacity)
    return image, grads


def solution(mesh):
    return jax.shard_map(
        shards,
        mesh=mesh,
        in_specs=(
            P("dev", None),
            P("dev", None),
            P(None, "dev"),
            P(None, "dev"),
            P(None, "dev"),
            P(None, "dev"),
            P(None, "dev"),
            P(None, "dev", None),
        ),
        out_specs=(P(None, "dev", None), P(None, "dev")),
        check_vma=False,
    )
```

```python
import functools
import math

import jax
import jax.numpy as jnp
import numpy as np
from jax import lax
from jax.experimental import pallas as pl
from jax.experimental.pallas import tpu as pltpu
from jax.sharding import PartitionSpec as P

F32 = jnp.float32
BF16 = jnp.bfloat16
LOG2E = math.log2(math.e)
SUB, LANE = 8, 128
DEAD = -10000.0


def lane_pick(table, lanes):
    return jnp.take_along_axis(table, lanes, axis=1, mode="promise_in_bounds")


def iota(shape, dim):
    return lax.broadcasted_iota(jnp.int32, shape, dim)


def sub_sum(x):
    for d in (4, 2, 1):
        x = x + pltpu.roll(x, d, 0)
    return x


def split2(x):
    one = x.astype(BF16).astype(F32)
    return one, x - one


def coefficient_rows(cx, cy, a, c, rho, op):
    b = rho * jnp.sqrt(a * c)
    bx, by = a * cx + b * cy, c * cy + b * cx
    one = jnp.log(op) - 0.5 * (cx * bx + cy * by)
    return [LOG2E * k for k in (-0.5 * a, -b, -0.5 * c, bx, by, one)]


def pick_tree(parts, bits):
    if len(parts) == 1:
        return parts[0]()
    half = len(parts) // 2
    return jnp.where(bits[half], pick_tree(parts[half:], bits), pick_tree(parts[:half], bits))


def pick_nine(table, ninth, idx, row, blocks):
    hi, lo = lax.shift_right_logical(idx, 7), lax.bitwise_and(idx, 127)
    bits = {1 << k: lax.bitwise_and(hi, 1 << k) != 0 for k in range(blocks.bit_length() - 1)}
    eight = pick_tree([lambda h=h: lane_pick(table(h), lo) for h in range(blocks)], bits)
    coarse = {k // SUB: v for k, v in bits.items() if k >= SUB}
    last = pick_tree(
        [lambda v=v: lane_pick(ninth[v * SUB : (v + 1) * SUB, :], lo) for v in range(blocks // SUB)], coarse
    )
    return eight, sub_sum(jnp.where(lax.bitwise_and(hi, 7) == row, last, 0.0))


MESH = pl.DeviceIdType.MESH
USED = 5
GROUP = 8
RIM = 10
RIMS = 32


def pack_pair(eight, last, left, row):
    low = pltpu.roll(eight, 4, 0)
    even = jnp.where(left, eight, pltpu.roll(low, 64, 1))
    odd = jnp.where(left, pltpu.roll(eight, 64, 1), low)
    return jnp.where(row < 4, even, last), jnp.where(row < 4, odd, pltpu.roll(last, 64, 1))


def unpack_pair(even, odd, left, row):
    high = jnp.where(left, even, pltpu.roll(odd, 64, 1))
    low = jnp.where(left, pltpu.roll(even, 64, 1), odd)
    return jnp.where(row < 4, high, pltpu.roll(low, 4, 0)), high[4:5, :]


def greet_all(n, me):
    barrier = pltpu.get_barrier_semaphore()

    def greet(k, carry):
        pl.semaphore_signal(barrier, inc=1, device_id=(lax.rem(me + k, n),), device_id_type=MESH)
        return carry

    lax.fori_loop(1, n, greet, 0)
    return barrier


def halo_copies(n, me, strip, before, after, send_sem, recv_sem):
    return [
        pltpu.make_async_remote_copy(
            src_ref=strip, dst_ref=to, send_sem=send_sem.at[k], recv_sem=recv_sem.at[k],
            device_id=(lax.rem(me + hop, n),), device_id_type=MESH,
        )
        for k, (hop, to) in enumerate(((1, before), (n - 1, after)))
    ]


def send_owned_kernel(*refs):
    sources, strip, (out, strips), x, table, ninth = refs[:6], refs[6], refs[7:9], *refs[9:12]
    places, (local_sem, send_sem, recv_sem, halo_send, halo_recv) = refs[12:18], refs[18:23]
    me = lax.axis_index("dev")
    n = lax.axis_size("dev")
    fetched = [pltpu.make_async_copy(a, b, local_sem.at[k]) for k, (a, b) in enumerate(zip(sources, places))]
    for copy in fetched:
        copy.start()
    barrier = greet_all(n, me)
    for copy in fetched:
        copy.wait()
    send, centres, conic, rho, opacity, colors = places
    rows = coefficient_rows(
        centres[0:1, :], centres[1:2, :], conic[0:1, :], conic[1:2, :], rho[...], opacity[...]
    )
    for p, value in enumerate(rows + [colors[0:1, :], colors[1:2, :]]):
        table[p : p + 1, :] = value
    blocks = table.shape[1] // LANE
    for h in range(blocks):
        ninth[h : h + 1, :] = colors[2:3, h * LANE : (h + 1) * LANE]
    left = iota((SUB, LANE), 1) < 64
    row = iota((SUB, LANE), 0)
    pairs = n // 2
    mine = me // 2
    used = pl.ds(0, USED)
    step = 4

    def fill(group):
        for k in range(step):
            i = lax.rem(mine + group * step + k, pairs)
            start = pl.multiple_of(i * LANE, LANE)
            idx = jnp.broadcast_to(jnp.maximum(send[0:1, pl.ds(start, LANE)], 0), (SUB, LANE))
            eight, last = pick_nine(lambda h: table[:, h * LANE : (h + 1) * LANE], ninth, idx, row, blocks)
            x[2 * i], x[2 * i + 1] = pack_pair(eight, last, left, row)

    def ship(k):
        for core in range(2):
            peer = 2 * lax.rem(mine + k, pairs) + core
            pltpu.make_async_remote_copy(
                src_ref=x.at[peer, used], dst_ref=out.at[me, used], send_sem=send_sem, recv_sem=recv_sem,
                device_id=(peer,), device_id_type=MESH,
            ).start()

    copies = halo_copies(n, me, strip, strips.at[0], strips.at[2], halo_send, halo_recv)
    copies.append(pltpu.make_async_copy(strip, strips.at[1], halo_recv.at[2]))
    early = 5

    def first(group, carry):
        fill(group)
        return carry

    lax.fori_loop(0, early, first, 0)
    pl.semaphore_wait(barrier, n - 1)
    for copy in copies:
        copy.start()
    partner = me + 1 - 2 * lax.rem(me, 2)
    own = pltpu.make_async_copy(x.at[me, used], out.at[me, used], local_sem.at[6])
    own.start()
    pltpu.make_async_remote_copy(
        src_ref=x.at[partner, used], dst_ref=out.at[me, used], send_sem=send_sem, recv_sem=recv_sem,
        device_id=(partner,), device_id_type=MESH,
    ).start()

    def ship_one(k, carry):
        ship(k)
        return carry

    lax.fori_loop(1, (early - 1) * step, ship_one, 0)

    def both(group, carry):
        for k in range(step):
            ship((group - 1) * step + k)
        fill(group)
        return carry

    lax.fori_loop(early, pairs // step, both, 0)
    lax.fori_loop(pairs - step, pairs, ship_one, 0)
    own.wait()
    rest = pl.ds(0, n - 1)
    pltpu.make_async_copy(x.at[rest, used], x.at[rest, used], send_sem).wait()
    pltpu.make_async_copy(out.at[rest, used], out.at[rest, used], recv_sem).wait()
    for copy in copies:
        copy.wait()


def send_owned(sources, strip, number):
    devices, owned = lax.axis_size("dev"), sources[1].shape[1]
    vmem, hbm = pl.BlockSpec(memory_space=pltpu.VMEM), pl.BlockSpec(memory_space=pltpu.HBM)
    return pl.pallas_call(
        send_owned_kernel,
        out_shape=[struct(devices, SUB, LANE), struct(3, *strip.shape)],
        in_specs=[hbm] * 7,
        out_specs=[hbm] * 2,
        scratch_shapes=[
            pltpu.VMEM((devices, SUB, LANE), F32),
            pltpu.VMEM((SUB, owned), F32),
            pltpu.VMEM((owned // LANE, LANE), F32),
        ]
        + [pltpu.VMEM(v.shape, v.dtype) for v in sources]
        + [pltpu.SemaphoreType.DMA((7,))]
        + [pltpu.SemaphoreType.DMA] * 2
        + [pltpu.SemaphoreType.DMA((3,))] * 2,
        compiler_params=pltpu.CompilerParams(
            collective_id=number, has_side_effects=True, vmem_limit_bytes=60 * 1024 * 1024
        ),
        name="owner_send",
    )(*sources, strip)


def block_transpose(x):
    row = iota(x.shape, 0)
    block = lax.shift_right_logical(iota(x.shape, 1), 4)
    for d in (1, 2, 4):
        low_row = lax.bitwise_and(row, d) == 0
        low_block = lax.bitwise_and(block, d) == 0
        down = pltpu.roll(pltpu.roll(x, SUB - d, 0), 16 * d, 1)
        back = pltpu.roll(pltpu.roll(x, d, 0), LANE - 16 * d, 1)
        x = jnp.where(low_row == low_block, x, jnp.where(low_row, down, back))
    return x


def basis_rows(lanes):
    pixel = iota((1, lanes), 1)
    v = lax.shift_right_logical(pixel, 4).astype(F32) - 7.5
    u = lax.bitwise_and(pixel, 15).astype(F32) - 7.5
    return [u * u, u * v, v * v, u, v, jnp.ones_like(u)]


def stack_rows(rows, count):
    shape = (count, next(r for r in rows if r is not None).shape[1])
    at = iota(shape, 0)
    result = jnp.zeros(shape, F32)
    for p, row in enumerate(rows):
        if row is not None:
            result = jnp.where(at == p, jnp.broadcast_to(row, shape), result)
    return result


def scan_sub(x):
    at = iota(x.shape, 0)
    x = jnp.where(at == 0, 1.0, pltpu.roll(x, 1, 0))
    for d in (1, 2, 4):
        x = x * jnp.where(at >= d, pltpu.roll(x, d, 0), 1.0)
    return x


def take_turns(order, **workers):
    for name in order:
        next(workers[name], None)
    for worker in workers.values():
        for _ in worker:
            pass


def segments(count):
    groups = count // SUB // 2
    return [(seg, j, (seg * groups + j) * SUB) for j in range(groups) for seg in range(2)]


def split3(x):
    one, rest = split2(x)
    two, three = split2(rest)
    return one, two, three


def gather_columns(raw, flat, cols, slot):
    count = raw.shape[1]
    blocks = flat.shape[0] // (SUB + 1)
    row = iota((SUB, LANE), 0)
    wide = 2 * LANE
    founds = []
    for n in range(count // wide):
        idx = jnp.maximum(raw[:, n * wide : (n + 1) * wide], 0)
        hi, lo = lax.shift_right_logical(idx, 8), lax.bitwise_and(idx, 255)
        hot = onehot(lo, 256)
        found = jnp.dot(flat[...], jnp.concatenate([hot] * 2, axis=0), preferred_element_type=F32)
        founds.append((hi, found))
        yield
    for q in range(count // LANE):
        hi, found = founds[q // 2]
        span = slice((q % 2) * LANE, (q % 2 + 1) * LANE)
        out = slice(q * LANE, (q + 1) * LANE)
        hq = jnp.broadcast_to(hi[:, span], (SUB, LANE))
        bits = {1 << k: lax.bitwise_and(hq, 1 << k) != 0 for k in range(blocks.bit_length() - 1)}
        acc = pick_tree([lambda h=h: found[h * SUB : (h + 1) * SUB, span] for h in range(blocks)], bits)
        coarse = {k // SUB: v for k, v in bits.items() if k >= SUB}
        base = blocks * SUB
        last = pick_tree(
            [lambda v=v: found[base + v * SUB : base + (v + 1) * SUB, span] for v in range(blocks // SUB)], coarse
        )
        last = sub_sum(jnp.where(lax.bitwise_and(hq, 7) == row, last, 0.0))
        yield
        acc = jnp.where((row == 5) & (jnp.broadcast_to(raw[:, out], (SUB, LANE)) < 0), DEAD, acc)
        one, two, three = split3(acc)
        b_one, b_two = split2(last)
        more = jnp.where(row == 1, b_two, jnp.where(row == 7, last, b_one))
        more = jnp.where((row == 3) | (row == 4), pltpu.roll(one, 5, 0), more)
        more = jnp.where((row == 5) | (row == 6), pltpu.roll(acc, 7, 0), more)
        stack = jnp.concatenate([one, two, three, more], axis=0)
        cols[slot, out, :] = jnp.concatenate([stack, jnp.zeros((LANE - 32, LANE), F32)], axis=0).T
        yield


TURNS = "d" * 8 + "g" + "d" * 6 + "g" + "d" * 2 + "gg" + "d" * 2 + "gg" + "d" * 2 + "gg" + "d" * 4 + "gg"


def draw_tile(slot, tile, basis, chunk_rend, chunk_start, left_out, cols, alphas, rends):
    count = cols.shape[1]
    ones = jnp.ones((SUB, 256), F32)
    product = [ones, ones]
    piece = 64
    for c in range(count // piece):
        span = slice(c * piece, (c + 1) * piece)
        left = cols[slot, span, 0:32].astype(BF16)
        left_out[slot, span, :] = left
        alpha = jnp.exp2(jnp.dot(left, basis, preferred_element_type=F32))
        alphas[slot, span, :] = alpha
        rest = 1.0 - alpha
        parts = [rest[k * SUB : (k + 1) * SUB, :] for k in range(piece // SUB)]
        while len(parts) > 1:
            parts = [parts[k] * parts[k + 1] for k in range(0, len(parts), 2)]
        seg = 2 * c * piece // count
        product[seg] = product[seg] * parts[0]
        yield

    begin = scan_sub(product[0] * product[1])
    trans = [begin, begin * product[0]]
    zero = jnp.zeros((SUB, 256), F32)
    sums = [[zero] * 3, [zero] * 3]
    for seg in range(2):
        chunk_start[slot, seg] = trans[seg]
    for seg, j, at in segments(count):
        weight = trans[seg] * alphas[slot, at : at + SUB, :]
        trans[seg] = trans[seg] - weight
        color = cols[slot, at : at + SUB, :]
        sums[seg] = [t + weight * color[:, 29 + ch : 30 + ch] for ch, t in enumerate(sums[seg])]
        if seg == 1 and j % 2 == 1:
            yield
    for ch in range(3):
        for seg in range(2):
            chunk_rend[slot, ch, seg] = sums[seg][ch]
        rends[ch, pl.ds(tile, 1), :] = sub_sum(sums[0][ch] + sums[1][ch])[0:1, :]


def forward_kernel(
    lists, recv, target, image, grad, chunk_rend, chunk_start, left_out, pieces, ninth, flat, cols, alphas, rends,
    image_too, head, tail, *loss_refs
):
    step = pl.program_id(0)
    me = lax.axis_index("dev")
    n = lax.axis_size("dev")

    @pl.when(step == 0)
    def _():
        greet_sides(me, n)

    row = iota((SUB, LANE), 0)

    @pl.when(step == 0)
    def _():
        blocks = pieces.shape[0] // SUB
        left = iota((SUB, LANE), 1) < 64

        def block(h, carry):
            lasts = []
            for half in range(2):
                owner = 4 * h + 2 * half
                eight, last = unpack_pair(recv[owner], recv[owner + 1], left, row)
                pieces[pl.ds(pl.multiple_of(h * SUB, SUB), SUB), half * LANE : (half + 1) * LANE] = eight
                lasts.append(last)
            ninth[pl.ds(h, 1), :] = jnp.concatenate(lasts, axis=1)
            return carry

        lax.fori_loop(0, blocks, block, 0)
        for rows, source in ((slice(0, blocks * SUB), pieces), (slice(blocks * SUB, None), ninth)):
            for k, part in enumerate(split2(source[...])):
                flat[rows, k * 256 : (k + 1) * 256] = part.astype(BF16)
        for _ in gather_columns(lists[0], flat, cols, 0):
            pass

    basis = stack_rows((basis_rows(256) + [None, None]) * 3, 32).astype(BF16)
    for slot in range(2):
        tile = 2 * step + slot
        later = jnp.minimum(tile + 1, lists.shape[0] - 1)
        take_turns(
            TURNS,
            g=gather_columns(lists[later], flat, cols, 1 - slot),
            d=draw_tile(slot, tile, basis, chunk_rend, chunk_start, left_out, cols, alphas, rends),
        )

    @pl.when(step == pl.num_programs(0) - 1)
    def _():
        for ch in range(3):
            for g in range(rends.shape[1] // SUB):
                for h in range(2):
                    block = block_transpose(rends[ch, g * SUB : (g + 1) * SUB, h * LANE : (h + 1) * LANE])
                    span = slice(g * LANE, (g + 1) * LANE)
                    for to in (image, image_too):
                        to[ch, h * SUB : (h + 1) * SUB, span] = block
                    at = RIM * ch
                    if h == 0:
                        head[at : at + SUB, span] = block
                        tail[at : at + 2, span] = block[6:8, :]
                    else:
                        head[at + SUB : at + RIM, span] = block[0:2, :]
                        tail[at + 2 : at + RIM, span] = block
        loss_gradient(me, n, image_too, head, tail, target, grad, *loss_refs)


def taps_of():
    offsets = np.arange(11, dtype=np.float32) - np.float32(5)
    taps = np.exp(-offsets * offsets / np.float32(4.5)).astype(np.float32)
    return [float(t) for t in taps / taps.sum(dtype=np.float32)]


TAPS = taps_of()


def blur_rows(read, start, count):
    total = TAPS[5] * read(start, count)
    for m in range(1, 6):
        total = total + TAPS[5 + m] * (read(start - m, count) + read(start + m, count))
    return total


def blur_lanes(x):
    rows, width = x.shape
    pad = jnp.zeros((rows, LANE), F32)
    wide = jnp.concatenate([x, pad], axis=1)
    total = TAPS[5] * x
    for m in range(1, 6):
        both = pltpu.roll(wide, m, 1) + pltpu.roll(wide, width + LANE - m, 1)
        total = total + TAPS[5 + m] * both[:, :width]
    return total


def rim_copies(me, n, head, tail, before, after, send_sem, recv_sem):
    sides = []
    for k, (hop, source, to) in enumerate(((1, tail, before), (n - 1, head, after))):
        side = []
        for part in range(RIMS // SUB):
            rows = pl.ds(part * SUB, SUB)
            side.append(
                pltpu.make_async_remote_copy(
                    src_ref=source.at[rows], dst_ref=to.at[rows],
                    send_sem=send_sem.at[2 * part + k], recv_sem=recv_sem.at[2 * part + k],
                    device_id=(lax.rem(me + hop, n),), device_id_type=MESH,
                )
            )
        sides.append(side)
    return sides


def greet_sides(me, n):
    barrier = pltpu.get_barrier_semaphore()
    for there, hop in ((me < n - 1, 1), (me > 0, n - 1)):
        @pl.when(there)
        def _():
            pl.semaphore_signal(barrier, inc=1, device_id=(lax.rem(me + hop, n),), device_id_type=MESH)


def meet_sides(me, n):
    sides = 2 - jnp.where(me == 0, 1, 0) - jnp.where(me == n - 1, 1, 0)
    pl.semaphore_wait(pltpu.get_barrier_semaphore(), sides)


def loss_gradient(
    me, n, centre, head, tail, target, grad, before, after, pads, maps, blurred, send_sem, recv_sem
):
    height, width = centre.shape[1:]
    rim = RIM
    up, down = rim_copies(me, n, head, tail, before, after, send_sem, recv_sem)
    meet_sides(me, n)
    for there, side in ((me < n - 1, up), (me > 0, down)):
        @pl.when(there)
        def _():
            for copy in side:
                copy.start()
    t_before, t_centre, t_after = target.at[0], target.at[1], target.at[2]
    at = iota((2 * height, width), 0) - height // 2 + me * height
    inside = (at >= 0) & (at < n * height)

    def wide_blur(k):
        vertical = blur_rows(lambda s, c: pads[k, s : s + c, :], height // 2, 2 * height)
        return blur_lanes(vertical)

    edge = height - rim
    for k in range(5):
        pads[k, 0:edge, :] = jnp.zeros((edge, width), F32)
        pads[k, 3 * height - edge :, :] = jnp.zeros((edge, width), F32)
    for ch in range(3):
        first = jnp.where(me > 0, t_before[ch, edge:height, :], 0.0)
        last = jnp.where(me < n - 1, t_after[ch, 0:rim, :], 0.0)
        for rows, tt in (
            (slice(edge, height), first), (slice(height, 2 * height), t_centre[ch]),
            (slice(2 * height, 2 * height + rim), last),
        ):
            pads[1, rows, :] = tt
            pads[3, rows, :] = tt * tt
        blurred[ch, 0] = wide_blur(1)
        blurred[ch, 1] = wide_blur(3)

    for ch in range(3):
        parts = slice(0, 2) if ch == 0 else slice(ch + 1, ch + 2)
        for there, side in ((me > 0, up[parts]), (me < n - 1, down[parts])):
            @pl.when(there)
            def _():
                for copy in side:
                    copy.wait_recv()

        for rows, keep, r, t in (
            (slice(edge, height), me > 0, before[rim * ch : rim * (ch + 1), :], t_before[ch, edge:height, :]),
            (slice(height, 2 * height), None, centre[ch], t_centre[ch]),
            (slice(2 * height, 2 * height + rim), me < n - 1, after[rim * ch : rim * (ch + 1), :], t_after[ch, 0:rim, :]),
        ):
            if keep is not None:
                r, t = jnp.where(keep, r, 0.0), jnp.where(keep, t, 0.0)
            pads[0, rows, :] = r
            pads[2, rows, :] = r * r
            pads[4, rows, :] = r * t
        mr, rr, rt = wide_blur(0), wide_blur(2), wide_blur(4)
        mt, tt = blurred[ch, 0], blurred[ch, 1]
        cv = rt - mr * mt
        top1 = 2.0 * mr * mt + 0.0001
        top2 = 2.0 * cv + 0.0009
        low1 = mr * mr + mt * mt + 0.0001
        low2 = (rr - mr * mr) + (tt - mt * mt) + 0.0009
        inv1, inv2 = 1.0 / low1, 1.0 / low2
        both = inv1 * inv2
        ssim = top1 * top2 * both
        d_rr = -ssim * inv2
        d_rt = 2.0 * top1 * both
        d_mr = 2.0 * (mt * (top2 - top1) * both + mr * ssim * (inv2 - inv1))
        for k, value in enumerate((d_mr, d_rr, d_rt)):
            maps[k] = jnp.where(inside, value, 0.0)

        def back_blur(k):
            vertical = blur_rows(lambda s, c: maps[k, s : s + c, :], height // 2, height)
            return blur_lanes(vertical)

        g_mr, g_rr, g_rt = (back_blur(k) for k in range(3))
        r, t = centre[ch], t_centre[ch]
        grad[ch] = 1.6 * (r - t) - 0.2 * (g_mr + 2.0 * r * g_rr + t * g_rt)
    for there, side in ((me < n - 1, up), (me > 0, down)):
        @pl.when(there)
        def _():
            for copy in side:
                copy.wait_send()


NT = (((1,), (1,)), ((), ()))


def onehot(lo, rows):
    return jnp.where(iota((rows, lo.shape[1]), 0) == lo, 1.0, 0.0).astype(BF16)


def spread(values, hi, blocks):
    masked = [jnp.where(hi == h, values, 0.0) for h in range(blocks)]
    return jnp.concatenate(masked, axis=0)


def scatter_block(eight, ninth, idx, blocks):
    span = idx.shape[1]
    hi, lo = lax.shift_right_arithmetic(idx, 8), lax.bitwise_and(idx, 255)
    hot = onehot(lo, 256)
    hi8 = jnp.broadcast_to(hi, (SUB, span))
    own = iota((blocks, span), 0) == hi
    left = []
    for values, extra in zip(split2(eight), split2(ninth)):
        left.append(spread(values, hi8, blocks))
        left.append(jnp.where(own, jnp.broadcast_to(extra, own.shape), 0.0))
    left = jnp.concatenate(left, axis=0).astype(BF16)
    both = lax.dot_general(left, hot, NT, preferred_element_type=F32)
    return both[: blocks * (SUB + 1), :] + both[blocks * (SUB + 1) :, :]


def shade_tile(slot, tile, left_in, chunk_rend, chunk_start, cots, halves):
    count = left_in.shape[1]
    rows = [cots[tile, ch : ch + 1, :] for ch in range(3)]
    ones, twos = zip(*(split2(r) for r in rows))
    basis = stack_rows((basis_rows(256) + [None, None]) * 3, 32)
    back = stack_rows(
        [None] * 6 + [ones[0], ones[1]] + [None] * 6 + [ones[0], ones[1]] + [None] * 6
        + [ones[0], ones[1], ones[2], ones[2], twos[2], twos[0], twos[1]], 32
    )
    right = jnp.concatenate([basis, back], axis=1).astype(BF16)

    inside = [sum(chunk_rend[slot, ch, seg] * rows[ch] for ch in range(3)) for seg in range(2)]
    at8 = iota((SUB, 256), 0)
    later = inside[0] + inside[1]
    later = jnp.where(at8 == SUB - 1, 0.0, pltpu.roll(later, SUB - 1, 0))
    for d in (1, 2, 4):
        later = later + jnp.where(at8 < SUB - d, pltpu.roll(later, SUB - d, 0), 0.0)
    behind = [later + inside[1] + inside[0], later + inside[1]]
    trans = [chunk_start[slot, seg] for seg in range(2)]

    piece = 64
    order = [c // 2 + (c % 2) * (count // piece // 2) for c in range(count // piece)]

    def field_of(c):
        return jnp.dot(left_in[slot, c * piece : (c + 1) * piece, :], right, preferred_element_type=F32)

    ahead = 1
    fields = [field_of(c) for c in order[:ahead]]
    for n, c in enumerate(order):
        if n + ahead < len(order):
            fields.append(field_of(order[n + ahead]))
        seg = 2 * c * piece // count
        field = fields[n]
        alpha = jnp.exp2(field[:, 0:256])
        ratio = alpha / (1.0 - alpha)
        parts = []
        for k in range(piece // SUB):
            span = slice(k * SUB, (k + 1) * SUB)
            weight = trans[seg] * alpha[span]
            trans[seg] = trans[seg] - weight
            shown = weight * field[span, 256:512]
            behind[seg] = behind[seg] - shown
            parts.append((shown - ratio[span] * behind[seg], weight))
        at = slice(c * piece, (c + 1) * piece)
        value = jnp.concatenate([p[0] for p in parts], axis=0)
        one = value.astype(BF16)
        halves[slot, at, 0:256] = one
        halves[slot, at, 256:512] = (value - one.astype(F32)).astype(BF16)
        halves[slot, at, 512:768] = jnp.concatenate([p[1] for p in parts], axis=0).astype(BF16)
        yield


BACK_TURNS = "fss" * 4


def find_moments(slot, tile, cots, halves, grads):
    rows = [cots[tile, ch : ch + 1, :] for ch in range(3)]
    ones, twos = zip(*(split2(r) for r in rows))
    base = stack_rows(basis_rows(256), 16)
    colours = stack_rows([None] * 6 + list(ones) + list(twos), 16)
    kernel = jnp.concatenate([base, base, colours], axis=1).astype(BF16)
    wide = 128
    for n in range(halves.shape[1] // wide):
        at = slice(n * wide, (n + 1) * wide)
        found = lax.dot_general(kernel, halves[slot, at, :], NT, preferred_element_type=F32)
        low = found[8:16, :]
        at16 = iota(low.shape, 0)
        top = found[0:8, :] + jnp.where(at16 >= 6, pltpu.roll(low, 5, 0), 0.0)
        grads[tile, 0:8, at] = top
        grads[tile, 8:9, at] = low[0:1, :] + low[3:4, :]
        yield


def gather_home(me, n, back, send, centres, conic, rho, opacity, out, total, rows, own, recv_sem):
    left = iota((SUB, LANE), 1) < 64
    row = iota((SUB, LANE), 0)
    pairs = n // 2
    mine = me // 2
    blocks = centres.shape[1] // 256
    used = pl.ds(0, USED)
    total[...] = jnp.zeros_like(total)

    def chunk(g, messages):
        arrived = back.at[pl.ds(0, messages), used]
        pltpu.make_async_copy(arrived, arrived, recv_sem.at[g]).wait()
        eight, ninth, idx = [], [], []
        for k in range(GROUP):
            i = lax.rem(mine + pairs - (g * GROUP + k), pairs)
            values, last = unpack_pair(back[2 * i], back[2 * i + 1], left, row)
            eight.append(values)
            ninth.append(last)
            idx.append(send[0:1, pl.ds(pl.multiple_of(i * LANE, LANE), LANE)])
        total[...] = total[...] + scatter_block(
            jnp.concatenate(eight, axis=1), jnp.concatenate(ninth, axis=1), jnp.concatenate(idx, axis=1), blocks
        )

    own.wait()
    chunk(0, 2 * GROUP - 1)

    def later(g, carry):
        chunk(g, 2 * GROUP)
        return carry

    lax.fori_loop(1, pairs // GROUP, later, 0)
    for h in range(blocks):
        span = slice(h * 256, (h + 1) * 256)
        rows[0:8, span] = total[h * SUB : (h + 1) * SUB, :]
        rows[8:9, span] = total[blocks * SUB + h : blocks * SUB + h + 1, :]
    m_uu, m_uv, m_vv, m_u, m_v, m_1 = (rows[p : p + 1, :] for p in range(6))
    cx, cy = centres[0:1, :], centres[1:2, :]
    a, c = conic[0:1, :], conic[1:2, :]
    r = rho[...]
    root = jnp.sqrt(a * c)
    b = r * root
    x1, y1 = m_u - cx * m_1, m_v - cy * m_1
    xx = m_uu - cx * (m_u + x1)
    yy = m_vv - cy * (m_v + y1)
    xy = m_uv - cx * m_v - cy * x1
    out[0:1, :] = a * x1 + b * y1
    out[1:2, :] = c * y1 + b * x1
    out[2:3, :] = -0.5 * xx - xy * (0.5 * r * (root / a))
    out[3:4, :] = -0.5 * yy - xy * (0.5 * r * (root / c))
    out[4:5, :] = -xy * root
    out[5:6, :] = m_1 / opacity[...]
    out[6:9, :] = rows[6:9, :]


def backward_kernel(
    lists, left_in, grad, chunk_rend, chunk_start, send, centres, conic, rho, opacity, result,
    cots, halves, grads, slots, out, back, total, rows, local_sem, send_sem, recv_sem
):
    me = lax.axis_index("dev")
    n = lax.axis_size("dev")
    barrier = pltpu.get_barrier_semaphore()
    each = (n - 1) // (lists.shape[0] // 2)

    def greet(k):
        pl.semaphore_signal(barrier, inc=1, device_id=(lax.rem(me + k, n),), device_id_type=MESH)

    step = pl.program_id(0)
    steps = pl.num_programs(0)

    steps_static = lists.shape[0] // 2

    @pl.when(step == 0)
    def _():
        for k in range(each * steps_static + 1, n):
            greet(k)
        for ch in range(3):
            for g in range(cots.shape[0] // SUB):
                for h in range(2):
                    span = slice(h * LANE, (h + 1) * LANE)
                    block = block_transpose(grad[ch, h * SUB : (h + 1) * SUB, g * LANE : (g + 1) * LANE])
                    for t in range(SUB):
                        cots[g * SUB + t, ch : ch + 1, span] = block[t : t + 1, :]

    for k in range(each):
        greet(step * each + k + 1)
    for slot in range(2):
        tile = 2 * step + slot
        past = jnp.maximum(tile - 1, 0)
        take_turns(
            BACK_TURNS,
            f=find_moments(1 - slot, past, cots, halves, grads),
            s=shade_tile(slot, tile, left_in, chunk_rend, chunk_start, cots, halves),
        )

    @pl.when(step == steps - 1)
    def _():
        for _ in find_moments(1, 2 * step + 1, cots, halves, grads):
            pass
        slots[...] = jnp.zeros_like(slots)
        blocks = slots.shape[0] // (SUB + 1)
        group = 2

        def chunk(c, carry):
            each = [c * group + k for k in range(group)]
            idx = jnp.concatenate([jnp.maximum(lists[t], 0) for t in each], axis=1)
            eight = jnp.concatenate([grads[t, 0:8, :] for t in each], axis=1)
            ninth = jnp.concatenate([grads[t, 8:9, :] for t in each], axis=1)
            slots[...] = slots[...] + scatter_block(eight, ninth, idx, blocks)
            return carry

        lax.fori_loop(0, cots.shape[0] // group, chunk, 0)
        left = iota((SUB, LANE), 1) < 64
        row = iota((SUB, LANE), 0)
        for h in range(blocks):
            for half in range(2):
                span = slice(half * LANE, (half + 1) * LANE)
                acc = slots[h * SUB : (h + 1) * SUB, span]
                extra = jnp.broadcast_to(slots[blocks * SUB + h : blocks * SUB + h + 1, span], (SUB, LANE))
                owner = 4 * h + 2 * half
                out[owner], out[owner + 1] = pack_pair(acc, extra, left, row)
        pl.semaphore_wait(barrier, n - 1)
        used = pl.ds(0, USED)
        own = pltpu.make_async_copy(out.at[me, used], back.at[me, used], local_sem)
        own.start()
        pairs = n // 2
        mine = me // 2

        def ship_to(peer, k):
            pltpu.make_async_remote_copy(
                src_ref=out.at[peer, used], dst_ref=back.at[me, used],
                send_sem=send_sem, recv_sem=recv_sem.at[k // GROUP],
                device_id=(peer,), device_id_type=MESH,
            ).start()

        ship_to(me + 1 - 2 * lax.rem(me, 2), 0)

        def ship(k, carry):
            for core in range(2):
                ship_to(2 * lax.rem(mine + k, pairs) + core, k)
            return carry

        lax.fori_loop(1, pairs, ship, 0)
        gather_home(me, n, back, send, centres, conic, rho, opacity, result, total, rows, own, recv_sem)
        sent = out.at[pl.ds(0, n - 1), used]
        pltpu.make_async_copy(sent, sent, send_sem).wait()


def struct(*shape, dtype=F32):
    return jax.ShapeDtypeStruct(shape, dtype)


def shards(tile_lists, send_rows, centres, conic, rho, opacity, colors, target):
    devices = lax.axis_size("dev")
    owned = centres.shape[1]
    tiles, count = tile_lists.shape
    height, width = target.shape[1], target.shape[2]
    pixels = height * height
    params = lambda mib: pltpu.CompilerParams(vmem_limit_bytes=mib << 20)
    sources = (send_rows, centres, conic, rho, opacity, colors)
    lists = tile_lists.reshape(tiles, SUB, count // SUB).transpose(0, 2, 1).reshape(tiles, 1, count)
    incoming, t_strips = send_owned(sources, target, 0)
    whole = lambda *shape: pl.BlockSpec(shape, lambda t: (0,) * len(shape))
    per = 2
    per_tile = lambda *shape: pl.BlockSpec((per,) + shape, lambda t: (t,) + (0,) * len(shape))
    hi_blocks = devices * 64 // 256
    image, pixel_grad, chunk_rend, chunk_start, left = pl.pallas_call(
        forward_kernel,
        grid=(tiles // per,),
        in_specs=[whole(tiles, 1, count), whole(devices, SUB, LANE), whole(3, 3, height, width)],
        out_specs=[
            whole(3, height, width), whole(3, height, width),
            per_tile(3, 2, SUB, pixels), per_tile(2, SUB, pixels), per_tile(count, 32),
        ],
        out_shape=[
            struct(3, height, width),
            struct(3, height, width),
            struct(tiles, 3, 2, SUB, pixels),
            struct(tiles, 2, SUB, pixels),
            struct(tiles, count, 32, dtype=BF16),
        ],
        scratch_shapes=[
            pltpu.VMEM((hi_blocks * SUB, 256), F32),
            pltpu.VMEM((hi_blocks, 256), F32),
            pltpu.VMEM((hi_blocks * (SUB + 1), 2 * 256), BF16),
            pltpu.VMEM((per, count, LANE), F32),
            pltpu.VMEM((per, count, pixels), F32),
            pltpu.VMEM((3, tiles, pixels), F32),
            pltpu.VMEM((3, height, width), F32),
        ]
        + [pltpu.VMEM((RIMS, width), F32)] * 4
        + [
            pltpu.VMEM((5, 3 * height, width), F32),
            pltpu.VMEM((3, 2 * height, width), F32),
            pltpu.VMEM((3, 2, 2 * height, width), F32),
        ]
        + [pltpu.SemaphoreType.DMA((8,))] * 2,
        compiler_params=pltpu.CompilerParams(collective_id=1, has_side_effects=True, vmem_limit_bytes=20 << 20),
        name="tile_forward",
    )(lists, incoming, t_strips)

    grads = pl.pallas_call(
        backward_kernel,
        grid=(tiles // per,),
        in_specs=[
            whole(tiles, 1, count), per_tile(count, 32), whole(3, height, width),
            per_tile(3, 2, SUB, pixels), per_tile(2, SUB, pixels),
        ]
        + [whole(*v.shape) for v in sources[:5]],
        out_specs=whole(9, owned),
        out_shape=struct(9, owned),
        scratch_shapes=[
            pltpu.VMEM((tiles, 3, pixels), F32),
            pltpu.VMEM((per, count, 3 * pixels), BF16),
            pltpu.VMEM((tiles, 16, count), F32),
            pltpu.VMEM((hi_blocks * (SUB + 1), 256), F32),
            pltpu.VMEM((devices, SUB, LANE), F32),
            pltpu.VMEM((devices, SUB, LANE), F32),
            pltpu.VMEM((owned // 256 * (SUB + 1), 256), F32),
            pltpu.VMEM((16, owned), F32),
            pltpu.SemaphoreType.DMA,
            pltpu.SemaphoreType.DMA,
            pltpu.SemaphoreType.DMA((devices // 2 // GROUP,)),
        ],
        compiler_params=pltpu.CompilerParams(collective_id=2, has_side_effects=True, vmem_limit_bytes=24 << 20),
        name="tile_backward",
    )(lists, left, pixel_grad, chunk_rend, chunk_start, *sources[:5])
    return image, grads


def solution(mesh):
    return jax.shard_map(
        shards,
        mesh=mesh,
        in_specs=(
            P("dev", None),
            P("dev", None),
            P(None, "dev"),
            P(None, "dev"),
            P(None, "dev"),
            P(None, "dev"),
            P(None, "dev"),
            P(None, "dev", None),
        ),
        out_specs=(P(None, "dev", None), P(None, "dev")),
        check_vma=False,
    )
```

```python
import functools
import math

import jax
import jax.numpy as jnp
import numpy as np
from jax import lax
from jax.experimental import pallas as pl
from jax.experimental.pallas import tpu as pltpu
from jax.sharding import PartitionSpec as P

F32 = jnp.float32
BF16 = jnp.bfloat16
LOG2E = math.log2(math.e)
SUB, LANE = 8, 128
DEAD = -10000.0


def lane_pick(table, lanes):
    return jnp.take_along_axis(table, lanes, axis=1, mode="promise_in_bounds")


def iota(shape, dim):
    return lax.broadcasted_iota(jnp.int32, shape, dim)


def sub_sum(x):
    for d in (4, 2, 1):
        x = x + pltpu.roll(x, d, 0)
    return x


def split2(x):
    one = x.astype(BF16).astype(F32)
    return one, x - one


def coefficient_rows(cx, cy, a, c, rho, op):
    b = rho * jnp.sqrt(a * c)
    bx, by = a * cx + b * cy, c * cy + b * cx
    one = jnp.log(op) - 0.5 * (cx * bx + cy * by)
    return [LOG2E * k for k in (-0.5 * a, -b, -0.5 * c, bx, by, one)]


def pick_tree(parts, bits):
    if len(parts) == 1:
        return parts[0]()
    half = len(parts) // 2
    return jnp.where(bits[half], pick_tree(parts[half:], bits), pick_tree(parts[:half], bits))


def pick_nine(table, ninth, idx, row, blocks):
    hi, lo = lax.shift_right_logical(idx, 7), lax.bitwise_and(idx, 127)
    bits = {1 << k: lax.bitwise_and(hi, 1 << k) != 0 for k in range(blocks.bit_length() - 1)}
    eight = pick_tree([lambda h=h: lane_pick(table(h), lo) for h in range(blocks)], bits)
    coarse = {k // SUB: v for k, v in bits.items() if k >= SUB}
    last = pick_tree(
        [lambda v=v: lane_pick(ninth[v * SUB : (v + 1) * SUB, :], lo) for v in range(blocks // SUB)], coarse
    )
    return eight, sub_sum(jnp.where(lax.bitwise_and(hi, 7) == row, last, 0.0))


MESH = pl.DeviceIdType.MESH
USED = 5
GROUP = 8
RIM = 10
RIMS = 32


def pack_pair(eight, last, left, row):
    low = pltpu.roll(eight, 4, 0)
    even = jnp.where(left, eight, pltpu.roll(low, 64, 1))
    odd = jnp.where(left, pltpu.roll(eight, 64, 1), low)
    return jnp.where(row < 4, even, last), jnp.where(row < 4, odd, pltpu.roll(last, 64, 1))


def unpack_pair(even, odd, left, row):
    high = jnp.where(left, even, pltpu.roll(odd, 64, 1))
    low = jnp.where(left, pltpu.roll(even, 64, 1), odd)
    return jnp.where(row < 4, high, pltpu.roll(low, 4, 0)), high[4:5, :]


def greet_all(n, me):
    barrier = pltpu.get_barrier_semaphore()

    def greet(k, carry):
        pl.semaphore_signal(barrier, inc=1, device_id=(lax.rem(me + k, n),), device_id_type=MESH)
        return carry

    lax.fori_loop(1, n, greet, 0)
    return barrier


def halo_copies(n, me, strip, before, after, send_sem, recv_sem):
    return [
        pltpu.make_async_remote_copy(
            src_ref=strip, dst_ref=to, send_sem=send_sem.at[k], recv_sem=recv_sem.at[k],
            device_id=(lax.rem(me + hop, n),), device_id_type=MESH,
        )
        for k, (hop, to) in enumerate(((1, before), (n - 1, after)))
    ]


def send_owned_kernel(*refs):
    sources, strip, (out, strips, lists), x, table, ninth = refs[:7], refs[7], refs[8:11], *refs[11:14]
    places, sorted_lists, (local_sem, send_sem, recv_sem, halo_send, halo_recv) = refs[14:21], refs[21], refs[22:27]
    me = lax.axis_index("dev")
    n = lax.axis_size("dev")
    fetched = [pltpu.make_async_copy(a, b, local_sem.at[k]) for k, (a, b) in enumerate(zip(sources, places))]
    for copy in fetched:
        copy.start()
    barrier = greet_all(n, me)
    for copy in fetched:
        copy.wait()
    send, centres, conic, rho, opacity, colors, raw_lists = places
    rows = coefficient_rows(
        centres[0:1, :], centres[1:2, :], conic[0:1, :], conic[1:2, :], rho[...], opacity[...]
    )
    for p, value in enumerate(rows + [colors[0:1, :], colors[1:2, :]]):
        table[p : p + 1, :] = value
    blocks = table.shape[1] // LANE
    for h in range(blocks):
        ninth[h : h + 1, :] = colors[2:3, h * LANE : (h + 1) * LANE]
    left = iota((SUB, LANE), 1) < 64
    row = iota((SUB, LANE), 0)
    pairs = n // 2
    mine = me // 2
    used = pl.ds(0, USED)
    step = 4

    def fill(group):
        for k in range(step):
            i = lax.rem(mine + group * step + k, pairs)
            start = pl.multiple_of(i * LANE, LANE)
            idx = jnp.broadcast_to(jnp.maximum(send[0:1, pl.ds(start, LANE)], 0), (SUB, LANE))
            eight, last = pick_nine(lambda h: table[:, h * LANE : (h + 1) * LANE], ninth, idx, row, blocks)
            x[2 * i], x[2 * i + 1] = pack_pair(eight, last, left, row)

    def ship(k):
        for core in range(2):
            peer = 2 * lax.rem(mine + k, pairs) + core
            pltpu.make_async_remote_copy(
                src_ref=x.at[peer, used], dst_ref=out.at[me, used], send_sem=send_sem, recv_sem=recv_sem,
                device_id=(peer,), device_id_type=MESH,
            ).start()

    copies = halo_copies(n, me, strip, strips.at[0], strips.at[2], halo_send, halo_recv)
    copies.append(pltpu.make_async_copy(strip, strips.at[1], halo_recv.at[2]))
    early = 5

    def first(group, carry):
        fill(group)
        return carry

    lax.fori_loop(0, early, first, 0)
    pl.semaphore_wait(barrier, n - 1)
    for copy in copies:
        copy.start()
    partner = me + 1 - 2 * lax.rem(me, 2)
    own = pltpu.make_async_copy(x.at[me, used], out.at[me, used], local_sem.at[7])
    own.start()
    pltpu.make_async_remote_copy(
        src_ref=x.at[partner, used], dst_ref=out.at[me, used], send_sem=send_sem, recv_sem=recv_sem,
        device_id=(partner,), device_id_type=MESH,
    ).start()

    def ship_one(k, carry):
        ship(k)
        return carry

    lax.fori_loop(1, (early - 1) * step, ship_one, 0)

    def both(group, carry):
        for k in range(step):
            ship((group - 1) * step + k)
        fill(group)
        return carry

    lax.fori_loop(early, pairs // step, both, 0)
    lax.fori_loop(pairs - step, pairs, ship_one, 0)
    lane = iota((SUB, LANE), 1)
    place = lax.bitwise_and(lane, 7)
    count = raw_lists.shape[1]
    for q in range(count // LANE):
        source = lax.bitwise_and(place, 1) * 64 + (LANE // SUB) * q + lax.shift_right_logical(lane, 3)
        half = lax.shift_right_logical(place, 1)
        for g in range(raw_lists.shape[0] // SUB):
            mixed = jnp.zeros((SUB, LANE), jnp.int32)
            for b in range(count // LANE):
                block = raw_lists[g * SUB : (g + 1) * SUB, b * LANE : (b + 1) * LANE]
                mixed = jnp.where(half == b, lane_pick(block, source), mixed)
            for t in range(SUB):
                sorted_lists[g * SUB + t, :, q * LANE : (q + 1) * LANE] = mixed[t : t + 1, :]
    own.wait()
    rest = pl.ds(0, n - 1)
    pltpu.make_async_copy(x.at[rest, used], x.at[rest, used], send_sem).wait()
    pltpu.make_async_copy(out.at[rest, used], out.at[rest, used], recv_sem).wait()
    keep = pltpu.make_async_copy(sorted_lists, lists, local_sem.at[8])
    keep.start()
    for copy in copies:
        copy.wait()
    keep.wait()


def send_owned(sources, strip, number):
    devices, owned = lax.axis_size("dev"), sources[1].shape[1]
    vmem, hbm = pl.BlockSpec(memory_space=pltpu.VMEM), pl.BlockSpec(memory_space=pltpu.HBM)
    return pl.pallas_call(
        send_owned_kernel,
        out_shape=[
            struct(devices, SUB, LANE),
            struct(3, *strip.shape),
            struct(sources[6].shape[0], 1, sources[6].shape[1], dtype=jnp.int32),
        ],
        in_specs=[hbm] * 8,
        out_specs=[hbm] * 3,
        scratch_shapes=[
            pltpu.VMEM((devices, SUB, LANE), F32),
            pltpu.VMEM((SUB, owned), F32),
            pltpu.VMEM((owned // LANE, LANE), F32),
        ]
        + [pltpu.VMEM(v.shape, v.dtype) for v in sources]
        + [pltpu.VMEM((sources[6].shape[0], 1, sources[6].shape[1]), jnp.int32)]
        + [pltpu.SemaphoreType.DMA((9,))]
        + [pltpu.SemaphoreType.DMA] * 2
        + [pltpu.SemaphoreType.DMA((3,))] * 2,
        compiler_params=pltpu.CompilerParams(
            collective_id=number, has_side_effects=True, vmem_limit_bytes=60 * 1024 * 1024
        ),
        name="owner_send",
    )(*sources, strip)


def block_transpose(x):
    row = iota(x.shape, 0)
    block = lax.shift_right_logical(iota(x.shape, 1), 4)
    for d in (1, 2, 4):
        low_row = lax.bitwise_and(row, d) == 0
        low_block = lax.bitwise_and(block, d) == 0
        down = pltpu.roll(pltpu.roll(x, SUB - d, 0), 16 * d, 1)
        back = pltpu.roll(pltpu.roll(x, d, 0), LANE - 16 * d, 1)
        x = jnp.where(low_row == low_block, x, jnp.where(low_row, down, back))
    return x


def basis_rows(lanes):
    pixel = iota((1, lanes), 1)
    v = lax.shift_right_logical(pixel, 4).astype(F32) - 7.5
    u = lax.bitwise_and(pixel, 15).astype(F32) - 7.5
    return [u * u, u * v, v * v, u, v, jnp.ones_like(u)]


def stack_rows(rows, count):
    shape = (count, next(r for r in rows if r is not None).shape[1])
    at = iota(shape, 0)
    result = jnp.zeros(shape, F32)
    for p, row in enumerate(rows):
        if row is not None:
            result = jnp.where(at == p, jnp.broadcast_to(row, shape), result)
    return result


def scan_sub(x):
    at = iota(x.shape, 0)
    x = jnp.where(at == 0, 1.0, pltpu.roll(x, 1, 0))
    for d in (1, 2, 4):
        x = x * jnp.where(at >= d, pltpu.roll(x, d, 0), 1.0)
    return x


def take_turns(order, **workers):
    for name in order:
        next(workers[name], None)
    for worker in workers.values():
        for _ in worker:
            pass


def segments(count):
    groups = count // SUB // 2
    return [(seg, j, (seg * groups + j) * SUB) for j in range(groups) for seg in range(2)]


def split3(x):
    one, rest = split2(x)
    two, three = split2(rest)
    return one, two, three


def gather_columns(raw, flat, cols, slot):
    count = raw.shape[1]
    blocks = flat.shape[0] // (SUB + 1)
    row = iota((SUB, LANE), 0)
    wide = 2 * LANE
    founds = []
    for n in range(count // wide):
        idx = jnp.maximum(raw[:, n * wide : (n + 1) * wide], 0)
        hi, lo = lax.shift_right_logical(idx, 8), lax.bitwise_and(idx, 255)
        hot = onehot(lo, 256)
        found = jnp.dot(flat[...], jnp.concatenate([hot] * 2, axis=0), preferred_element_type=F32)
        founds.append((hi, found))
        yield
    for q in range(count // LANE):
        hi, found = founds[q // 2]
        span = slice((q % 2) * LANE, (q % 2 + 1) * LANE)
        out = slice(q * LANE, (q + 1) * LANE)
        hq = jnp.broadcast_to(hi[:, span], (SUB, LANE))
        bits = {1 << k: lax.bitwise_and(hq, 1 << k) != 0 for k in range(blocks.bit_length() - 1)}
        acc = pick_tree([lambda h=h: found[h * SUB : (h + 1) * SUB, span] for h in range(blocks)], bits)
        coarse = {k // SUB: v for k, v in bits.items() if k >= SUB}
        base = blocks * SUB
        last = pick_tree(
            [lambda v=v: found[base + v * SUB : base + (v + 1) * SUB, span] for v in range(blocks // SUB)], coarse
        )
        last = sub_sum(jnp.where(lax.bitwise_and(hq, 7) == row, last, 0.0))
        yield
        acc = jnp.where((row == 5) & (jnp.broadcast_to(raw[:, out], (SUB, LANE)) < 0), DEAD, acc)
        one, two, three = split3(acc)
        b_one, b_two = split2(last)
        more = jnp.where(row == 1, b_two, jnp.where(row == 7, last, b_one))
        more = jnp.where((row == 3) | (row == 4), pltpu.roll(one, 5, 0), more)
        more = jnp.where((row == 5) | (row == 6), pltpu.roll(acc, 7, 0), more)
        stack = jnp.concatenate([one, two, three, more], axis=0)
        cols[slot, out, :] = jnp.concatenate([stack, jnp.zeros((LANE - 32, LANE), F32)], axis=0).T
        yield


TURNS = "d" * 8 + "g" + "d" * 6 + "g" + "d" * 2 + "gg" + "d" * 2 + "gg" + "d" * 2 + "gg" + "d" * 4 + "gg"


def draw_tile(slot, tile, basis, chunk_rend, chunk_start, left_out, cols, alphas, rends):
    count = cols.shape[1]
    ones = jnp.ones((SUB, 256), F32)
    product = [ones, ones]
    piece = 64
    for c in range(count // piece):
        span = slice(c * piece, (c + 1) * piece)
        left = cols[slot, span, 0:32].astype(BF16)
        left_out[slot, span, :] = left
        alpha = jnp.exp2(jnp.dot(left, basis, preferred_element_type=F32))
        alphas[slot, span, :] = alpha
        rest = 1.0 - alpha
        parts = [rest[k * SUB : (k + 1) * SUB, :] for k in range(piece // SUB)]
        while len(parts) > 1:
            parts = [parts[k] * parts[k + 1] for k in range(0, len(parts), 2)]
        seg = 2 * c * piece // count
        product[seg] = product[seg] * parts[0]
        yield

    begin = scan_sub(product[0] * product[1])
    trans = [begin, begin * product[0]]
    zero = jnp.zeros((SUB, 256), F32)
    sums = [[zero] * 3, [zero] * 3]
    for seg in range(2):
        chunk_start[slot, seg] = trans[seg]
    for seg, j, at in segments(count):
        weight = trans[seg] * alphas[slot, at : at + SUB, :]
        trans[seg] = trans[seg] - weight
        color = cols[slot, at : at + SUB, :]
        sums[seg] = [t + weight * color[:, 29 + ch : 30 + ch] for ch, t in enumerate(sums[seg])]
        if seg == 1 and j % 2 == 1:
            yield
    for ch in range(3):
        for seg in range(2):
            chunk_rend[slot, ch, seg] = sums[seg][ch]
        rends[ch, pl.ds(tile, 1), :] = sub_sum(sums[0][ch] + sums[1][ch])[0:1, :]


def forward_kernel(
    lists, recv, target, image, grad, chunk_rend, chunk_start, left_out, pieces, ninth, flat, cols, alphas, rends,
    image_too, head, tail, *loss_refs
):
    step = pl.program_id(0)
    me = lax.axis_index("dev")
    n = lax.axis_size("dev")

    @pl.when(step == 0)
    def _():
        greet_sides(me, n)

    row = iota((SUB, LANE), 0)

    @pl.when(step == 0)
    def _():
        blocks = pieces.shape[0] // SUB
        left = iota((SUB, LANE), 1) < 64

        def block(h, carry):
            lasts = []
            for half in range(2):
                owner = 4 * h + 2 * half
                eight, last = unpack_pair(recv[owner], recv[owner + 1], left, row)
                pieces[pl.ds(pl.multiple_of(h * SUB, SUB), SUB), half * LANE : (half + 1) * LANE] = eight
                lasts.append(last)
            ninth[pl.ds(h, 1), :] = jnp.concatenate(lasts, axis=1)
            return carry

        lax.fori_loop(0, blocks, block, 0)
        for rows, source in ((slice(0, blocks * SUB), pieces), (slice(blocks * SUB, None), ninth)):
            for k, part in enumerate(split2(source[...])):
                flat[rows, k * 256 : (k + 1) * 256] = part.astype(BF16)
        for _ in gather_columns(lists[0], flat, cols, 0):
            pass

    basis = stack_rows((basis_rows(256) + [None, None]) * 3, 32).astype(BF16)
    for slot in range(2):
        tile = 2 * step + slot
        later = jnp.minimum(tile + 1, lists.shape[0] - 1)
        take_turns(
            TURNS,
            g=gather_columns(lists[later], flat, cols, 1 - slot),
            d=draw_tile(slot, tile, basis, chunk_rend, chunk_start, left_out, cols, alphas, rends),
        )

    @pl.when(step == pl.num_programs(0) - 1)
    def _():
        for ch in range(3):
            for g in range(rends.shape[1] // SUB):
                for h in range(2):
                    block = block_transpose(rends[ch, g * SUB : (g + 1) * SUB, h * LANE : (h + 1) * LANE])
                    span = slice(g * LANE, (g + 1) * LANE)
                    for to in (image, image_too):
                        to[ch, h * SUB : (h + 1) * SUB, span] = block
                    at = RIM * ch
                    if h == 0:
                        head[at : at + SUB, span] = block
                        tail[at : at + 2, span] = block[6:8, :]
                    else:
                        head[at + SUB : at + RIM, span] = block[0:2, :]
                        tail[at + 2 : at + RIM, span] = block
        loss_gradient(me, n, image_too, head, tail, target, grad, *loss_refs)


def taps_of():
    offsets = np.arange(11, dtype=np.float32) - np.float32(5)
    taps = np.exp(-offsets * offsets / np.float32(4.5)).astype(np.float32)
    return [float(t) for t in taps / taps.sum(dtype=np.float32)]


TAPS = taps_of()


def blur_rows(read, start, count):
    total = TAPS[5] * read(start, count)
    for m in range(1, 6):
        total = total + TAPS[5 + m] * (read(start - m, count) + read(start + m, count))
    return total


def blur_lanes(x):
    rows, width = x.shape
    pad = jnp.zeros((rows, LANE), F32)
    wide = jnp.concatenate([x, pad], axis=1)
    total = TAPS[5] * x
    for m in range(1, 6):
        both = pltpu.roll(wide, m, 1) + pltpu.roll(wide, width + LANE - m, 1)
        total = total + TAPS[5 + m] * both[:, :width]
    return total


def rim_copies(me, n, head, tail, before, after, send_sem, recv_sem):
    sides = []
    for k, (hop, source, to) in enumerate(((1, tail, before), (n - 1, head, after))):
        side = []
        for part in range(RIMS // SUB):
            rows = pl.ds(part * SUB, SUB)
            side.append(
                pltpu.make_async_remote_copy(
                    src_ref=source.at[rows], dst_ref=to.at[rows],
                    send_sem=send_sem.at[2 * part + k], recv_sem=recv_sem.at[2 * part + k],
                    device_id=(lax.rem(me + hop, n),), device_id_type=MESH,
                )
            )
        sides.append(side)
    return sides


def greet_sides(me, n):
    barrier = pltpu.get_barrier_semaphore()
    for there, hop in ((me < n - 1, 1), (me > 0, n - 1)):
        @pl.when(there)
        def _():
            pl.semaphore_signal(barrier, inc=1, device_id=(lax.rem(me + hop, n),), device_id_type=MESH)


def meet_sides(me, n):
    sides = 2 - jnp.where(me == 0, 1, 0) - jnp.where(me == n - 1, 1, 0)
    pl.semaphore_wait(pltpu.get_barrier_semaphore(), sides)


def loss_gradient(
    me, n, centre, head, tail, target, grad, before, after, pads, maps, blurred, send_sem, recv_sem
):
    height, width = centre.shape[1:]
    rim = RIM
    up, down = rim_copies(me, n, head, tail, before, after, send_sem, recv_sem)
    meet_sides(me, n)
    for there, side in ((me < n - 1, up), (me > 0, down)):
        @pl.when(there)
        def _():
            for copy in side:
                copy.start()
    t_before, t_centre, t_after = target.at[0], target.at[1], target.at[2]
    at = iota((2 * height, width), 0) - height // 2 + me * height
    inside = (at >= 0) & (at < n * height)

    def wide_blur(k):
        vertical = blur_rows(lambda s, c: pads[k, s : s + c, :], height // 2, 2 * height)
        return blur_lanes(vertical)

    edge = height - rim
    for k in range(5):
        pads[k, 0:edge, :] = jnp.zeros((edge, width), F32)
        pads[k, 3 * height - edge :, :] = jnp.zeros((edge, width), F32)
    for ch in range(3):
        first = jnp.where(me > 0, t_before[ch, edge:height, :], 0.0)
        last = jnp.where(me < n - 1, t_after[ch, 0:rim, :], 0.0)
        for rows, tt in (
            (slice(edge, height), first), (slice(height, 2 * height), t_centre[ch]),
            (slice(2 * height, 2 * height + rim), last),
        ):
            pads[1, rows, :] = tt
            pads[3, rows, :] = tt * tt
        blurred[ch, 0] = wide_blur(1)
        blurred[ch, 1] = wide_blur(3)

    for ch in range(3):
        parts = slice(0, 2) if ch == 0 else slice(ch + 1, ch + 2)
        for there, side in ((me > 0, up[parts]), (me < n - 1, down[parts])):
            @pl.when(there)
            def _():
                for copy in side:
                    copy.wait_recv()

        for rows, keep, r, t in (
            (slice(edge, height), me > 0, before[rim * ch : rim * (ch + 1), :], t_before[ch, edge:height, :]),
            (slice(height, 2 * height), None, centre[ch], t_centre[ch]),
            (slice(2 * height, 2 * height + rim), me < n - 1, after[rim * ch : rim * (ch + 1), :], t_after[ch, 0:rim, :]),
        ):
            if keep is not None:
                r, t = jnp.where(keep, r, 0.0), jnp.where(keep, t, 0.0)
            pads[0, rows, :] = r
            pads[2, rows, :] = r * r
            pads[4, rows, :] = r * t
        mr, rr, rt = wide_blur(0), wide_blur(2), wide_blur(4)
        mt, tt = blurred[ch, 0], blurred[ch, 1]
        cv = rt - mr * mt
        top1 = 2.0 * mr * mt + 0.0001
        top2 = 2.0 * cv + 0.0009
        low1 = mr * mr + mt * mt + 0.0001
        low2 = (rr - mr * mr) + (tt - mt * mt) + 0.0009
        inv1, inv2 = 1.0 / low1, 1.0 / low2
        both = inv1 * inv2
        ssim = top1 * top2 * both
        d_rr = -ssim * inv2
        d_rt = 2.0 * top1 * both
        d_mr = 2.0 * (mt * (top2 - top1) * both + mr * ssim * (inv2 - inv1))
        for k, value in enumerate((d_mr, d_rr, d_rt)):
            maps[k] = jnp.where(inside, value, 0.0)

        def back_blur(k):
            vertical = blur_rows(lambda s, c: maps[k, s : s + c, :], height // 2, height)
            return blur_lanes(vertical)

        g_mr, g_rr, g_rt = (back_blur(k) for k in range(3))
        r, t = centre[ch], t_centre[ch]
        grad[ch] = 1.6 * (r - t) - 0.2 * (g_mr + 2.0 * r * g_rr + t * g_rt)
    for there, side in ((me < n - 1, up), (me > 0, down)):
        @pl.when(there)
        def _():
            for copy in side:
                copy.wait_send()


NT = (((1,), (1,)), ((), ()))


def onehot(lo, rows):
    return jnp.where(iota((rows, lo.shape[1]), 0) == lo, 1.0, 0.0).astype(BF16)


def spread(values, hi, blocks):
    masked = [jnp.where(hi == h, values, 0.0) for h in range(blocks)]
    return jnp.concatenate(masked, axis=0)


def scatter_block(eight, ninth, idx, blocks):
    span = idx.shape[1]
    hi, lo = lax.shift_right_arithmetic(idx, 8), lax.bitwise_and(idx, 255)
    hot = onehot(lo, 256)
    hi8 = jnp.broadcast_to(hi, (SUB, span))
    own = iota((blocks, span), 0) == hi
    left = []
    for values, extra in zip(split2(eight), split2(ninth)):
        left.append(spread(values, hi8, blocks))
        left.append(jnp.where(own, jnp.broadcast_to(extra, own.shape), 0.0))
    left = jnp.concatenate(left, axis=0).astype(BF16)
    both = lax.dot_general(left, hot, NT, preferred_element_type=F32)
    return both[: blocks * (SUB + 1), :] + both[blocks * (SUB + 1) :, :]


def shade_tile(slot, tile, left_in, chunk_rend, chunk_start, cots, halves):
    count = left_in.shape[1]
    rows = [cots[tile, ch : ch + 1, :] for ch in range(3)]
    ones, twos = zip(*(split2(r) for r in rows))
    basis = stack_rows((basis_rows(256) + [None, None]) * 3, 32)
    back = stack_rows(
        [None] * 6 + [ones[0], ones[1]] + [None] * 6 + [ones[0], ones[1]] + [None] * 6
        + [ones[0], ones[1], ones[2], ones[2], twos[2], twos[0], twos[1]], 32
    )
    right = jnp.concatenate([basis, back], axis=1).astype(BF16)

    inside = [sum(chunk_rend[slot, ch, seg] * rows[ch] for ch in range(3)) for seg in range(2)]
    at8 = iota((SUB, 256), 0)
    later = inside[0] + inside[1]
    later = jnp.where(at8 == SUB - 1, 0.0, pltpu.roll(later, SUB - 1, 0))
    for d in (1, 2, 4):
        later = later + jnp.where(at8 < SUB - d, pltpu.roll(later, SUB - d, 0), 0.0)
    behind = [later + inside[1] + inside[0], later + inside[1]]
    trans = [chunk_start[slot, seg] for seg in range(2)]

    piece = 64
    order = [c // 2 + (c % 2) * (count // piece // 2) for c in range(count // piece)]

    def field_of(c):
        return jnp.dot(left_in[slot, c * piece : (c + 1) * piece, :], right, preferred_element_type=F32)

    ahead = 1
    fields = [field_of(c) for c in order[:ahead]]
    for n, c in enumerate(order):
        if n + ahead < len(order):
            fields.append(field_of(order[n + ahead]))
        seg = 2 * c * piece // count
        field = fields[n]
        alpha = jnp.exp2(field[:, 0:256])
        ratio = alpha / (1.0 - alpha)
        parts = []
        for k in range(piece // SUB):
            span = slice(k * SUB, (k + 1) * SUB)
            weight = trans[seg] * alpha[span]
            trans[seg] = trans[seg] - weight
            shown = weight * field[span, 256:512]
            behind[seg] = behind[seg] - shown
            parts.append((shown - ratio[span] * behind[seg], weight))
        at = slice(c * piece, (c + 1) * piece)
        value = jnp.concatenate([p[0] for p in parts], axis=0)
        one = value.astype(BF16)
        halves[slot, at, 0:256] = one
        halves[slot, at, 256:512] = (value - one.astype(F32)).astype(BF16)
        halves[slot, at, 512:768] = jnp.concatenate([p[1] for p in parts], axis=0).astype(BF16)
        yield


BACK_TURNS = "fss" * 4


def find_moments(slot, tile, cots, halves, grads):
    rows = [cots[tile, ch : ch + 1, :] for ch in range(3)]
    ones, twos = zip(*(split2(r) for r in rows))
    base = stack_rows(basis_rows(256), 16)
    colours = stack_rows([None] * 6 + list(ones) + list(twos), 16)
    kernel = jnp.concatenate([base, base, colours], axis=1).astype(BF16)
    wide = 128
    for n in range(halves.shape[1] // wide):
        at = slice(n * wide, (n + 1) * wide)
        found = lax.dot_general(kernel, halves[slot, at, :], NT, preferred_element_type=F32)
        low = found[8:16, :]
        at16 = iota(low.shape, 0)
        top = found[0:8, :] + jnp.where(at16 >= 6, pltpu.roll(low, 5, 0), 0.0)
        grads[tile, 0:8, at] = top
        grads[tile, 8:9, at] = low[0:1, :] + low[3:4, :]
        yield


def gather_home(me, n, back, send, centres, conic, rho, opacity, out, total, rows, own, recv_sem):
    left = iota((SUB, LANE), 1) < 64
    row = iota((SUB, LANE), 0)
    pairs = n // 2
    mine = me // 2
    blocks = centres.shape[1] // 256
    used = pl.ds(0, USED)
    total[...] = jnp.zeros_like(total)

    def chunk(g, messages):
        arrived = back.at[pl.ds(0, messages), used]
        pltpu.make_async_copy(arrived, arrived, recv_sem.at[g]).wait()
        eight, ninth, idx = [], [], []
        for k in range(GROUP):
            i = lax.rem(mine + pairs - (g * GROUP + k), pairs)
            values, last = unpack_pair(back[2 * i], back[2 * i + 1], left, row)
            eight.append(values)
            ninth.append(last)
            idx.append(send[0:1, pl.ds(pl.multiple_of(i * LANE, LANE), LANE)])
        total[...] = total[...] + scatter_block(
            jnp.concatenate(eight, axis=1), jnp.concatenate(ninth, axis=1), jnp.concatenate(idx, axis=1), blocks
        )

    own.wait()
    chunk(0, 2 * GROUP - 1)

    def later(g, carry):
        chunk(g, 2 * GROUP)
        return carry

    lax.fori_loop(1, pairs // GROUP, later, 0)
    for h in range(blocks):
        span = slice(h * 256, (h + 1) * 256)
        rows[0:8, span] = total[h * SUB : (h + 1) * SUB, :]
        rows[8:9, span] = total[blocks * SUB + h : blocks * SUB + h + 1, :]
    m_uu, m_uv, m_vv, m_u, m_v, m_1 = (rows[p : p + 1, :] for p in range(6))
    cx, cy = centres[0:1, :], centres[1:2, :]
    a, c = conic[0:1, :], conic[1:2, :]
    r = rho[...]
    root = jnp.sqrt(a * c)
    b = r * root
    x1, y1 = m_u - cx * m_1, m_v - cy * m_1
    xx = m_uu - cx * (m_u + x1)
    yy = m_vv - cy * (m_v + y1)
    xy = m_uv - cx * m_v - cy * x1
    out[0:1, :] = a * x1 + b * y1
    out[1:2, :] = c * y1 + b * x1
    out[2:3, :] = -0.5 * xx - xy * (0.5 * r * (root / a))
    out[3:4, :] = -0.5 * yy - xy * (0.5 * r * (root / c))
    out[4:5, :] = -xy * root
    out[5:6, :] = m_1 / opacity[...]
    out[6:9, :] = rows[6:9, :]


def backward_kernel(
    lists, left_in, grad, chunk_rend, chunk_start, send, centres, conic, rho, opacity, result,
    cots, halves, grads, slots, out, back, total, rows, local_sem, send_sem, recv_sem
):
    me = lax.axis_index("dev")
    n = lax.axis_size("dev")
    barrier = pltpu.get_barrier_semaphore()
    each = (n - 1) // (lists.shape[0] // 2)

    def greet(k):
        pl.semaphore_signal(barrier, inc=1, device_id=(lax.rem(me + k, n),), device_id_type=MESH)

    step = pl.program_id(0)
    steps = pl.num_programs(0)

    steps_static = lists.shape[0] // 2

    @pl.when(step == 0)
    def _():
        for k in range(each * steps_static + 1, n):
            greet(k)
        for ch in range(3):
            for g in range(cots.shape[0] // SUB):
                for h in range(2):
                    span = slice(h * LANE, (h + 1) * LANE)
                    block = block_transpose(grad[ch, h * SUB : (h + 1) * SUB, g * LANE : (g + 1) * LANE])
                    for t in range(SUB):
                        cots[g * SUB + t, ch : ch + 1, span] = block[t : t + 1, :]

    for k in range(each):
        greet(step * each + k + 1)
    for slot in range(2):
        tile = 2 * step + slot
        past = jnp.maximum(tile - 1, 0)
        take_turns(
            BACK_TURNS,
            f=find_moments(1 - slot, past, cots, halves, grads),
            s=shade_tile(slot, tile, left_in, chunk_rend, chunk_start, cots, halves),
        )

    @pl.when(step == steps - 1)
    def _():
        for _ in find_moments(1, 2 * step + 1, cots, halves, grads):
            pass
        slots[...] = jnp.zeros_like(slots)
        blocks = slots.shape[0] // (SUB + 1)
        group = 2

        def chunk(c, carry):
            each = [c * group + k for k in range(group)]
            idx = jnp.concatenate([jnp.maximum(lists[t], 0) for t in each], axis=1)
            eight = jnp.concatenate([grads[t, 0:8, :] for t in each], axis=1)
            ninth = jnp.concatenate([grads[t, 8:9, :] for t in each], axis=1)
            slots[...] = slots[...] + scatter_block(eight, ninth, idx, blocks)
            return carry

        lax.fori_loop(0, cots.shape[0] // group, chunk, 0)
        left = iota((SUB, LANE), 1) < 64
        row = iota((SUB, LANE), 0)
        for h in range(blocks):
            for half in range(2):
                span = slice(half * LANE, (half + 1) * LANE)
                acc = slots[h * SUB : (h + 1) * SUB, span]
                extra = jnp.broadcast_to(slots[blocks * SUB + h : blocks * SUB + h + 1, span], (SUB, LANE))
                owner = 4 * h + 2 * half
                out[owner], out[owner + 1] = pack_pair(acc, extra, left, row)
        pl.semaphore_wait(barrier, n - 1)
        used = pl.ds(0, USED)
        own = pltpu.make_async_copy(out.at[me, used], back.at[me, used], local_sem)
        own.start()
        pairs = n // 2
        mine = me // 2

        def ship_to(peer, k):
            pltpu.make_async_remote_copy(
                src_ref=out.at[peer, used], dst_ref=back.at[me, used],
                send_sem=send_sem, recv_sem=recv_sem.at[k // GROUP],
                device_id=(peer,), device_id_type=MESH,
            ).start()

        ship_to(me + 1 - 2 * lax.rem(me, 2), 0)

        def ship(k, carry):
            for core in range(2):
                ship_to(2 * lax.rem(mine + k, pairs) + core, k)
            return carry

        lax.fori_loop(1, pairs, ship, 0)
        gather_home(me, n, back, send, centres, conic, rho, opacity, result, total, rows, own, recv_sem)
        sent = out.at[pl.ds(0, n - 1), used]
        pltpu.make_async_copy(sent, sent, send_sem).wait()


def struct(*shape, dtype=F32):
    return jax.ShapeDtypeStruct(shape, dtype)


def shards(tile_lists, send_rows, centres, conic, rho, opacity, colors, target):
    devices = lax.axis_size("dev")
    owned = centres.shape[1]
    tiles, count = tile_lists.shape
    height, width = target.shape[1], target.shape[2]
    pixels = height * height
    params = lambda mib: pltpu.CompilerParams(vmem_limit_bytes=mib << 20)
    sources = (send_rows, centres, conic, rho, opacity, colors)
    incoming, t_strips, lists = send_owned(sources + (tile_lists,), target, 0)
    whole = lambda *shape: pl.BlockSpec(shape, lambda t: (0,) * len(shape))
    per = 2
    per_tile = lambda *shape: pl.BlockSpec((per,) + shape, lambda t: (t,) + (0,) * len(shape))
    hi_blocks = devices * 64 // 256
    image, pixel_grad, chunk_rend, chunk_start, left = pl.pallas_call(
        forward_kernel,
        grid=(tiles // per,),
        in_specs=[whole(tiles, 1, count), whole(devices, SUB, LANE), whole(3, 3, height, width)],
        out_specs=[
            whole(3, height, width), whole(3, height, width),
            per_tile(3, 2, SUB, pixels), per_tile(2, SUB, pixels), per_tile(count, 32),
        ],
        out_shape=[
            struct(3, height, width),
            struct(3, height, width),
            struct(tiles, 3, 2, SUB, pixels),
            struct(tiles, 2, SUB, pixels),
            struct(tiles, count, 32, dtype=BF16),
        ],
        scratch_shapes=[
            pltpu.VMEM((hi_blocks * SUB, 256), F32),
            pltpu.VMEM((hi_blocks, 256), F32),
            pltpu.VMEM((hi_blocks * (SUB + 1), 2 * 256), BF16),
            pltpu.VMEM((per, count, LANE), F32),
            pltpu.VMEM((per, count, pixels), F32),
            pltpu.VMEM((3, tiles, pixels), F32),
            pltpu.VMEM((3, height, width), F32),
        ]
        + [pltpu.VMEM((RIMS, width), F32)] * 4
        + [
            pltpu.VMEM((5, 3 * height, width), F32),
            pltpu.VMEM((3, 2 * height, width), F32),
            pltpu.VMEM((3, 2, 2 * height, width), F32),
        ]
        + [pltpu.SemaphoreType.DMA((8,))] * 2,
        compiler_params=pltpu.CompilerParams(collective_id=1, has_side_effects=True, vmem_limit_bytes=60 * 1024 * 1024),
        name="tile_forward",
    )(lists, incoming, t_strips)

    grads = pl.pallas_call(
        backward_kernel,
        grid=(tiles // per,),
        in_specs=[
            whole(tiles, 1, count), per_tile(count, 32), whole(3, height, width),
            per_tile(3, 2, SUB, pixels), per_tile(2, SUB, pixels),
        ]
        + [whole(*v.shape) for v in sources[:5]],
        out_specs=whole(9, owned),
        out_shape=struct(9, owned),
        scratch_shapes=[
            pltpu.VMEM((tiles, 3, pixels), F32),
            pltpu.VMEM((per, count, 3 * pixels), BF16),
            pltpu.VMEM((tiles, 16, count), F32),
            pltpu.VMEM((hi_blocks * (SUB + 1), 256), F32),
            pltpu.VMEM((devices, SUB, LANE), F32),
            pltpu.VMEM((devices, SUB, LANE), F32),
            pltpu.VMEM((owned // 256 * (SUB + 1), 256), F32),
            pltpu.VMEM((16, owned), F32),
            pltpu.SemaphoreType.DMA,
            pltpu.SemaphoreType.DMA,
            pltpu.SemaphoreType.DMA((devices // 2 // GROUP,)),
        ],
        compiler_params=pltpu.CompilerParams(collective_id=2, has_side_effects=True, vmem_limit_bytes=60 * 1024 * 1024),
        name="tile_backward",
    )(lists, left, pixel_grad, chunk_rend, chunk_start, *sources[:5])
    return image, grads


def solution(mesh):
    return jax.shard_map(
        shards,
        mesh=mesh,
        in_specs=(
            P("dev", None),
            P("dev", None),
            P(None, "dev"),
            P(None, "dev"),
            P(None, "dev"),
            P(None, "dev"),
            P(None, "dev"),
            P(None, "dev", None),
        ),
        out_specs=(P(None, "dev", None), P(None, "dev")),
        check_vma=False,
    )
```

```python
import functools
import math

import jax
import jax.numpy as jnp
import numpy as np
from jax import lax
from jax.experimental import pallas as pl
from jax.experimental.pallas import tpu as pltpu
from jax.sharding import PartitionSpec as P

F32 = jnp.float32
BF16 = jnp.bfloat16
LOG2E = math.log2(math.e)
SUB, LANE = 8, 128
DEAD = -10000.0


def lane_pick(table, lanes):
    return jnp.take_along_axis(table, lanes, axis=1, mode="promise_in_bounds")


def iota(shape, dim):
    return lax.broadcasted_iota(jnp.int32, shape, dim)


def sub_sum(x):
    for d in (4, 2, 1):
        x = x + pltpu.roll(x, d, 0)
    return x


def split2(x):
    one = x.astype(BF16).astype(F32)
    return one, x - one


def coefficient_rows(cx, cy, a, c, rho, op):
    b = rho * jnp.sqrt(a * c)
    bx, by = a * cx + b * cy, c * cy + b * cx
    one = jnp.log(op) - 0.5 * (cx * bx + cy * by)
    return [LOG2E * k for k in (-0.5 * a, -b, -0.5 * c, bx, by, one)]


def pick_tree(parts, bits):
    if len(parts) == 1:
        return parts[0]()
    half = len(parts) // 2
    return jnp.where(bits[half], pick_tree(parts[half:], bits), pick_tree(parts[:half], bits))


def pick_nine(table, ninth, idx, row, blocks):
    hi, lo = lax.shift_right_logical(idx, 7), lax.bitwise_and(idx, 127)
    bits = {1 << k: lax.bitwise_and(hi, 1 << k) != 0 for k in range(blocks.bit_length() - 1)}
    eight = pick_tree([lambda h=h: lane_pick(table(h), lo) for h in range(blocks)], bits)
    coarse = {k // SUB: v for k, v in bits.items() if k >= SUB}
    last = pick_tree(
        [lambda v=v: lane_pick(ninth[v * SUB : (v + 1) * SUB, :], lo) for v in range(blocks // SUB)], coarse
    )
    return eight, sub_sum(jnp.where(lax.bitwise_and(hi, 7) == row, last, 0.0))


MESH = pl.DeviceIdType.MESH
USED = 5
GROUP = 8
RIM = 10
RIMS = 32


def pack_pair(eight, last, left, row):
    low = pltpu.roll(eight, 4, 0)
    even = jnp.where(left, eight, pltpu.roll(low, 64, 1))
    odd = jnp.where(left, pltpu.roll(eight, 64, 1), low)
    return jnp.where(row < 4, even, last), jnp.where(row < 4, odd, pltpu.roll(last, 64, 1))


def unpack_pair(even, odd, left, row):
    high = jnp.where(left, even, pltpu.roll(odd, 64, 1))
    low = jnp.where(left, pltpu.roll(even, 64, 1), odd)
    return jnp.where(row < 4, high, pltpu.roll(low, 4, 0)), high[4:5, :]


def greet_all(n, me):
    barrier = pltpu.get_barrier_semaphore()

    def greet(k, carry):
        pl.semaphore_signal(barrier, inc=1, device_id=(lax.rem(me + k, n),), device_id_type=MESH)
        return carry

    lax.fori_loop(1, n, greet, 0)
    return barrier


def halo_copies(n, me, strip, before, after, send_sem, recv_sem):
    return [
        pltpu.make_async_remote_copy(
            src_ref=strip, dst_ref=to, send_sem=send_sem.at[k], recv_sem=recv_sem.at[k],
            device_id=(lax.rem(me + hop, n),), device_id_type=MESH,
        )
        for k, (hop, to) in enumerate(((1, before), (n - 1, after)))
    ]


def send_owned(
    me, n, sources, strip, out, strips, x, table, ninth, places, sorted_lists,
    local_sem, send_sem, recv_sem, halo_send, halo_recv
):
    fetched = [pltpu.make_async_copy(a, b, local_sem.at[k]) for k, (a, b) in enumerate(zip(sources, places))]
    for copy in fetched:
        copy.start()
    barrier = greet_all(n, me)
    for copy in fetched:
        copy.wait()
    send, centres, conic, rho, opacity, colors, raw_lists = places
    rows = coefficient_rows(
        centres[0:1, :], centres[1:2, :], conic[0:1, :], conic[1:2, :], rho[...], opacity[...]
    )
    for p, value in enumerate(rows + [colors[0:1, :], colors[1:2, :]]):
        table[p : p + 1, :] = value
    blocks = table.shape[1] // LANE
    for h in range(blocks):
        ninth[h : h + 1, :] = colors[2:3, h * LANE : (h + 1) * LANE]
    left = iota((SUB, LANE), 1) < 64
    row = iota((SUB, LANE), 0)
    pairs = n // 2
    mine = me // 2
    used = pl.ds(0, USED)
    step = 4

    def fill(group):
        for k in range(step):
            i = lax.rem(mine + group * step + k, pairs)
            start = pl.multiple_of(i * LANE, LANE)
            idx = jnp.broadcast_to(jnp.maximum(send[0:1, pl.ds(start, LANE)], 0), (SUB, LANE))
            eight, last = pick_nine(lambda h: table[:, h * LANE : (h + 1) * LANE], ninth, idx, row, blocks)
            x[2 * i], x[2 * i + 1] = pack_pair(eight, last, left, row)

    def ship(k):
        for core in range(2):
            peer = 2 * lax.rem(mine + k, pairs) + core
            pltpu.make_async_remote_copy(
                src_ref=x.at[peer, used], dst_ref=out.at[me, used], send_sem=send_sem, recv_sem=recv_sem,
                device_id=(peer,), device_id_type=MESH,
            ).start()

    copies = halo_copies(n, me, strip, strips.at[0], strips.at[2], halo_send, halo_recv)
    copies.append(pltpu.make_async_copy(strip, strips.at[1], halo_recv.at[2]))
    early = 5

    def first(group, carry):
        fill(group)
        return carry

    lax.fori_loop(0, early, first, 0)
    pl.semaphore_wait(barrier, n - 1)
    for copy in copies:
        copy.start()
    partner = me + 1 - 2 * lax.rem(me, 2)
    own = pltpu.make_async_copy(x.at[me, used], out.at[me, used], local_sem.at[7])
    own.start()
    pltpu.make_async_remote_copy(
        src_ref=x.at[partner, used], dst_ref=out.at[me, used], send_sem=send_sem, recv_sem=recv_sem,
        device_id=(partner,), device_id_type=MESH,
    ).start()

    def ship_one(k, carry):
        ship(k)
        return carry

    lax.fori_loop(1, (early - 1) * step, ship_one, 0)

    def both(group, carry):
        for k in range(step):
            ship((group - 1) * step + k)
        fill(group)
        return carry

    lax.fori_loop(early, pairs // step, both, 0)
    lax.fori_loop(pairs - step, pairs, ship_one, 0)
    lane = iota((SUB, LANE), 1)
    place = lax.bitwise_and(lane, 7)
    count = raw_lists.shape[1]
    for q in range(count // LANE):
        source = lax.bitwise_and(place, 1) * 64 + (LANE // SUB) * q + lax.shift_right_logical(lane, 3)
        half = lax.shift_right_logical(place, 1)
        for g in range(raw_lists.shape[0] // SUB):
            mixed = jnp.zeros((SUB, LANE), jnp.int32)
            for b in range(count // LANE):
                block = raw_lists[g * SUB : (g + 1) * SUB, b * LANE : (b + 1) * LANE]
                mixed = jnp.where(half == b, lane_pick(block, source), mixed)
            for t in range(SUB):
                sorted_lists[g * SUB + t, :, q * LANE : (q + 1) * LANE] = mixed[t : t + 1, :]
    own.wait()
    rest = pl.ds(0, n - 1)
    pltpu.make_async_copy(x.at[rest, used], x.at[rest, used], send_sem).wait()
    pltpu.make_async_copy(out.at[rest, used], out.at[rest, used], recv_sem).wait()
    for copy in copies:
        copy.wait()


def block_transpose(x):
    row = iota(x.shape, 0)
    block = lax.shift_right_logical(iota(x.shape, 1), 4)
    for d in (1, 2, 4):
        low_row = lax.bitwise_and(row, d) == 0
        low_block = lax.bitwise_and(block, d) == 0
        down = pltpu.roll(pltpu.roll(x, SUB - d, 0), 16 * d, 1)
        back = pltpu.roll(pltpu.roll(x, d, 0), LANE - 16 * d, 1)
        x = jnp.where(low_row == low_block, x, jnp.where(low_row, down, back))
    return x


def basis_rows(lanes):
    pixel = iota((1, lanes), 1)
    v = lax.shift_right_logical(pixel, 4).astype(F32) - 7.5
    u = lax.bitwise_and(pixel, 15).astype(F32) - 7.5
    return [u * u, u * v, v * v, u, v, jnp.ones_like(u)]


def stack_rows(rows, count):
    shape = (count, next(r for r in rows if r is not None).shape[1])
    at = iota(shape, 0)
    result = jnp.zeros(shape, F32)
    for p, row in enumerate(rows):
        if row is not None:
            result = jnp.where(at == p, jnp.broadcast_to(row, shape), result)
    return result


def scan_sub(x):
    at = iota(x.shape, 0)
    x = jnp.where(at == 0, 1.0, pltpu.roll(x, 1, 0))
    for d in (1, 2, 4):
        x = x * jnp.where(at >= d, pltpu.roll(x, d, 0), 1.0)
    return x


def take_turns(order, **workers):
    for name in order:
        next(workers[name], None)
    for worker in workers.values():
        for _ in worker:
            pass


def segments(count):
    groups = count // SUB // 2
    return [(seg, j, (seg * groups + j) * SUB) for j in range(groups) for seg in range(2)]


def split3(x):
    one, rest = split2(x)
    two, three = split2(rest)
    return one, two, three


def gather_columns(raw, flat, cols, slot):
    count = raw.shape[1]
    blocks = flat.shape[0] // (SUB + 1)
    row = iota((SUB, LANE), 0)
    wide = 2 * LANE
    founds = []
    for n in range(count // wide):
        idx = jnp.maximum(raw[:, n * wide : (n + 1) * wide], 0)
        hi, lo = lax.shift_right_logical(idx, 8), lax.bitwise_and(idx, 255)
        hot = onehot(lo, 256)
        found = jnp.dot(flat[...], jnp.concatenate([hot] * 2, axis=0), preferred_element_type=F32)
        founds.append((hi, found))
        yield
    for q in range(count // LANE):
        hi, found = founds[q // 2]
        span = slice((q % 2) * LANE, (q % 2 + 1) * LANE)
        out = slice(q * LANE, (q + 1) * LANE)
        hq = jnp.broadcast_to(hi[:, span], (SUB, LANE))
        bits = {1 << k: lax.bitwise_and(hq, 1 << k) != 0 for k in range(blocks.bit_length() - 1)}
        acc = pick_tree([lambda h=h: found[h * SUB : (h + 1) * SUB, span] for h in range(blocks)], bits)
        coarse = {k // SUB: v for k, v in bits.items() if k >= SUB}
        base = blocks * SUB
        last = pick_tree(
            [lambda v=v: found[base + v * SUB : base + (v + 1) * SUB, span] for v in range(blocks // SUB)], coarse
        )
        last = sub_sum(jnp.where(lax.bitwise_and(hq, 7) == row, last, 0.0))
        yield
        acc = jnp.where((row == 5) & (jnp.broadcast_to(raw[:, out], (SUB, LANE)) < 0), DEAD, acc)
        one, two, three = split3(acc)
        b_one, b_two = split2(last)
        more = jnp.where(row == 1, b_two, jnp.where(row == 7, last, b_one))
        more = jnp.where((row == 3) | (row == 4), pltpu.roll(one, 5, 0), more)
        more = jnp.where((row == 5) | (row == 6), pltpu.roll(acc, 7, 0), more)
        stack = jnp.concatenate([one, two, three, more], axis=0)
        cols[slot, out, :] = jnp.concatenate([stack, jnp.zeros((LANE - 32, LANE), F32)], axis=0).T
        yield


TURNS = "d" * 8 + "g" + "d" * 6 + "g" + "d" * 2 + "gg" + "d" * 2 + "gg" + "d" * 2 + "gg" + "d" * 4 + "gg"


def draw_tile(slot, tile, basis, chunk_rend, chunk_start, left_out, cols, alphas, rends):
    count = cols.shape[1]
    ones = jnp.ones((SUB, 256), F32)
    product = [ones, ones]
    piece = 64
    for c in range(count // piece):
        span = slice(c * piece, (c + 1) * piece)
        left = cols[slot, span, 0:32].astype(BF16)
        left_out[slot, span, :] = left
        alpha = jnp.exp2(jnp.dot(left, basis, preferred_element_type=F32))
        alphas[slot, span, :] = alpha
        rest = 1.0 - alpha
        parts = [rest[k * SUB : (k + 1) * SUB, :] for k in range(piece // SUB)]
        while len(parts) > 1:
            parts = [parts[k] * parts[k + 1] for k in range(0, len(parts), 2)]
        seg = 2 * c * piece // count
        product[seg] = product[seg] * parts[0]
        yield

    begin = scan_sub(product[0] * product[1])
    trans = [begin, begin * product[0]]
    zero = jnp.zeros((SUB, 256), F32)
    sums = [[zero] * 3, [zero] * 3]
    for seg in range(2):
        chunk_start[slot, seg] = trans[seg]
    for seg, j, at in segments(count):
        weight = trans[seg] * alphas[slot, at : at + SUB, :]
        trans[seg] = trans[seg] - weight
        color = cols[slot, at : at + SUB, :]
        sums[seg] = [t + weight * color[:, 29 + ch : 30 + ch] for ch, t in enumerate(sums[seg])]
        if seg == 1 and j % 2 == 1:
            yield
    for ch in range(3):
        for seg in range(2):
            chunk_rend[slot, ch, seg] = sums[seg][ch]
        rends[ch, pl.ds(tile, 1), :] = sub_sum(sums[0][ch] + sums[1][ch])[0:1, :]


def forward_kernel(*refs):
    sources, target, image, grad, chunk_rend, chunk_start, left_out, lists_out = refs[:7], *refs[7:14]
    pieces, ninth, flat, cols, alphas, rends, image_too, head, tail, *loss_refs = refs[14:30]
    recv, lists, strips, *send_refs = refs[30:]
    step = pl.program_id(0)
    me = lax.axis_index("dev")
    n = lax.axis_size("dev")

    @pl.when(step == 0)
    def _():
        x, table, own_ninth, *more = send_refs
        send_owned(me, n, sources, target, recv, strips, x, table, own_ninth, more[:7], lists, *more[7:])
        lists_out[...] = lists[...]

    row = iota((SUB, LANE), 0)

    @pl.when(step == 0)
    def _():
        blocks = pieces.shape[0] // SUB
        left = iota((SUB, LANE), 1) < 64

        def block(h, carry):
            lasts = []
            for half in range(2):
                owner = 4 * h + 2 * half
                eight, last = unpack_pair(recv[owner], recv[owner + 1], left, row)
                pieces[pl.ds(pl.multiple_of(h * SUB, SUB), SUB), half * LANE : (half + 1) * LANE] = eight
                lasts.append(last)
            ninth[pl.ds(h, 1), :] = jnp.concatenate(lasts, axis=1)
            return carry

        lax.fori_loop(0, blocks, block, 0)
        for rows, source in ((slice(0, blocks * SUB), pieces), (slice(blocks * SUB, None), ninth)):
            for k, part in enumerate(split2(source[...])):
                flat[rows, k * 256 : (k + 1) * 256] = part.astype(BF16)
        for _ in gather_columns(lists[0], flat, cols, 0):
            pass

    basis = stack_rows((basis_rows(256) + [None, None]) * 3, 32).astype(BF16)
    for slot in range(2):
        tile = 2 * step + slot
        later = jnp.minimum(tile + 1, lists.shape[0] - 1)
        take_turns(
            TURNS,
            g=gather_columns(lists[later], flat, cols, 1 - slot),
            d=draw_tile(slot, tile, basis, chunk_rend, chunk_start, left_out, cols, alphas, rends),
        )

    @pl.when(step == pl.num_programs(0) - 1)
    def _():
        for ch in range(3):
            for g in range(rends.shape[1] // SUB):
                for h in range(2):
                    block = block_transpose(rends[ch, g * SUB : (g + 1) * SUB, h * LANE : (h + 1) * LANE])
                    span = slice(g * LANE, (g + 1) * LANE)
                    for to in (image, image_too):
                        to[ch, h * SUB : (h + 1) * SUB, span] = block
                    at = RIM * ch
                    if h == 0:
                        head[at : at + SUB, span] = block
                        tail[at : at + 2, span] = block[6:8, :]
                    else:
                        head[at + SUB : at + RIM, span] = block[0:2, :]
                        tail[at + 2 : at + RIM, span] = block
        loss_gradient(me, n, image_too, head, tail, strips, grad, *loss_refs)


def taps_of():
    offsets = np.arange(11, dtype=np.float32) - np.float32(5)
    taps = np.exp(-offsets * offsets / np.float32(4.5)).astype(np.float32)
    return [float(t) for t in taps / taps.sum(dtype=np.float32)]


TAPS = taps_of()


def blur_rows(read, start, count):
    total = TAPS[5] * read(start, count)
    for m in range(1, 6):
        total = total + TAPS[5 + m] * (read(start - m, count) + read(start + m, count))
    return total


def blur_lanes(x):
    rows, width = x.shape
    pad = jnp.zeros((rows, LANE), F32)
    wide = jnp.concatenate([x, pad], axis=1)
    total = TAPS[5] * x
    for m in range(1, 6):
        both = pltpu.roll(wide, m, 1) + pltpu.roll(wide, width + LANE - m, 1)
        total = total + TAPS[5 + m] * both[:, :width]
    return total


def rim_copies(me, n, head, tail, before, after, send_sem, recv_sem):
    sides = []
    for k, (hop, source, to) in enumerate(((1, tail, before), (n - 1, head, after))):
        side = []
        for part in range(RIMS // SUB):
            rows = pl.ds(part * SUB, SUB)
            side.append(
                pltpu.make_async_remote_copy(
                    src_ref=source.at[rows], dst_ref=to.at[rows],
                    send_sem=send_sem.at[2 * part + k], recv_sem=recv_sem.at[2 * part + k],
                    device_id=(lax.rem(me + hop, n),), device_id_type=MESH,
                )
            )
        sides.append(side)
    return sides


def loss_gradient(
    me, n, centre, head, tail, target, grad, before, after, pads, maps, blurred, send_sem, recv_sem
):
    height, width = centre.shape[1:]
    rim = RIM
    up, down = rim_copies(me, n, head, tail, before, after, send_sem, recv_sem)
    for there, side in ((me < n - 1, up), (me > 0, down)):
        @pl.when(there)
        def _():
            for copy in side:
                copy.start()
    t_before, t_centre, t_after = target.at[0], target.at[1], target.at[2]
    at = iota((2 * height, width), 0) - height // 2 + me * height
    inside = (at >= 0) & (at < n * height)

    def wide_blur(k):
        vertical = blur_rows(lambda s, c: pads[k, s : s + c, :], height // 2, 2 * height)
        return blur_lanes(vertical)

    edge = height - rim
    for k in range(5):
        pads[k, 0:edge, :] = jnp.zeros((edge, width), F32)
        pads[k, 3 * height - edge :, :] = jnp.zeros((edge, width), F32)
    for ch in range(3):
        first = jnp.where(me > 0, t_before[ch, edge:height, :], 0.0)
        last = jnp.where(me < n - 1, t_after[ch, 0:rim, :], 0.0)
        for rows, tt in (
            (slice(edge, height), first), (slice(height, 2 * height), t_centre[ch]),
            (slice(2 * height, 2 * height + rim), last),
        ):
            pads[1, rows, :] = tt
            pads[3, rows, :] = tt * tt
        blurred[ch, 0] = wide_blur(1)
        blurred[ch, 1] = wide_blur(3)

    for ch in range(3):
        parts = slice(0, 2) if ch == 0 else slice(ch + 1, ch + 2)
        for there, side in ((me > 0, up[parts]), (me < n - 1, down[parts])):
            @pl.when(there)
            def _():
                for copy in side:
                    copy.wait_recv()

        for rows, keep, r, t in (
            (slice(edge, height), me > 0, before[rim * ch : rim * (ch + 1), :], t_before[ch, edge:height, :]),
            (slice(height, 2 * height), None, centre[ch], t_centre[ch]),
            (slice(2 * height, 2 * height + rim), me < n - 1, after[rim * ch : rim * (ch + 1), :], t_after[ch, 0:rim, :]),
        ):
            if keep is not None:
                r, t = jnp.where(keep, r, 0.0), jnp.where(keep, t, 0.0)
            pads[0, rows, :] = r
            pads[2, rows, :] = r * r
            pads[4, rows, :] = r * t
        mr, rr, rt = wide_blur(0), wide_blur(2), wide_blur(4)
        mt, tt = blurred[ch, 0], blurred[ch, 1]
        cv = rt - mr * mt
        top1 = 2.0 * mr * mt + 0.0001
        top2 = 2.0 * cv + 0.0009
        low1 = mr * mr + mt * mt + 0.0001
        low2 = (rr - mr * mr) + (tt - mt * mt) + 0.0009
        inv1, inv2 = 1.0 / low1, 1.0 / low2
        both = inv1 * inv2
        ssim = top1 * top2 * both
        d_rr = -ssim * inv2
        d_rt = 2.0 * top1 * both
        d_mr = 2.0 * (mt * (top2 - top1) * both + mr * ssim * (inv2 - inv1))
        for k, value in enumerate((d_mr, d_rr, d_rt)):
            maps[k] = jnp.where(inside, value, 0.0)

        def back_blur(k):
            vertical = blur_rows(lambda s, c: maps[k, s : s + c, :], height // 2, height)
            return blur_lanes(vertical)

        g_mr, g_rr, g_rt = (back_blur(k) for k in range(3))
        r, t = centre[ch], t_centre[ch]
        grad[ch] = 1.6 * (r - t) - 0.2 * (g_mr + 2.0 * r * g_rr + t * g_rt)
    for there, side in ((me < n - 1, up), (me > 0, down)):
        @pl.when(there)
        def _():
            for copy in side:
                copy.wait_send()


NT = (((1,), (1,)), ((), ()))


def onehot(lo, rows):
    return jnp.where(iota((rows, lo.shape[1]), 0) == lo, 1.0, 0.0).astype(BF16)


def spread(values, hi, blocks):
    masked = [jnp.where(hi == h, values, 0.0) for h in range(blocks)]
    return jnp.concatenate(masked, axis=0)


def scatter_block(eight, ninth, idx, blocks):
    span = idx.shape[1]
    hi, lo = lax.shift_right_arithmetic(idx, 8), lax.bitwise_and(idx, 255)
    hot = onehot(lo, 256)
    hi8 = jnp.broadcast_to(hi, (SUB, span))
    own = iota((blocks, span), 0) == hi
    left = []
    for values, extra in zip(split2(eight), split2(ninth)):
        left.append(spread(values, hi8, blocks))
        left.append(jnp.where(own, jnp.broadcast_to(extra, own.shape), 0.0))
    left = jnp.concatenate(left, axis=0).astype(BF16)
    both = lax.dot_general(left, hot, NT, preferred_element_type=F32)
    return both[: blocks * (SUB + 1), :] + both[blocks * (SUB + 1) :, :]


def shade_tile(slot, tile, left_in, chunk_rend, chunk_start, cots, halves):
    count = left_in.shape[1]
    rows = [cots[tile, ch : ch + 1, :] for ch in range(3)]
    ones, twos = zip(*(split2(r) for r in rows))
    basis = stack_rows((basis_rows(256) + [None, None]) * 3, 32)
    back = stack_rows(
        [None] * 6 + [ones[0], ones[1]] + [None] * 6 + [ones[0], ones[1]] + [None] * 6
        + [ones[0], ones[1], ones[2], ones[2], twos[2], twos[0], twos[1]], 32
    )
    right = jnp.concatenate([basis, back], axis=1).astype(BF16)

    inside = [sum(chunk_rend[slot, ch, seg] * rows[ch] for ch in range(3)) for seg in range(2)]
    at8 = iota((SUB, 256), 0)
    later = inside[0] + inside[1]
    later = jnp.where(at8 == SUB - 1, 0.0, pltpu.roll(later, SUB - 1, 0))
    for d in (1, 2, 4):
        later = later + jnp.where(at8 < SUB - d, pltpu.roll(later, SUB - d, 0), 0.0)
    behind = [later + inside[1] + inside[0], later + inside[1]]
    trans = [chunk_start[slot, seg] for seg in range(2)]

    piece = 64
    order = [c // 2 + (c % 2) * (count // piece // 2) for c in range(count // piece)]

    def field_of(c):
        return jnp.dot(left_in[slot, c * piece : (c + 1) * piece, :], right, preferred_element_type=F32)

    ahead = 1
    fields = [field_of(c) for c in order[:ahead]]
    for n, c in enumerate(order):
        if n + ahead < len(order):
            fields.append(field_of(order[n + ahead]))
        seg = 2 * c * piece // count
        field = fields[n]
        alpha = jnp.exp2(field[:, 0:256])
        ratio = alpha / (1.0 - alpha)
        parts = []
        for k in range(piece // SUB):
            span = slice(k * SUB, (k + 1) * SUB)
            weight = trans[seg] * alpha[span]
            trans[seg] = trans[seg] - weight
            shown = weight * field[span, 256:512]
            behind[seg] = behind[seg] - shown
            parts.append((shown - ratio[span] * behind[seg], weight))
        at = slice(c * piece, (c + 1) * piece)
        value = jnp.concatenate([p[0] for p in parts], axis=0)
        one = value.astype(BF16)
        halves[slot, at, 0:256] = one
        halves[slot, at, 256:512] = (value - one.astype(F32)).astype(BF16)
        halves[slot, at, 512:768] = jnp.concatenate([p[1] for p in parts], axis=0).astype(BF16)
        yield


BACK_TURNS = "fss" * 4


def find_moments(slot, tile, cots, halves, grads):
    rows = [cots[tile, ch : ch + 1, :] for ch in range(3)]
    ones, twos = zip(*(split2(r) for r in rows))
    base = stack_rows(basis_rows(256), 16)
    colours = stack_rows([None] * 6 + list(ones) + list(twos), 16)
    kernel = jnp.concatenate([base, base, colours], axis=1).astype(BF16)
    wide = 128
    for n in range(halves.shape[1] // wide):
        at = slice(n * wide, (n + 1) * wide)
        found = lax.dot_general(kernel, halves[slot, at, :], NT, preferred_element_type=F32)
        low = found[8:16, :]
        at16 = iota(low.shape, 0)
        top = found[0:8, :] + jnp.where(at16 >= 6, pltpu.roll(low, 5, 0), 0.0)
        grads[tile, 0:8, at] = top
        grads[tile, 8:9, at] = low[0:1, :] + low[3:4, :]
        yield


def gather_home(me, n, back, send, centres, conic, rho, opacity, out, total, rows, own, recv_sem):
    left = iota((SUB, LANE), 1) < 64
    row = iota((SUB, LANE), 0)
    pairs = n // 2
    mine = me // 2
    blocks = centres.shape[1] // 256
    used = pl.ds(0, USED)
    total[...] = jnp.zeros_like(total)

    def chunk(g, messages):
        arrived = back.at[pl.ds(0, messages), used]
        pltpu.make_async_copy(arrived, arrived, recv_sem.at[g]).wait()
        eight, ninth, idx = [], [], []
        for k in range(GROUP):
            i = lax.rem(mine + pairs - (g * GROUP + k), pairs)
            values, last = unpack_pair(back[2 * i], back[2 * i + 1], left, row)
            eight.append(values)
            ninth.append(last)
            idx.append(send[0:1, pl.ds(pl.multiple_of(i * LANE, LANE), LANE)])
        total[...] = total[...] + scatter_block(
            jnp.concatenate(eight, axis=1), jnp.concatenate(ninth, axis=1), jnp.concatenate(idx, axis=1), blocks
        )

    own.wait()
    chunk(0, 2 * GROUP - 1)

    def later(g, carry):
        chunk(g, 2 * GROUP)
        return carry

    lax.fori_loop(1, pairs // GROUP, later, 0)
    for h in range(blocks):
        span = slice(h * 256, (h + 1) * 256)
        rows[0:8, span] = total[h * SUB : (h + 1) * SUB, :]
        rows[8:9, span] = total[blocks * SUB + h : blocks * SUB + h + 1, :]
    m_uu, m_uv, m_vv, m_u, m_v, m_1 = (rows[p : p + 1, :] for p in range(6))
    cx, cy = centres[0:1, :], centres[1:2, :]
    a, c = conic[0:1, :], conic[1:2, :]
    r = rho[...]
    root = jnp.sqrt(a * c)
    b = r * root
    x1, y1 = m_u - cx * m_1, m_v - cy * m_1
    xx = m_uu - cx * (m_u + x1)
    yy = m_vv - cy * (m_v + y1)
    xy = m_uv - cx * m_v - cy * x1
    out[0:1, :] = a * x1 + b * y1
    out[1:2, :] = c * y1 + b * x1
    out[2:3, :] = -0.5 * xx - xy * (0.5 * r * (root / a))
    out[3:4, :] = -0.5 * yy - xy * (0.5 * r * (root / c))
    out[4:5, :] = -xy * root
    out[5:6, :] = m_1 / opacity[...]
    out[6:9, :] = rows[6:9, :]


def backward_kernel(
    lists, left_in, grad, chunk_rend, chunk_start, send, centres, conic, rho, opacity, result,
    cots, halves, grads, slots, out, back, total, rows, local_sem, send_sem, recv_sem
):
    me = lax.axis_index("dev")
    n = lax.axis_size("dev")
    barrier = pltpu.get_barrier_semaphore()
    each = (n - 1) // (lists.shape[0] // 2)

    def greet(k):
        pl.semaphore_signal(barrier, inc=1, device_id=(lax.rem(me + k, n),), device_id_type=MESH)

    step = pl.program_id(0)
    steps = pl.num_programs(0)

    steps_static = lists.shape[0] // 2

    @pl.when(step == 0)
    def _():
        for k in range(each * steps_static + 1, n):
            greet(k)
        for ch in range(3):
            for g in range(cots.shape[0] // SUB):
                for h in range(2):
                    span = slice(h * LANE, (h + 1) * LANE)
                    block = block_transpose(grad[ch, h * SUB : (h + 1) * SUB, g * LANE : (g + 1) * LANE])
                    for t in range(SUB):
                        cots[g * SUB + t, ch : ch + 1, span] = block[t : t + 1, :]

    for k in range(each):
        greet(step * each + k + 1)
    for slot in range(2):
        tile = 2 * step + slot
        past = jnp.maximum(tile - 1, 0)
        take_turns(
            BACK_TURNS,
            f=find_moments(1 - slot, past, cots, halves, grads),
            s=shade_tile(slot, tile, left_in, chunk_rend, chunk_start, cots, halves),
        )

    @pl.when(step == steps - 1)
    def _():
        for _ in find_moments(1, 2 * step + 1, cots, halves, grads):
            pass
        slots[...] = jnp.zeros_like(slots)
        blocks = slots.shape[0] // (SUB + 1)
        group = 2

        def chunk(c, carry):
            each = [c * group + k for k in range(group)]
            idx = jnp.concatenate([jnp.maximum(lists[t], 0) for t in each], axis=1)
            eight = jnp.concatenate([grads[t, 0:8, :] for t in each], axis=1)
            ninth = jnp.concatenate([grads[t, 8:9, :] for t in each], axis=1)
            slots[...] = slots[...] + scatter_block(eight, ninth, idx, blocks)
            return carry

        lax.fori_loop(0, cots.shape[0] // group, chunk, 0)
        left = iota((SUB, LANE), 1) < 64
        row = iota((SUB, LANE), 0)
        for h in range(blocks):
            for half in range(2):
                span = slice(half * LANE, (half + 1) * LANE)
                acc = slots[h * SUB : (h + 1) * SUB, span]
                extra = jnp.broadcast_to(slots[blocks * SUB + h : blocks * SUB + h + 1, span], (SUB, LANE))
                owner = 4 * h + 2 * half
                out[owner], out[owner + 1] = pack_pair(acc, extra, left, row)
        pl.semaphore_wait(barrier, n - 1)
        used = pl.ds(0, USED)
        own = pltpu.make_async_copy(out.at[me, used], back.at[me, used], local_sem)
        own.start()
        pairs = n // 2
        mine = me // 2

        def ship_to(peer, k):
            pltpu.make_async_remote_copy(
                src_ref=out.at[peer, used], dst_ref=back.at[me, used],
                send_sem=send_sem, recv_sem=recv_sem.at[k // GROUP],
                device_id=(peer,), device_id_type=MESH,
            ).start()

        ship_to(me + 1 - 2 * lax.rem(me, 2), 0)

        def ship(k, carry):
            for core in range(2):
                ship_to(2 * lax.rem(mine + k, pairs) + core, k)
            return carry

        lax.fori_loop(1, pairs, ship, 0)
        gather_home(me, n, back, send, centres, conic, rho, opacity, result, total, rows, own, recv_sem)
        sent = out.at[pl.ds(0, n - 1), used]
        pltpu.make_async_copy(sent, sent, send_sem).wait()


def struct(*shape, dtype=F32):
    return jax.ShapeDtypeStruct(shape, dtype)


def shards(tile_lists, send_rows, centres, conic, rho, opacity, colors, target):
    devices = lax.axis_size("dev")
    owned = centres.shape[1]
    tiles, count = tile_lists.shape
    height, width = target.shape[1], target.shape[2]
    pixels = height * height
    params = lambda mib: pltpu.CompilerParams(vmem_limit_bytes=mib << 20)
    sources = (send_rows, centres, conic, rho, opacity, colors, tile_lists)
    whole = lambda *shape: pl.BlockSpec(shape, lambda t: (0,) * len(shape))
    per = 2
    per_tile = lambda *shape: pl.BlockSpec((per,) + shape, lambda t: (t,) + (0,) * len(shape))
    hi_blocks = devices * 64 // 256
    image, pixel_grad, chunk_rend, chunk_start, left, lists = pl.pallas_call(
        forward_kernel,
        grid=(tiles // per,),
        in_specs=[pl.BlockSpec(memory_space=pltpu.HBM)] * 8,
        out_specs=[
            whole(3, height, width), whole(3, height, width),
            per_tile(3, 2, SUB, pixels), per_tile(2, SUB, pixels), per_tile(count, 32), whole(tiles, 1, count),
        ],
        out_shape=[
            struct(3, height, width),
            struct(3, height, width),
            struct(tiles, 3, 2, SUB, pixels),
            struct(tiles, 2, SUB, pixels),
            struct(tiles, count, 32, dtype=BF16),
            struct(tiles, 1, count, dtype=jnp.int32),
        ],
        scratch_shapes=[
            pltpu.VMEM((hi_blocks * SUB, 256), F32),
            pltpu.VMEM((hi_blocks, 256), F32),
            pltpu.VMEM((hi_blocks * (SUB + 1), 2 * 256), BF16),
            pltpu.VMEM((per, count, LANE), F32),
            pltpu.VMEM((per, count, pixels), F32),
            pltpu.VMEM((3, tiles, pixels), F32),
            pltpu.VMEM((3, height, width), F32),
        ]
        + [pltpu.VMEM((RIMS, width), F32)] * 4
        + [
            pltpu.VMEM((5, 3 * height, width), F32),
            pltpu.VMEM((3, 2 * height, width), F32),
            pltpu.VMEM((3, 2, 2 * height, width), F32),
        ]
        + [pltpu.SemaphoreType.DMA((8,))] * 2
        + [
            pltpu.VMEM((devices, SUB, LANE), F32),
            pltpu.VMEM((tiles, 1, count), jnp.int32),
            pltpu.VMEM((3, 3, height, width), F32),
            pltpu.VMEM((devices, SUB, LANE), F32),
            pltpu.VMEM((SUB, owned), F32),
            pltpu.VMEM((owned // LANE, LANE), F32),
        ]
        + [pltpu.VMEM(v.shape, v.dtype) for v in sources]
        + [pltpu.SemaphoreType.DMA((8,))]
        + [pltpu.SemaphoreType.DMA] * 2
        + [pltpu.SemaphoreType.DMA((3,))] * 2,
        compiler_params=pltpu.CompilerParams(collective_id=0, has_side_effects=True, vmem_limit_bytes=60 * 1024 * 1024),
        name="tile_forward",
    )(*sources, target)

    grads = pl.pallas_call(
        backward_kernel,
        grid=(tiles // per,),
        in_specs=[
            whole(tiles, 1, count), per_tile(count, 32), whole(3, height, width),
            per_tile(3, 2, SUB, pixels), per_tile(2, SUB, pixels),
        ]
        + [whole(*v.shape) for v in sources[:5]],
        out_specs=whole(9, owned),
        out_shape=struct(9, owned),
        scratch_shapes=[
            pltpu.VMEM((tiles, 3, pixels), F32),
            pltpu.VMEM((per, count, 3 * pixels), BF16),
            pltpu.VMEM((tiles, 16, count), F32),
            pltpu.VMEM((hi_blocks * (SUB + 1), 256), F32),
            pltpu.VMEM((devices, SUB, LANE), F32),
            pltpu.VMEM((devices, SUB, LANE), F32),
            pltpu.VMEM((owned // 256 * (SUB + 1), 256), F32),
            pltpu.VMEM((16, owned), F32),
            pltpu.SemaphoreType.DMA,
            pltpu.SemaphoreType.DMA,
            pltpu.SemaphoreType.DMA((devices // 2 // GROUP,)),
        ],
        compiler_params=pltpu.CompilerParams(collective_id=1, has_side_effects=True, vmem_limit_bytes=60 * 1024 * 1024),
        name="tile_backward",
    )(lists, left, pixel_grad, chunk_rend, chunk_start, *sources[:5])
    return image, grads


def solution(mesh):
    return jax.shard_map(
        shards,
        mesh=mesh,
        in_specs=(
            P("dev", None),
            P("dev", None),
            P(None, "dev"),
            P(None, "dev"),
            P(None, "dev"),
            P(None, "dev"),
            P(None, "dev"),
            P(None, "dev", None),
        ),
        out_specs=(P(None, "dev", None), P(None, "dev")),
        check_vma=False,
    )
```

```python
import functools
import math

import jax
import jax.numpy as jnp
import numpy as np
from jax import lax
from jax.experimental import pallas as pl
from jax.experimental.pallas import tpu as pltpu
from jax.sharding import PartitionSpec as P

F32 = jnp.float32
BF16 = jnp.bfloat16
LOG2E = math.log2(math.e)
SUB, LANE = 8, 128
DEAD = -10000.0


def lane_pick(table, lanes):
    return jnp.take_along_axis(table, lanes, axis=1, mode="promise_in_bounds")


def iota(shape, dim):
    return lax.broadcasted_iota(jnp.int32, shape, dim)


def sub_sum(x):
    for d in (4, 2, 1):
        x = x + pltpu.roll(x, d, 0)
    return x


def split2(x):
    one = x.astype(BF16).astype(F32)
    return one, x - one


def coefficient_rows(cx, cy, a, c, rho, op):
    b = rho * jnp.sqrt(a * c)
    bx, by = a * cx + b * cy, c * cy + b * cx
    one = jnp.log(op) - 0.5 * (cx * bx + cy * by)
    return [LOG2E * k for k in (-0.5 * a, -b, -0.5 * c, bx, by, one)]


def pick_tree(parts, bits):
    if len(parts) == 1:
        return parts[0]()
    half = len(parts) // 2
    return jnp.where(bits[half], pick_tree(parts[half:], bits), pick_tree(parts[:half], bits))


def pick_nine(table, ninth, idx, row, blocks):
    hi, lo = lax.shift_right_logical(idx, 7), lax.bitwise_and(idx, 127)
    bits = {1 << k: lax.bitwise_and(hi, 1 << k) != 0 for k in range(blocks.bit_length() - 1)}
    eight = pick_tree([lambda h=h: lane_pick(table(h), lo) for h in range(blocks)], bits)
    coarse = {k // SUB: v for k, v in bits.items() if k >= SUB}
    last = pick_tree(
        [lambda v=v: lane_pick(ninth[v * SUB : (v + 1) * SUB, :], lo) for v in range(blocks // SUB)], coarse
    )
    return eight, sub_sum(jnp.where(lax.bitwise_and(hi, 7) == row, last, 0.0))


MESH = pl.DeviceIdType.MESH
USED = 5
GROUP = 8
RIM = 10
RIMS = 32


def pack_pair(eight, last, left, row):
    low = pltpu.roll(eight, 4, 0)
    even = jnp.where(left, eight, pltpu.roll(low, 64, 1))
    odd = jnp.where(left, pltpu.roll(eight, 64, 1), low)
    return jnp.where(row < 4, even, last), jnp.where(row < 4, odd, pltpu.roll(last, 64, 1))


def unpack_pair(even, odd, left, row):
    high = jnp.where(left, even, pltpu.roll(odd, 64, 1))
    low = jnp.where(left, pltpu.roll(even, 64, 1), odd)
    return jnp.where(row < 4, high, pltpu.roll(low, 4, 0)), high[4:5, :]


def greet_all(n, me):
    barrier = pltpu.get_barrier_semaphore()

    def greet(k, carry):
        pl.semaphore_signal(barrier, inc=1, device_id=(lax.rem(me + k, n),), device_id_type=MESH)
        return carry

    lax.fori_loop(1, n, greet, 0)
    return barrier


def halo_copies(n, me, strip, before, after, send_sem, recv_sem):
    return [
        pltpu.make_async_remote_copy(
            src_ref=strip, dst_ref=to, send_sem=send_sem.at[k], recv_sem=recv_sem.at[k],
            device_id=(lax.rem(me + hop, n),), device_id_type=MESH,
        )
        for k, (hop, to) in enumerate(((1, before), (n - 1, after)))
    ]


def send_owned(
    me, n, sources, strip, out, strips, x, table, ninth, places, sorted_lists,
    local_sem, send_sem, recv_sem, halo_send, halo_recv
):
    fetched = [pltpu.make_async_copy(a, b, local_sem.at[k]) for k, (a, b) in enumerate(zip(sources, places))]
    for copy in fetched:
        copy.start()
    barrier = greet_all(n, me)
    for copy in fetched:
        copy.wait()
    send, centres, conic, rho, opacity, colors, raw_lists = places
    rows = coefficient_rows(
        centres[0:1, :], centres[1:2, :], conic[0:1, :], conic[1:2, :], rho[...], opacity[...]
    )
    for p, value in enumerate(rows + [colors[0:1, :], colors[1:2, :]]):
        table[p : p + 1, :] = value
    blocks = table.shape[1] // LANE
    for h in range(blocks):
        ninth[h : h + 1, :] = colors[2:3, h * LANE : (h + 1) * LANE]
    left = iota((SUB, LANE), 1) < 64
    row = iota((SUB, LANE), 0)
    pairs = n // 2
    mine = me // 2
    used = pl.ds(0, USED)
    step = 4

    def fill(group):
        for k in range(step):
            i = lax.rem(mine + group * step + k, pairs)
            start = pl.multiple_of(i * LANE, LANE)
            idx = jnp.broadcast_to(jnp.maximum(send[0:1, pl.ds(start, LANE)], 0), (SUB, LANE))
            eight, last = pick_nine(lambda h: table[:, h * LANE : (h + 1) * LANE], ninth, idx, row, blocks)
            x[2 * i], x[2 * i + 1] = pack_pair(eight, last, left, row)

    def ship(k):
        for core in range(2):
            peer = 2 * lax.rem(mine + k, pairs) + core
            pltpu.make_async_remote_copy(
                src_ref=x.at[peer, used], dst_ref=out.at[me, used], send_sem=send_sem, recv_sem=recv_sem,
                device_id=(peer,), device_id_type=MESH,
            ).start()

    copies = halo_copies(n, me, strip, strips.at[0], strips.at[2], halo_send, halo_recv)
    copies.append(pltpu.make_async_copy(strip, strips.at[1], halo_recv.at[2]))
    early = 5

    def first(group, carry):
        fill(group)
        return carry

    lax.fori_loop(0, early, first, 0)
    pl.semaphore_wait(barrier, n - 1)
    for copy in copies:
        copy.start()
    partner = me + 1 - 2 * lax.rem(me, 2)
    own = pltpu.make_async_copy(x.at[me, used], out.at[me, used], local_sem.at[7])
    own.start()
    pltpu.make_async_remote_copy(
        src_ref=x.at[partner, used], dst_ref=out.at[me, used], send_sem=send_sem, recv_sem=recv_sem,
        device_id=(partner,), device_id_type=MESH,
    ).start()

    def ship_one(k, carry):
        ship(k)
        return carry

    lax.fori_loop(1, (early - 1) * step, ship_one, 0)

    def both(group, carry):
        for k in range(step):
            ship((group - 1) * step + k)
        fill(group)
        return carry

    lax.fori_loop(early, pairs // step, both, 0)
    lax.fori_loop(pairs - step, pairs, ship_one, 0)
    lane = iota((SUB, LANE), 1)
    place = lax.bitwise_and(lane, 7)
    count = raw_lists.shape[1]
    for q in range(count // LANE):
        source = lax.bitwise_and(place, 1) * 64 + (LANE // SUB) * q + lax.shift_right_logical(lane, 3)
        half = lax.shift_right_logical(place, 1)
        for g in range(raw_lists.shape[0] // SUB):
            mixed = jnp.zeros((SUB, LANE), jnp.int32)
            for b in range(count // LANE):
                block = raw_lists[g * SUB : (g + 1) * SUB, b * LANE : (b + 1) * LANE]
                mixed = jnp.where(half == b, lane_pick(block, source), mixed)
            for t in range(SUB):
                sorted_lists[g * SUB + t, :, q * LANE : (q + 1) * LANE] = mixed[t : t + 1, :]
    own.wait()
    rest = pl.ds(0, n - 1)
    pltpu.make_async_copy(x.at[rest, used], x.at[rest, used], send_sem).wait()
    pltpu.make_async_copy(out.at[rest, used], out.at[rest, used], recv_sem).wait()
    for copy in copies:
        copy.wait()


def block_transpose(x):
    row = iota(x.shape, 0)
    block = lax.shift_right_logical(iota(x.shape, 1), 4)
    for d in (1, 2, 4):
        low_row = lax.bitwise_and(row, d) == 0
        low_block = lax.bitwise_and(block, d) == 0
        down = pltpu.roll(pltpu.roll(x, SUB - d, 0), 16 * d, 1)
        back = pltpu.roll(pltpu.roll(x, d, 0), LANE - 16 * d, 1)
        x = jnp.where(low_row == low_block, x, jnp.where(low_row, down, back))
    return x


def basis_rows(lanes):
    pixel = iota((1, lanes), 1)
    v = lax.shift_right_logical(pixel, 4).astype(F32) - 7.5
    u = lax.bitwise_and(pixel, 15).astype(F32) - 7.5
    return [u * u, u * v, v * v, u, v, jnp.ones_like(u)]


def stack_rows(rows, count):
    shape = (count, next(r for r in rows if r is not None).shape[1])
    at = iota(shape, 0)
    result = jnp.zeros(shape, F32)
    for p, row in enumerate(rows):
        if row is not None:
            result = jnp.where(at == p, jnp.broadcast_to(row, shape), result)
    return result


def scan_sub(x):
    at = iota(x.shape, 0)
    x = jnp.where(at == 0, 1.0, pltpu.roll(x, 1, 0))
    for d in (1, 2, 4):
        x = x * jnp.where(at >= d, pltpu.roll(x, d, 0), 1.0)
    return x


def take_turns(order, **workers):
    for name in order:
        next(workers[name], None)
    for worker in workers.values():
        for _ in worker:
            pass


def segments(count):
    groups = count // SUB // 2
    return [(seg, j, (seg * groups + j) * SUB) for j in range(groups) for seg in range(2)]


def split3(x):
    one, rest = split2(x)
    two, three = split2(rest)
    return one, two, three


def gather_columns(raw, flat, cols, slot):
    count = raw.shape[1]
    blocks = flat.shape[0] // (SUB + 1)
    row = iota((SUB, LANE), 0)
    wide = 2 * LANE
    founds = []
    for n in range(count // wide):
        idx = jnp.maximum(raw[:, n * wide : (n + 1) * wide], 0)
        hi, lo = lax.shift_right_logical(idx, 8), lax.bitwise_and(idx, 255)
        hot = onehot(lo, 256)
        found = jnp.dot(flat[...], jnp.concatenate([hot] * 2, axis=0), preferred_element_type=F32)
        founds.append((hi, found))
        yield
    for q in range(count // LANE):
        hi, found = founds[q // 2]
        span = slice((q % 2) * LANE, (q % 2 + 1) * LANE)
        out = slice(q * LANE, (q + 1) * LANE)
        hq = jnp.broadcast_to(hi[:, span], (SUB, LANE))
        bits = {1 << k: lax.bitwise_and(hq, 1 << k) != 0 for k in range(blocks.bit_length() - 1)}
        acc = pick_tree([lambda h=h: found[h * SUB : (h + 1) * SUB, span] for h in range(blocks)], bits)
        coarse = {k // SUB: v for k, v in bits.items() if k >= SUB}
        base = blocks * SUB
        last = pick_tree(
            [lambda v=v: found[base + v * SUB : base + (v + 1) * SUB, span] for v in range(blocks // SUB)], coarse
        )
        last = sub_sum(jnp.where(lax.bitwise_and(hq, 7) == row, last, 0.0))
        yield
        acc = jnp.where((row == 5) & (jnp.broadcast_to(raw[:, out], (SUB, LANE)) < 0), DEAD, acc)
        one, two, three = split3(acc)
        b_one, b_two = split2(last)
        more = jnp.where(row == 1, b_two, jnp.where(row == 7, last, b_one))
        more = jnp.where((row == 3) | (row == 4), pltpu.roll(one, 5, 0), more)
        more = jnp.where((row == 5) | (row == 6), pltpu.roll(acc, 7, 0), more)
        stack = jnp.concatenate([one, two, three, more], axis=0)
        cols[slot, out, :] = jnp.concatenate([stack, jnp.zeros((LANE - 32, LANE), F32)], axis=0).T
        yield


TURNS = "d" * 8 + "g" + "d" * 6 + "g" + "d" * 2 + "gg" + "d" * 2 + "gg" + "d" * 2 + "gg" + "d" * 4 + "gg"


def draw_tile(slot, tile, basis, chunk_rend, chunk_start, left_out, cols, alphas, rends):
    count = cols.shape[1]
    ones = jnp.ones((SUB, 256), F32)
    product = [ones, ones]
    piece = 64
    for c in range(count // piece):
        span = slice(c * piece, (c + 1) * piece)
        left = cols[slot, span, 0:32].astype(BF16)
        left_out[slot, span, :] = left
        alpha = jnp.exp2(jnp.dot(left, basis, preferred_element_type=F32))
        alphas[slot, span, :] = alpha
        rest = 1.0 - alpha
        parts = [rest[k * SUB : (k + 1) * SUB, :] for k in range(piece // SUB)]
        while len(parts) > 1:
            parts = [parts[k] * parts[k + 1] for k in range(0, len(parts), 2)]
        seg = 2 * c * piece // count
        product[seg] = product[seg] * parts[0]
        yield

    begin = scan_sub(product[0] * product[1])
    trans = [begin, begin * product[0]]
    zero = jnp.zeros((SUB, 256), F32)
    sums = [[zero] * 3, [zero] * 3]
    for seg in range(2):
        chunk_start[slot, seg] = trans[seg]
    for seg, j, at in segments(count):
        weight = trans[seg] * alphas[slot, at : at + SUB, :]
        trans[seg] = trans[seg] - weight
        color = cols[slot, at : at + SUB, :]
        sums[seg] = [t + weight * color[:, 29 + ch : 30 + ch] for ch, t in enumerate(sums[seg])]
        if seg == 1 and j % 2 == 1:
            yield
    for ch in range(3):
        for seg in range(2):
            chunk_rend[slot, ch, seg] = sums[seg][ch]
        rends[ch, pl.ds(tile, 1), :] = sub_sum(sums[0][ch] + sums[1][ch])[0:1, :]


def step_kernel(*refs):
    sources, target, image, result = refs[:7], *refs[7:10]
    pieces, ninth, flat, cols, alphas, rends, image_too, head, tail, *loss_refs = refs[10:26]
    recv, lists, strips, *send_refs = refs[26:44]
    grad, chunk_rend, chunk_start, left_out, *back_refs = refs[44:]
    me = lax.axis_index("dev")
    n = lax.axis_size("dev")
    x, table, own_ninth, *more = send_refs
    send_owned(me, n, sources, target, recv, strips, x, table, own_ninth, more[:7], lists, *more[7:])
    row = iota((SUB, LANE), 0)
    blocks = pieces.shape[0] // SUB
    left = iota((SUB, LANE), 1) < 64

    def block(h, carry):
        lasts = []
        for half in range(2):
            owner = 4 * h + 2 * half
            eight, last = unpack_pair(recv[owner], recv[owner + 1], left, row)
            pieces[pl.ds(pl.multiple_of(h * SUB, SUB), SUB), half * LANE : (half + 1) * LANE] = eight
            lasts.append(last)
        ninth[pl.ds(h, 1), :] = jnp.concatenate(lasts, axis=1)
        return carry

    lax.fori_loop(0, blocks, block, 0)
    for rows, source in ((slice(0, blocks * SUB), pieces), (slice(blocks * SUB, None), ninth)):
        for k, part in enumerate(split2(source[...])):
            flat[rows, k * 256 : (k + 1) * 256] = part.astype(BF16)
    for _ in gather_columns(lists[0], flat, cols, 0):
        pass
    basis = stack_rows((basis_rows(256) + [None, None]) * 3, 32).astype(BF16)

    def forward(step, carry):
        views = [ref.at[pl.ds(2 * step, 2)] for ref in (chunk_rend, chunk_start, left_out)]
        for slot in range(2):
            tile = 2 * step + slot
            later = jnp.minimum(tile + 1, lists.shape[0] - 1)
            take_turns(
                TURNS,
                g=gather_columns(lists[later], flat, cols, 1 - slot),
                d=draw_tile(slot, tile, basis, *views, cols, alphas, rends),
            )
        return carry

    lax.fori_loop(0, lists.shape[0] // 2, forward, 0)
    for ch in range(3):
        for g in range(rends.shape[1] // SUB):
            for h in range(2):
                block = block_transpose(rends[ch, g * SUB : (g + 1) * SUB, h * LANE : (h + 1) * LANE])
                span = slice(g * LANE, (g + 1) * LANE)
                for to in (image, image_too):
                    to[ch, h * SUB : (h + 1) * SUB, span] = block
                at = RIM * ch
                if h == 0:
                    head[at : at + SUB, span] = block
                    tail[at : at + 2, span] = block[6:8, :]
                else:
                    head[at + SUB : at + RIM, span] = block[0:2, :]
                    tail[at + 2 : at + RIM, span] = block
    loss_gradient(me, n, image_too, head, tail, strips, grad, *loss_refs)
    shade_all(me, n, lists, left_out, grad, chunk_rend, chunk_start, *more[:5], result, *back_refs)


def taps_of():
    offsets = np.arange(11, dtype=np.float32) - np.float32(5)
    taps = np.exp(-offsets * offsets / np.float32(4.5)).astype(np.float32)
    return [float(t) for t in taps / taps.sum(dtype=np.float32)]


TAPS = taps_of()


def blur_rows(read, start, count):
    total = TAPS[5] * read(start, count)
    for m in range(1, 6):
        total = total + TAPS[5 + m] * (read(start - m, count) + read(start + m, count))
    return total


def blur_lanes(x):
    rows, width = x.shape
    pad = jnp.zeros((rows, LANE), F32)
    wide = jnp.concatenate([x, pad], axis=1)
    total = TAPS[5] * x
    for m in range(1, 6):
        both = pltpu.roll(wide, m, 1) + pltpu.roll(wide, width + LANE - m, 1)
        total = total + TAPS[5 + m] * both[:, :width]
    return total


def rim_copies(me, n, head, tail, before, after, send_sem, recv_sem):
    sides = []
    for k, (hop, source, to) in enumerate(((1, tail, before), (n - 1, head, after))):
        side = []
        for part in range(RIMS // SUB):
            rows = pl.ds(part * SUB, SUB)
            side.append(
                pltpu.make_async_remote_copy(
                    src_ref=source.at[rows], dst_ref=to.at[rows],
                    send_sem=send_sem.at[2 * part + k], recv_sem=recv_sem.at[2 * part + k],
                    device_id=(lax.rem(me + hop, n),), device_id_type=MESH,
                )
            )
        sides.append(side)
    return sides


def loss_gradient(
    me, n, centre, head, tail, target, grad, before, after, pads, maps, blurred, send_sem, recv_sem
):
    height, width = centre.shape[1:]
    rim = RIM
    up, down = rim_copies(me, n, head, tail, before, after, send_sem, recv_sem)
    for there, side in ((me < n - 1, up), (me > 0, down)):
        @pl.when(there)
        def _():
            for copy in side:
                copy.start()
    t_before, t_centre, t_after = target.at[0], target.at[1], target.at[2]
    at = iota((2 * height, width), 0) - height // 2 + me * height
    inside = (at >= 0) & (at < n * height)

    def wide_blur(k):
        vertical = blur_rows(lambda s, c: pads[k, s : s + c, :], height // 2, 2 * height)
        return blur_lanes(vertical)

    edge = height - rim
    for k in range(5):
        pads[k, 0:edge, :] = jnp.zeros((edge, width), F32)
        pads[k, 3 * height - edge :, :] = jnp.zeros((edge, width), F32)
    for ch in range(3):
        first = jnp.where(me > 0, t_before[ch, edge:height, :], 0.0)
        last = jnp.where(me < n - 1, t_after[ch, 0:rim, :], 0.0)
        for rows, tt in (
            (slice(edge, height), first), (slice(height, 2 * height), t_centre[ch]),
            (slice(2 * height, 2 * height + rim), last),
        ):
            pads[1, rows, :] = tt
            pads[3, rows, :] = tt * tt
        blurred[ch, 0] = wide_blur(1)
        blurred[ch, 1] = wide_blur(3)

    for ch in range(3):
        parts = slice(0, 2) if ch == 0 else slice(ch + 1, ch + 2)
        for there, side in ((me > 0, up[parts]), (me < n - 1, down[parts])):
            @pl.when(there)
            def _():
                for copy in side:
                    copy.wait_recv()

        for rows, keep, r, t in (
            (slice(edge, height), me > 0, before[rim * ch : rim * (ch + 1), :], t_before[ch, edge:height, :]),
            (slice(height, 2 * height), None, centre[ch], t_centre[ch]),
            (slice(2 * height, 2 * height + rim), me < n - 1, after[rim * ch : rim * (ch + 1), :], t_after[ch, 0:rim, :]),
        ):
            if keep is not None:
                r, t = jnp.where(keep, r, 0.0), jnp.where(keep, t, 0.0)
            pads[0, rows, :] = r
            pads[2, rows, :] = r * r
            pads[4, rows, :] = r * t
        mr, rr, rt = wide_blur(0), wide_blur(2), wide_blur(4)
        mt, tt = blurred[ch, 0], blurred[ch, 1]
        cv = rt - mr * mt
        top1 = 2.0 * mr * mt + 0.0001
        top2 = 2.0 * cv + 0.0009
        low1 = mr * mr + mt * mt + 0.0001
        low2 = (rr - mr * mr) + (tt - mt * mt) + 0.0009
        inv1, inv2 = 1.0 / low1, 1.0 / low2
        both = inv1 * inv2
        ssim = top1 * top2 * both
        d_rr = -ssim * inv2
        d_rt = 2.0 * top1 * both
        d_mr = 2.0 * (mt * (top2 - top1) * both + mr * ssim * (inv2 - inv1))
        for k, value in enumerate((d_mr, d_rr, d_rt)):
            maps[k] = jnp.where(inside, value, 0.0)

        def back_blur(k):
            vertical = blur_rows(lambda s, c: maps[k, s : s + c, :], height // 2, height)
            return blur_lanes(vertical)

        g_mr, g_rr, g_rt = (back_blur(k) for k in range(3))
        r, t = centre[ch], t_centre[ch]
        grad[ch] = 1.6 * (r - t) - 0.2 * (g_mr + 2.0 * r * g_rr + t * g_rt)
    for there, side in ((me < n - 1, up), (me > 0, down)):
        @pl.when(there)
        def _():
            for copy in side:
                copy.wait_send()


NT = (((1,), (1,)), ((), ()))


def onehot(lo, rows):
    return jnp.where(iota((rows, lo.shape[1]), 0) == lo, 1.0, 0.0).astype(BF16)


def spread(values, hi, blocks):
    masked = [jnp.where(hi == h, values, 0.0) for h in range(blocks)]
    return jnp.concatenate(masked, axis=0)


def scatter_block(eight, ninth, idx, blocks):
    span = idx.shape[1]
    hi, lo = lax.shift_right_arithmetic(idx, 8), lax.bitwise_and(idx, 255)
    hot = onehot(lo, 256)
    hi8 = jnp.broadcast_to(hi, (SUB, span))
    own = iota((blocks, span), 0) == hi
    left = []
    for values, extra in zip(split2(eight), split2(ninth)):
        left.append(spread(values, hi8, blocks))
        left.append(jnp.where(own, jnp.broadcast_to(extra, own.shape), 0.0))
    left = jnp.concatenate(left, axis=0).astype(BF16)
    both = lax.dot_general(left, hot, NT, preferred_element_type=F32)
    return both[: blocks * (SUB + 1), :] + both[blocks * (SUB + 1) :, :]


def shade_tile(slot, tile, left_in, chunk_rend, chunk_start, cots, halves):
    count = left_in.shape[1]
    rows = [cots[tile, ch : ch + 1, :] for ch in range(3)]
    ones, twos = zip(*(split2(r) for r in rows))
    basis = stack_rows((basis_rows(256) + [None, None]) * 3, 32)
    back = stack_rows(
        [None] * 6 + [ones[0], ones[1]] + [None] * 6 + [ones[0], ones[1]] + [None] * 6
        + [ones[0], ones[1], ones[2], ones[2], twos[2], twos[0], twos[1]], 32
    )
    right = jnp.concatenate([basis, back], axis=1).astype(BF16)

    inside = [sum(chunk_rend[slot, ch, seg] * rows[ch] for ch in range(3)) for seg in range(2)]
    at8 = iota((SUB, 256), 0)
    later = inside[0] + inside[1]
    later = jnp.where(at8 == SUB - 1, 0.0, pltpu.roll(later, SUB - 1, 0))
    for d in (1, 2, 4):
        later = later + jnp.where(at8 < SUB - d, pltpu.roll(later, SUB - d, 0), 0.0)
    behind = [later + inside[1] + inside[0], later + inside[1]]
    trans = [chunk_start[slot, seg] for seg in range(2)]

    piece = 64
    order = [c // 2 + (c % 2) * (count // piece // 2) for c in range(count // piece)]

    def field_of(c):
        return jnp.dot(left_in[slot, c * piece : (c + 1) * piece, :], right, preferred_element_type=F32)

    ahead = 1
    fields = [field_of(c) for c in order[:ahead]]
    for n, c in enumerate(order):
        if n + ahead < len(order):
            fields.append(field_of(order[n + ahead]))
        seg = 2 * c * piece // count
        field = fields[n]
        alpha = jnp.exp2(field[:, 0:256])
        ratio = alpha / (1.0 - alpha)
        parts = []
        for k in range(piece // SUB):
            span = slice(k * SUB, (k + 1) * SUB)
            weight = trans[seg] * alpha[span]
            trans[seg] = trans[seg] - weight
            shown = weight * field[span, 256:512]
            behind[seg] = behind[seg] - shown
            parts.append((shown - ratio[span] * behind[seg], weight))
        at = slice(c * piece, (c + 1) * piece)
        value = jnp.concatenate([p[0] for p in parts], axis=0)
        one = value.astype(BF16)
        halves[slot, at, 0:256] = one
        halves[slot, at, 256:512] = (value - one.astype(F32)).astype(BF16)
        halves[slot, at, 512:768] = jnp.concatenate([p[1] for p in parts], axis=0).astype(BF16)
        yield


BACK_TURNS = "fss" * 4


def find_moments(slot, tile, cots, halves, grads):
    rows = [cots[tile, ch : ch + 1, :] for ch in range(3)]
    ones, twos = zip(*(split2(r) for r in rows))
    base = stack_rows(basis_rows(256), 16)
    colours = stack_rows([None] * 6 + list(ones) + list(twos), 16)
    kernel = jnp.concatenate([base, base, colours], axis=1).astype(BF16)
    wide = 128
    for n in range(halves.shape[1] // wide):
        at = slice(n * wide, (n + 1) * wide)
        found = lax.dot_general(kernel, halves[slot, at, :], NT, preferred_element_type=F32)
        low = found[8:16, :]
        at16 = iota(low.shape, 0)
        top = found[0:8, :] + jnp.where(at16 >= 6, pltpu.roll(low, 5, 0), 0.0)
        grads[tile, 0:8, at] = top
        grads[tile, 8:9, at] = low[0:1, :] + low[3:4, :]
        yield


def gather_home(me, n, back, send, centres, conic, rho, opacity, out, total, rows, own, recv_sem):
    left = iota((SUB, LANE), 1) < 64
    row = iota((SUB, LANE), 0)
    pairs = n // 2
    mine = me // 2
    blocks = centres.shape[1] // 256
    used = pl.ds(0, USED)
    total[...] = jnp.zeros_like(total)

    def chunk(g, messages):
        arrived = back.at[pl.ds(0, messages), used]
        pltpu.make_async_copy(arrived, arrived, recv_sem.at[g]).wait()
        eight, ninth, idx = [], [], []
        for k in range(GROUP):
            i = lax.rem(mine + pairs - (g * GROUP + k), pairs)
            values, last = unpack_pair(back[2 * i], back[2 * i + 1], left, row)
            eight.append(values)
            ninth.append(last)
            idx.append(send[0:1, pl.ds(pl.multiple_of(i * LANE, LANE), LANE)])
        total[...] = total[...] + scatter_block(
            jnp.concatenate(eight, axis=1), jnp.concatenate(ninth, axis=1), jnp.concatenate(idx, axis=1), blocks
        )

    own.wait()
    chunk(0, 2 * GROUP - 1)

    def later(g, carry):
        chunk(g, 2 * GROUP)
        return carry

    lax.fori_loop(1, pairs // GROUP, later, 0)
    for h in range(blocks):
        span = slice(h * 256, (h + 1) * 256)
        rows[0:8, span] = total[h * SUB : (h + 1) * SUB, :]
        rows[8:9, span] = total[blocks * SUB + h : blocks * SUB + h + 1, :]
    m_uu, m_uv, m_vv, m_u, m_v, m_1 = (rows[p : p + 1, :] for p in range(6))
    cx, cy = centres[0:1, :], centres[1:2, :]
    a, c = conic[0:1, :], conic[1:2, :]
    r = rho[...]
    root = jnp.sqrt(a * c)
    b = r * root
    x1, y1 = m_u - cx * m_1, m_v - cy * m_1
    xx = m_uu - cx * (m_u + x1)
    yy = m_vv - cy * (m_v + y1)
    xy = m_uv - cx * m_v - cy * x1
    out[0:1, :] = a * x1 + b * y1
    out[1:2, :] = c * y1 + b * x1
    out[2:3, :] = -0.5 * xx - xy * (0.5 * r * (root / a))
    out[3:4, :] = -0.5 * yy - xy * (0.5 * r * (root / c))
    out[4:5, :] = -xy * root
    out[5:6, :] = m_1 / opacity[...]
    out[6:9, :] = rows[6:9, :]


def shade_all(
    me, n, lists, left_in, grad, chunk_rend, chunk_start, send, centres, conic, rho, opacity, result,
    cots, halves, grads, slots, out, back, total, rows, local_sem, send_sem, recv_sem
):
    for ch in range(3):
        for g in range(cots.shape[0] // SUB):
            for h in range(2):
                span = slice(h * LANE, (h + 1) * LANE)
                block = block_transpose(grad[ch, h * SUB : (h + 1) * SUB, g * LANE : (g + 1) * LANE])
                for t in range(SUB):
                    cots[g * SUB + t, ch : ch + 1, span] = block[t : t + 1, :]

    def backward(step, carry):
        views = [ref.at[pl.ds(2 * step, 2)] for ref in (left_in, chunk_rend, chunk_start)]
        for slot in range(2):
            tile = 2 * step + slot
            past = jnp.maximum(tile - 1, 0)
            take_turns(
                BACK_TURNS,
                f=find_moments(1 - slot, past, cots, halves, grads),
                s=shade_tile(slot, tile, *views, cots, halves),
            )
        return carry

    lax.fori_loop(0, cots.shape[0] // 2, backward, 0)
    for _ in find_moments(1, cots.shape[0] - 1, cots, halves, grads):
        pass
    slots[...] = jnp.zeros_like(slots)
    blocks = slots.shape[0] // (SUB + 1)
    group = 6

    def chunk(c, carry):
        each = [c * group + k for k in range(group)]
        idx = jnp.concatenate([jnp.maximum(lists[t], 0) for t in each], axis=1)
        eight = jnp.concatenate([grads[t, 0:8, :] for t in each], axis=1)
        ninth = jnp.concatenate([grads[t, 8:9, :] for t in each], axis=1)
        slots[...] = slots[...] + scatter_block(eight, ninth, idx, blocks)
        return carry

    lax.fori_loop(0, cots.shape[0] // group, chunk, 0)
    left = iota((SUB, LANE), 1) < 64
    row = iota((SUB, LANE), 0)
    for h in range(blocks):
        for half in range(2):
            span = slice(half * LANE, (half + 1) * LANE)
            acc = slots[h * SUB : (h + 1) * SUB, span]
            extra = jnp.broadcast_to(slots[blocks * SUB + h : blocks * SUB + h + 1, span], (SUB, LANE))
            owner = 4 * h + 2 * half
            out[owner], out[owner + 1] = pack_pair(acc, extra, left, row)
    used = pl.ds(0, USED)
    own = pltpu.make_async_copy(out.at[me, used], back.at[me, used], local_sem)
    own.start()
    pairs = n // 2
    mine = me // 2

    def ship_to(peer, k):
        pltpu.make_async_remote_copy(
            src_ref=out.at[peer, used], dst_ref=back.at[me, used],
            send_sem=send_sem, recv_sem=recv_sem.at[k // GROUP],
            device_id=(peer,), device_id_type=MESH,
        ).start()

    ship_to(me + 1 - 2 * lax.rem(me, 2), 0)

    def ship(k, carry):
        for core in range(2):
            ship_to(2 * lax.rem(mine + k, pairs) + core, k)
        return carry

    lax.fori_loop(1, pairs, ship, 0)
    gather_home(me, n, back, send, centres, conic, rho, opacity, result, total, rows, own, recv_sem)
    sent = out.at[pl.ds(0, n - 1), used]
    pltpu.make_async_copy(sent, sent, send_sem).wait()


def struct(*shape, dtype=F32):
    return jax.ShapeDtypeStruct(shape, dtype)


def shards(tile_lists, send_rows, centres, conic, rho, opacity, colors, target):
    devices = lax.axis_size("dev")
    owned = centres.shape[1]
    tiles, count = tile_lists.shape
    height, width = target.shape[1], target.shape[2]
    pixels = height * height
    params = lambda mib: pltpu.CompilerParams(vmem_limit_bytes=mib << 20)
    sources = (send_rows, centres, conic, rho, opacity, colors, tile_lists)
    per = 2
    hi_blocks = devices * 64 // 256
    vmem, hbm = pl.BlockSpec(memory_space=pltpu.VMEM), pl.BlockSpec(memory_space=pltpu.HBM)
    image, grads = pl.pallas_call(
        step_kernel,
        in_specs=[hbm] * 8,
        out_specs=[vmem] * 2,
        out_shape=[struct(3, height, width), struct(9, owned)],
        scratch_shapes=[
            pltpu.VMEM((hi_blocks * SUB, 256), F32),
            pltpu.VMEM((hi_blocks, 256), F32),
            pltpu.VMEM((hi_blocks * (SUB + 1), 2 * 256), BF16),
            pltpu.VMEM((per, count, LANE), F32),
            pltpu.VMEM((per, count, pixels), F32),
            pltpu.VMEM((3, tiles, pixels), F32),
            pltpu.VMEM((3, height, width), F32),
        ]
        + [pltpu.VMEM((RIMS, width), F32)] * 4
        + [
            pltpu.VMEM((5, 3 * height, width), F32),
            pltpu.VMEM((3, 2 * height, width), F32),
            pltpu.VMEM((3, 2, 2 * height, width), F32),
        ]
        + [pltpu.SemaphoreType.DMA((8,))] * 2
        + [
            pltpu.VMEM((devices, SUB, LANE), F32),
            pltpu.VMEM((tiles, 1, count), jnp.int32),
            pltpu.VMEM((3, 3, height, width), F32),
            pltpu.VMEM((devices, SUB, LANE), F32),
            pltpu.VMEM((SUB, owned), F32),
            pltpu.VMEM((owned // LANE, LANE), F32),
        ]
        + [pltpu.VMEM(v.shape, v.dtype) for v in sources]
        + [pltpu.SemaphoreType.DMA((8,))]
        + [pltpu.SemaphoreType.DMA] * 2
        + [pltpu.SemaphoreType.DMA((3,))] * 2
        + [
            pltpu.VMEM((3, height, width), F32),
            pltpu.VMEM((tiles, 3, 2, SUB, pixels), F32),
            pltpu.VMEM((tiles, 2, SUB, pixels), F32),
            pltpu.VMEM((tiles, count, 32), BF16),
        ]
        + [
            pltpu.VMEM((tiles, 3, pixels), F32),
            pltpu.VMEM((per, count, 3 * pixels), BF16),
            pltpu.VMEM((tiles, 16, count), F32),
            pltpu.VMEM((hi_blocks * (SUB + 1), 256), F32),
            pltpu.VMEM((devices, SUB, LANE), F32),
            pltpu.VMEM((devices, SUB, LANE), F32),
            pltpu.VMEM((owned // 256 * (SUB + 1), 256), F32),
            pltpu.VMEM((16, owned), F32),
            pltpu.SemaphoreType.DMA,
            pltpu.SemaphoreType.DMA,
            pltpu.SemaphoreType.DMA((devices // 2 // GROUP,)),
        ],
        compiler_params=pltpu.CompilerParams(collective_id=0, has_side_effects=True, vmem_limit_bytes=60 * 1024 * 1024),
        name="training_step",
    )(*sources, target)
    return image, grads


def solution(mesh):
    return jax.shard_map(
        shards,
        mesh=mesh,
        in_specs=(
            P("dev", None),
            P("dev", None),
            P(None, "dev"),
            P(None, "dev"),
            P(None, "dev"),
            P(None, "dev"),
            P(None, "dev"),
            P(None, "dev", None),
        ),
        out_specs=(P(None, "dev", None), P(None, "dev")),
        check_vma=False,
    )
```
